32 devices in a mesh: dp: 4 (over x, core), tensor: 8 (over z, y).
Axes of the slice: x: 2, y: 2, z: 4, core: 2. Of those that a mesh axis runs over, the one named last changes fastest.
Arguments:
- tokens: bfloat16 [8192, 1024], P('dp'), may hold values from -6 to 6
- segment_ids: int32 [4, 2048], P('dp'), may hold values from 0 to 7, never falling along the last dimension, each value on 1 to 512 neighbouring positions
- first_gain: bfloat16 [1024], replicated, may hold values from 0.5 to 1.5
- first_shift: bfloat16 [1024], replicated, may hold values from -3 to 3
- qkv_weight: bfloat16 [1024, 16, 192], P(None, 'tensor'), may hold values from -0.1875 to 0.1875
- qv_bias: bfloat16 [16, 128], P('tensor'), may hold values from -3 to 3
- out_weight: bfloat16 [1024, 1024], P('tensor'), may hold values from -0.5 to 0.5
- out_bias: bfloat16 [1024], replicated, may hold values from -2 to 2
- second_gain: bfloat16 [1024], replicated, may hold values from 0.5 to 1.5
- second_shift: bfloat16 [1024], replicated, may hold values from -3 to 3
- up_weight: bfloat16 [1024, 4096], P(None, 'tensor'), may hold values from -0.1875 to 0.1875
- up_bias: bfloat16 [4096], P('tensor'), may hold values from -3 to 3
- down_weight: bfloat16 [4096, 1024], P('tensor'), may hold values from -0.125 to 0.125
- down_bias: bfloat16 [1024], replicated, may hold values from -2 to 2
- cotangent: bfloat16 [8192, 1024], P('dp'), may hold values from -6 to 6
Outputs:
- output: bfloat16 [8192, 1024], P('dp')
- grad_tokens: bfloat16 [8192, 1024], P('dp')
- grad_first_gain: float32 [1024], replicated
- grad_first_shift: float32 [1024], replicated
- grad_qkv_weight: float32 [1024, 16, 192], P(None, 'tensor')
- grad_qv_bias: float32 [16, 128], P('tensor')
- grad_out_weight: float32 [1024, 1024], P('tensor')
- grad_out_bias: float32 [1024], replicated
- grad_second_gain: float32 [1024], replicated
- grad_second_shift: float32 [1024], replicated
- grad_up_weight: float32 [1024, 4096], P(None, 'tensor')
- grad_up_bias: float32 [4096], P('tensor')
- grad_down_weight: float32 [4096, 1024], P('tensor')
- grad_down_bias: float32 [1024], replicated
The draws below stay inside these ranges and needn't reach their ends.
Inputs may be any that keep to these rules, and one draw needn't show every extreme that they name: `segment_ids`: each row of 2048 positions is cut into documents of consecutive positions, at most 512 long, one exactly that long; ids never fall along a row.
All inputs are finite; a program needn't handle non-finite values.
Results may differ from the reference program's by a relative error of at most 0.023.
Values may be sent and summed in bfloat16 or wider, within the bound.
A program may use at most 128 MiB of HBM per device.

```python
import math
import jax
import jax.numpy as jnp
import numpy as np
from jax import lax

D = 1024
H = 16
HD = 64
FF = 4096
SEQ = 2048
ROWS = 4
TOKENS = 8192
N_TENSOR = 8


def shard_levels(key, dims, shards, least, top_value):
    gain = 1.0
    for dim, blocks in shards:
        draws = jax.random.uniform(jax.random.fold_in(jax.random.fold_in(key, 6), dim), (blocks,), jnp.float32, least / len(shards), top_value / len(shards))
        gain = gain * jnp.repeat(jnp.exp(draws), dims[dim] // blocks).reshape((-1,) + (1,) * (len(dims) - 1 - dim))
    return gain


def split_up(number_of, total, reach, slope):
    loads = [(1 << 20) // math.isqrt(rank ** slope) + 1 for rank in range(2, number_of + 1)]
    spare, given = total - reach - (number_of - 1), [1] * (number_of - 1)
    while spare > 0:
        candidates = [i for i in range(number_of - 1) if given[i] < reach]
        pool, budget = sum([loads[i] for i in candidates]), spare
        for i in candidates:
            more = min(reach - given[i], max(1, budget * loads[i] // pool), spare)
            given[i] = given[i] + more
            spare = spare - more
    return np.array([reach] + given)


def uneven_parts(stream_key, count, total, most, lean):
    if count == 2:
        one = jax.random.randint(stream_key, (), max(1, total - most), min(most, total - 1) + 1)
        return jnp.stack([one, total - one])
    lengths = jnp.asarray(split_up(count, total, most, lean), jnp.int32)
    twos = (count - 1) // 2
    giver, sink = lengths[1:1 + 2 * twos:2], lengths[2:2 + 2 * twos:2]
    margin = jnp.minimum(giver - 1, most - sink)
    moved = jax.random.randint(jax.random.fold_in(stream_key, 1), (twos,), 0, 1 << 20) % (margin + 1)
    lengths = lengths.at[1:1 + 2 * twos:2].set(giver - moved).at[2:2 + 2 * twos:2].set(sink + moved)
    return lengths[jax.random.permutation(jax.random.fold_in(stream_key, 2), count)]


def noise(own_key, dims, scale, reach, shards=(), held_as=jnp.bfloat16):
    array = jax.random.normal(own_key, dims, jnp.float32) * scale
    if len(shards) > 0:
        array = shard_levels(own_key, dims, shards, -0.22, 0.18) * array
    return jnp.clip(array, min=-reach, max=reach).astype(held_as)


def setup_inputs(seed: int = 0) -> dict:
    arg_keys = jax.random.split(jax.random.key(seed), 16)
    return {
        "tokens": noise(arg_keys[0], (TOKENS, D), 1.0, 6.0, ((0, 4),)),
        "segment_ids": jax.vmap(lambda own: jnp.searchsorted(jnp.cumsum(uneven_parts(own, 8, SEQ, SEQ // 4, 2)), jnp.arange(SEQ), side="right"))(jax.random.split(arg_keys[1], ROWS)).reshape((ROWS, SEQ)).astype(jnp.int32),
        "first_gain": jnp.clip(1.0 + 0.1 * jax.random.normal(arg_keys[2], (D,), jnp.float32), 0.5, 1.5).astype(jnp.bfloat16),
        "first_shift": noise(arg_keys[3], (D,), 0.5, 3.0),
        "qkv_weight": noise(arg_keys[4], (D, H, 3 * HD), D ** -0.5, 0.1875, ((1, 8),)),
        "qv_bias": noise(arg_keys[5], (H, 2 * HD), 0.5, 3.0, ((0, 8),)),
        "out_weight": noise(arg_keys[6], (D, D), (D // 8) ** -0.5, 0.5, ((0, 8),)),
        "out_bias": noise(arg_keys[7], (D,), 0.3, 2.0),
        "second_gain": jnp.clip(1.0 + 0.1 * jax.random.normal(arg_keys[8], (D,), jnp.float32), 0.5, 1.5).astype(jnp.bfloat16),
        "second_shift": noise(arg_keys[9], (D,), 0.5, 3.0),
        "up_weight": noise(arg_keys[10], (D, FF), D ** -0.5, 0.1875, ((1, 8),)),
        "up_bias": noise(arg_keys[11], (FF,), 0.5, 3.0, ((0, 8),)),
        "down_weight": noise(arg_keys[12], (FF, D), (FF // 2) ** -0.5, 0.125, ((0, 8),)),
        "down_bias": noise(arg_keys[13], (D,), 0.3, 2.0),
        "cotangent": noise(arg_keys[14], (TOKENS, D), 1.0, 6.0, ((0, 4),)),
    }


@jax.custom_vjp
def low(v):
    return lax.optimization_barrier(v.astype(jnp.bfloat16)).astype(jnp.float32)

@jax.custom_vjp
def low_back(v):
    return v

def low_keep(v):
    return (low(v), None)

def low_pass(kept, grad):
    return (grad,)

def back_keep(v):
    return (v, None)

def back_low(kept, grad):
    return (low(grad),)
low.defvjp(low_keep, low_pass)
low_back.defvjp(back_keep, back_low)
highest = lax.Precision.HIGHEST
norm_eps = 1e-05

def layer_norm(values, gain_vec, shift_vec):
    center = lax.optimization_barrier(jnp.mean(values, axis=-1, keepdims=True))
    offset = values - center
    spread = lax.optimization_barrier(jnp.mean(offset * offset, axis=-1, keepdims=True))
    return offset * lax.rsqrt(spread + norm_eps) * gain_vec + shift_vec

def gelu_tanh(values):
    return 0.5 * values * (1.0 + jnp.tanh(0.7978845608028654 * (values + 0.044715 * values * values * values)))

def attend(packed):
    query, keys, values, seg_row = packed
    length = query.shape[0]
    heads = query.shape[1]
    scale = 1.0 / math.sqrt(query.shape[2])
    scores = jnp.einsum('qhe,khe->hqk', query, keys, precision=highest) * scale
    places = jnp.arange(length, dtype=jnp.int32)
    distance = (places[:, None] - places[None, :]).astype(jnp.float32)
    slopes = jnp.exp2(-8.0 * (jnp.arange(heads, dtype=jnp.int32) + 1).astype(jnp.float32) / heads)
    scores = scores - slopes[:, None, None] * distance[None]
    allowed = (seg_row[:, None] == seg_row[None, :]) & (places[None, :] <= places[:, None])
    scores = jnp.where(allowed[None], scores, -1e+30)
    scores = low_back(scores)
    peak = lax.optimization_barrier(jnp.max(scores, axis=-1, keepdims=True))
    expo = jnp.exp(scores - peak)
    probs = low(expo / lax.optimization_barrier(jnp.sum(expo, axis=-1, keepdims=True)))
    return jnp.einsum('hqk,khe->qhe', probs, values, precision=highest)

def forward(tokens, first_gain, first_shift, qkv_weight, qv_bias, out_weight, out_bias, second_gain, second_shift, up_weight, up_bias, down_weight, down_bias, segment_ids):
    count = tokens.shape[0]
    normed = low(layer_norm(tokens, first_gain, first_shift))
    merged = jnp.einsum('td,dhe->the', normed, qkv_weight, precision=highest)
    query = low_back(low(merged[:, :, :HD] + qv_bias[:, :HD]))
    keys = low_back(low(merged[:, :, HD:2 * HD]))
    values = low_back(low(merged[:, :, 2 * HD:] + qv_bias[:, HD:]))

    def by_rows(arr):
        return arr.reshape(ROWS, SEQ, H, HD)
    context = lax.map(jax.checkpoint(attend), (by_rows(query), by_rows(keys), by_rows(values), segment_ids))
    context = low_back(low(context.reshape(count, N_TENSOR, D // N_TENSOR)))
    parts = low(jnp.einsum('tgc,gcd->gtd', context, out_weight.reshape(N_TENSOR, D // N_TENSOR, D), precision=highest))
    mixed = low_back(lax.optimization_barrier(jnp.sum(parts, axis=0)))
    middle = tokens + mixed + out_bias
    second = low(layer_norm(middle, second_gain, second_shift))
    upper = low_back(jnp.dot(second, up_weight, precision=highest) + up_bias)
    hidden = low(gelu_tanh(upper)).reshape(count, N_TENSOR, FF // N_TENSOR)
    parts_two = low(jnp.einsum('tgf,gfd->gtd', hidden, down_weight.reshape(N_TENSOR, FF // N_TENSOR, D), precision=highest))
    feed = low_back(lax.optimization_barrier(jnp.sum(parts_two, axis=0)))
    return middle + feed + down_bias

def reference(tokens, segment_ids, first_gain, first_shift, qkv_weight, qv_bias, out_weight, out_bias, second_gain, second_shift, up_weight, up_bias, down_weight, down_bias, cotangent):
    floats = [arr.astype(jnp.float32) for arr in (tokens, first_gain, first_shift, qkv_weight, qv_bias, out_weight, out_bias, second_gain, second_shift, up_weight, up_bias, down_weight, down_bias)]

    def layer(*params):
        return forward(*params, segment_ids)
    result, pull = jax.vjp(layer, *floats)
    grads = pull(cotangent.astype(jnp.float32))
    return (result.astype(jnp.bfloat16), grads[0].astype(jnp.bfloat16), grads[1], grads[2], grads[3], grads[4], grads[5], grads[6], grads[7], grads[8], grads[9], grads[10], grads[11], grads[12])
```

```python
import math

import jax
import jax.numpy as jnp
from jax import lax
from jax.sharding import PartitionSpec as P

norm_eps = 1e-05


def layer_norm(values, gain_vec, shift_vec):
    center = jnp.mean(values, axis=-1, keepdims=True)
    offset = values - center
    spread = jnp.mean(offset * offset, axis=-1, keepdims=True)
    return offset * lax.rsqrt(spread + norm_eps) * gain_vec + shift_vec


def gelu_tanh(values):
    return (
        0.5
        * values
        * (1.0 + jnp.tanh(0.7978845608028654 * (values + 0.044715 * values * values * values)))
    )


def head_slopes(local_heads):
    total = local_heads * lax.axis_size("tensor")
    first = lax.axis_index("tensor") * local_heads
    heads_idx = first + jnp.arange(local_heads, dtype=jnp.int32)
    return jnp.exp2(-8.0 * (heads_idx + 1).astype(jnp.float32) / total)


def block_scores(query_blk, keys, start, seg_row, slopes):
    rows = query_blk.shape[0]
    length = keys.shape[0]
    scale = 1.0 / math.sqrt(keys.shape[2])
    raw = jnp.einsum("qhe,khe->hqk", query_blk, keys, preferred_element_type=jnp.float32) * scale
    query_pos = start + jnp.arange(rows, dtype=jnp.int32)
    key_pos = jnp.arange(length, dtype=jnp.int32)
    distance = (query_pos[:, None] - key_pos[None, :]).astype(jnp.float32)
    raw = raw - slopes[:, None, None] * distance[None]
    query_seg = lax.dynamic_slice_in_dim(seg_row, start, rows, 0)
    allowed = (query_seg[:, None] == seg_row[None, :]) & (key_pos[None, :] <= query_pos[:, None])
    return jnp.where(allowed[None], raw, -1e30)


def attend_forward(query, keys, values, seg_row, slopes):
    length = query.shape[0]
    block = min(512, length)

    def one_block(index):
        start = index * block
        query_blk = lax.dynamic_slice_in_dim(query, start, block, 0)
        scores = block_scores(query_blk, keys, start, seg_row, slopes)
        peak = jnp.max(scores, axis=-1, keepdims=True)
        expo = jnp.exp(scores - peak)
        total = jnp.sum(expo, axis=-1, keepdims=True)
        weights_low = (expo / total).astype(jnp.bfloat16)
        ctx_blk = jnp.einsum(
            "hqk,khe->qhe", weights_low, values, preferred_element_type=jnp.float32
        )
        return (ctx_blk, (peak + jnp.log(total))[:, :, 0])

    ctx_blocks, lse_blocks = lax.map(one_block, jnp.arange(length // block, dtype=jnp.int32))
    return (ctx_blocks.reshape(query.shape), lse_blocks)


def attend_backward(query, keys, values, seg_row, slopes, lse_blocks, grad_context):
    length = query.shape[0]
    block = min(512, length)
    scale = 1.0 / math.sqrt(keys.shape[2])

    def one_block(carry, index):
        grad_keys, grad_values = carry
        start = index * block
        query_blk = lax.dynamic_slice_in_dim(query, start, block, 0)
        grad_blk = lax.dynamic_slice_in_dim(grad_context, start, block, 0)
        scores = block_scores(query_blk, keys, start, seg_row, slopes)
        probs = jnp.exp(scores - lse_blocks[index][:, :, None])
        probs_low = probs.astype(jnp.bfloat16)
        grad_probs = jnp.einsum(
            "qhe,khe->hqk", grad_blk, values, preferred_element_type=jnp.float32
        )
        inner = jnp.sum(probs * grad_probs, axis=-1, keepdims=True)
        grad_scores = (probs * (grad_probs - inner)).astype(jnp.bfloat16)
        grad_query = (
            jnp.einsum("hqk,khe->qhe", grad_scores, keys, preferred_element_type=jnp.float32)
            * scale
        )
        grad_keys = (
            grad_keys
            + jnp.einsum("hqk,qhe->khe", grad_scores, query_blk, preferred_element_type=jnp.float32)
            * scale
        )
        grad_values = grad_values + jnp.einsum(
            "hqk,qhe->khe", probs_low, grad_blk, preferred_element_type=jnp.float32
        )
        return ((grad_keys, grad_values), grad_query)

    empty = jnp.zeros(keys.shape, jnp.float32)
    (grad_keys, grad_values), grad_query = lax.scan(
        one_block, (empty, empty), jnp.arange(length // block, dtype=jnp.int32)
    )
    return (grad_query.reshape(query.shape), grad_keys, grad_values)


def attn_front(
    tokens_f, seg_row, first_gain, first_shift, qkv_weight, qv_bias, out_weight, out_bias
):
    length = tokens_f.shape[0]
    normed_low = layer_norm(
        tokens_f, first_gain.astype(jnp.float32), first_shift.astype(jnp.float32)
    ).astype(jnp.bfloat16)
    merged = jnp.einsum("td,dhe->the", normed_low, qkv_weight, preferred_element_type=jnp.float32)
    width = merged.shape[2] // 3
    bias_f = qv_bias.astype(jnp.float32)
    query = (merged[:, :, :width] + bias_f[:, :width]).astype(jnp.bfloat16)
    keys = merged[:, :, width : 2 * width].astype(jnp.bfloat16)
    values = (merged[:, :, 2 * width :] + bias_f[:, width:]).astype(jnp.bfloat16)
    slopes = head_slopes(query.shape[1])
    context, lse_blocks = attend_forward(query, keys, values, seg_row, slopes)
    context_low = context.reshape(length, -1).astype(jnp.bfloat16)
    partial_out = jnp.dot(context_low, out_weight, preferred_element_type=jnp.float32).astype(
        jnp.bfloat16
    )
    mixed = lax.psum(partial_out, "tensor").astype(jnp.float32)
    middle = tokens_f + mixed + out_bias.astype(jnp.float32)
    return (normed_low, query, keys, values, context_low, lse_blocks, middle, slopes)


def mlp_front(middle, second_gain, second_shift, up_weight, up_bias):
    second_low = layer_norm(
        middle, second_gain.astype(jnp.float32), second_shift.astype(jnp.float32)
    ).astype(jnp.bfloat16)
    upper = jnp.dot(second_low, up_weight, preferred_element_type=jnp.float32) + up_bias.astype(
        jnp.float32
    )
    hidden_low = gelu_tanh(upper).astype(jnp.bfloat16)
    return (second_low, upper, hidden_low)


def norm_pull(values, gain_vec, shift_vec, grad_norm):
    norm_value, pull_fn = jax.vjp(
        layer_norm, values, gain_vec.astype(jnp.float32), shift_vec.astype(jnp.float32)
    )
    return pull_fn(grad_norm)


def per_device(
    tokens,
    segment_ids,
    first_gain,
    first_shift,
    qkv_weight,
    qv_bias,
    out_weight,
    out_bias,
    second_gain,
    second_shift,
    up_weight,
    up_bias,
    down_weight,
    down_bias,
    cotangent,
):
    tokens_f = tokens.astype(jnp.float32)
    seg_row = segment_ids[0]
    saved = attn_front(
        tokens_f, seg_row, first_gain, first_shift, qkv_weight, qv_bias, out_weight, out_bias
    )
    middle = saved[6]
    second_low, upper, hidden_low = mlp_front(middle, second_gain, second_shift, up_weight, up_bias)
    part_down = jnp.dot(hidden_low, down_weight, preferred_element_type=jnp.float32).astype(
        jnp.bfloat16
    )
    feed = lax.psum(part_down, "tensor").astype(jnp.float32)
    output = (middle + feed + down_bias.astype(jnp.float32)).astype(jnp.bfloat16)
    normed_low, query, keys, values, context_low, lse_blocks, middle, slopes = saved
    grad_out = cotangent.astype(jnp.float32)
    grad_down_weight = jnp.einsum(
        "tf,td->fd", hidden_low, cotangent, preferred_element_type=jnp.float32
    )
    grad_down_bias = jnp.sum(grad_out, axis=0)
    grad_hidden = jnp.einsum(
        "td,fd->tf", cotangent, down_weight, preferred_element_type=jnp.float32
    )
    gelu_value, gelu_pull = jax.vjp(gelu_tanh, upper)
    grad_upper_low = gelu_pull(grad_hidden)[0].astype(jnp.bfloat16)
    grad_up_bias = jnp.sum(grad_upper_low.astype(jnp.float32), axis=0)
    grad_up_weight = jnp.einsum(
        "td,tf->df", second_low, grad_upper_low, preferred_element_type=jnp.float32
    )
    part_second = jnp.einsum(
        "tf,df->td", grad_upper_low, up_weight, preferred_element_type=jnp.float32
    )
    grad_second = lax.psum(part_second.astype(jnp.bfloat16), "tensor").astype(jnp.float32)
    grad_middle_norm, grad_second_gain, grad_second_shift = norm_pull(
        middle, second_gain, second_shift, grad_second
    )
    grad_middle = grad_out + grad_middle_norm
    mlp_grads = (
        lax.psum(grad_down_weight.astype(jnp.bfloat16), "dp").astype(jnp.float32),
        lax.psum(grad_up_weight.astype(jnp.bfloat16), "dp").astype(jnp.float32),
        lax.psum(grad_up_bias.astype(jnp.bfloat16), "dp").astype(jnp.float32),
        lax.psum(grad_down_bias.astype(jnp.bfloat16), "dp").astype(jnp.float32),
        lax.psum(grad_second_gain.astype(jnp.bfloat16), "dp").astype(jnp.float32),
        lax.psum(grad_second_shift.astype(jnp.bfloat16), "dp").astype(jnp.float32),
    )
    grad_middle_low = grad_middle.astype(jnp.bfloat16)
    grad_out_bias = jnp.sum(grad_middle, axis=0)
    grad_out_weight = jnp.einsum(
        "tc,td->cd", context_low, grad_middle_low, preferred_element_type=jnp.float32
    )
    grad_context = jnp.einsum(
        "td,cd->tc", grad_middle_low, out_weight, preferred_element_type=jnp.float32
    )
    grad_context = grad_context.astype(jnp.bfloat16).reshape(query.shape)
    grad_query, grad_keys, grad_values = attend_backward(
        query, keys, values, seg_row, slopes, lse_blocks, grad_context
    )
    grad_query_low = grad_query.astype(jnp.bfloat16)
    grad_values_low = grad_values.astype(jnp.bfloat16)
    grad_merged = jnp.concatenate(
        [grad_query_low, grad_keys.astype(jnp.bfloat16), grad_values_low], axis=2
    )
    grad_qv_bias = jnp.concatenate(
        [
            jnp.sum(grad_query_low.astype(jnp.float32), axis=0),
            jnp.sum(grad_values_low.astype(jnp.float32), axis=0),
        ],
        axis=1,
    )
    grad_qkv_weight = jnp.einsum(
        "td,the->dhe", normed_low, grad_merged, preferred_element_type=jnp.float32
    )
    part_first = jnp.einsum(
        "the,dhe->td", grad_merged, qkv_weight, preferred_element_type=jnp.float32
    )
    grad_first = lax.psum(part_first.astype(jnp.bfloat16), "tensor").astype(jnp.float32)
    grad_tokens_norm, grad_first_gain, grad_first_shift = norm_pull(
        tokens_f, first_gain, first_shift, grad_first
    )
    grad_tokens_f = grad_middle + grad_tokens_norm
    grad_tokens = grad_tokens_f.astype(jnp.bfloat16)
    attn_grads = (
        lax.psum(grad_qkv_weight.astype(jnp.bfloat16), "dp").astype(jnp.float32),
        lax.psum(grad_qv_bias.astype(jnp.bfloat16), "dp").astype(jnp.float32),
        lax.psum(grad_out_weight.astype(jnp.bfloat16), "dp").astype(jnp.float32),
        lax.psum(grad_out_bias.astype(jnp.bfloat16), "dp").astype(jnp.float32),
        lax.psum(grad_first_gain.astype(jnp.bfloat16), "dp").astype(jnp.float32),
        lax.psum(grad_first_shift.astype(jnp.bfloat16), "dp").astype(jnp.float32),
    )
    return (
        output,
        grad_tokens,
        attn_grads[4],
        attn_grads[5],
        attn_grads[0],
        attn_grads[1],
        attn_grads[2],
        attn_grads[3],
        mlp_grads[4],
        mlp_grads[5],
        mlp_grads[1],
        mlp_grads[2],
        mlp_grads[0],
        mlp_grads[3],
    )


def solution(mesh):
    return jax.shard_map(
        per_device,
        mesh=mesh,
        in_specs=(
            P("dp", None),
            P("dp", None),
            P(),
            P(),
            P(None, "tensor", None),
            P("tensor", None),
            P("tensor", None),
            P(),
            P(),
            P(),
            P(None, "tensor"),
            P("tensor"),
            P("tensor", None),
            P(),
            P("dp", None),
        ),
        out_specs=(
            P("dp", None),
            P("dp", None),
            P(),
            P(),
            P(None, "tensor", None),
            P("tensor", None),
            P("tensor", None),
            P(),
            P(),
            P(),
            P(None, "tensor"),
            P("tensor"),
            P("tensor", None),
            P(),
        ),
        check_vma=False,
    )
```

```python
import functools
import math

import jax
import jax.numpy as jnp
from jax import lax
from jax.experimental import pallas as pl
from jax.experimental.pallas import tpu as pltpu
from jax.sharding import PartitionSpec as P

MESH = pl.DeviceIdType.MESH
ANY = pl.BlockSpec(memory_space=pl.ANY)
VM = pl.BlockSpec(memory_space=pltpu.VMEM)


def grid_of(n_tensor):
    lines = min(4, n_tensor)
    return lines, n_tensor // lines


def where_am_i(n_tensor):
    lines, wide = grid_of(n_tensor)
    dp, t = lax.axis_index("dp"), lax.axis_index("tensor")
    return dp, t, t // wide, t % wide


def greet(peers):
    barrier = pltpu.get_barrier_semaphore()
    for ok, peer in peers:
        @pl.when(ok)
        def _():
            pl.semaphore_signal(barrier, inc=1, device_id=peer, device_id_type=MESH)
    pl.semaphore_wait(barrier, sum(jnp.int32(ok) for ok, peer in peers))


def neighbours(n_tensor, use_y=True, use_x=True, use_core=True):
    lines, wide = grid_of(n_tensor)
    dp, t, z, y = where_am_i(n_tensor)
    out = [(z > 0, (dp, t - wide)), (z < lines - 1, (dp, t + wide))]
    if use_y:
        out += [(y > 0, (dp, t - 1)), (y < wide - 1, (dp, t + 1))]
    if use_x:
        out.append((dp >= 0, (dp ^ 2, t)))
    if use_core:
        out.append((dp >= 0, (dp ^ 1, t)))
    return out


def gather_kernel(n_tensor, n_attn, n_mlp, *refs):
    lines, wide = grid_of(n_tensor)
    dp, t, z, y = where_am_i(n_tensor)
    n = n_attn + n_mlp
    own, full = refs[:n], refs[n : 2 * n]
    z_send, z_recv, y_send, y_recv, x_send, x_recv, c_send, c_recv, l_sem = refs[2 * n :]
    quad = dp % 4

    def slot(a, zz, yy):
        return zz * wide + yy if a < n_attn else zz

    def piece(ref, a, q):
        rows = own[a].shape[0] // 4
        return ref.at[pl.ds(pl.multiple_of(q * rows, rows), rows)]

    def block(a, zz, yy, q):
        return piece(full[a].at[slot(a, zz, yy)], a, q)

    def copy(src, dst, send, recv, peer):
        return pltpu.make_async_remote_copy(
            src_ref=src, dst_ref=dst, send_sem=send, recv_sem=recv, device_id=peer, device_id_type=MESH
        )

    greet(neighbours(n_tensor))
    local = [pltpu.make_async_copy(own[a], full[a].at[slot(a, z, y)], l_sem.at[a]) for a in range(n)]
    for c in local:
        c.start()
    up, down = (dp, t + wide), (dp, t - wide)

    def z_copy(a, zz, side, mine=False):
        src = piece(own[a], a, quad) if mine else block(a, zz, y, quad)
        return copy(src, block(a, zz, y, quad), z_send.at[side, a, zz], z_recv.at[side, a, zz], (up, down)[side])

    def y_copy(a, zz, yy, side, mine=False):
        src = piece(own[a], a, quad) if mine else block(a, zz, yy, quad)
        peer = ((dp, t + 1), (dp, t - 1))[side]
        return copy(src, block(a, zz, yy, quad), y_send.at[side, a, zz, yy], y_recv.at[side, a, zz, yy], peer)

    def x_copy(a, zz, yy, q):
        return copy(block(a, zz, yy, q), block(a, zz, yy, q), x_send.at[a, zz, yy], x_recv.at[a, zz, yy], (dp ^ 2, t))

    def c_copy(a, zz, yy, q, hop):
        return copy(
            block(a, zz, yy, q), block(a, zz, yy, q), c_send.at[hop, a, zz, yy], c_recv.at[hop, a, zz, yy], (dp ^ 1, t)
        )

    def spread(a, zz, yy):
        x_copy(a, zz, yy, quad).start()
        c_copy(a, zz, yy, quad, 0).start()

    def arrays(group):
        return range(n_attn) if group == 0 else range(n_attn, n)

    def y_start(zz, yy, side, mine=False):
        @pl.when((y < wide - 1) if side == 0 else (y > 0))
        def _():
            for a in range(n_attn):
                y_copy(a, zz, yy, side, mine).start()

    for group in range(2):
        for side in range(2):
            @pl.when((z < lines - 1) if side == 0 else (z > 0))
            def _():
                for a in arrays(group):
                    z_copy(a, z, side, True).start()
        if group == 0:
            for side in range(2):
                y_start(z, y, side, True)
    for group in range(2):
        for k in range(1, lines):
            for side in range(2):
                zz = z - k if side == 0 else z + k

                @pl.when((zz >= 0) if side == 0 else (zz < lines))
                def _():
                    for a in arrays(group):
                        z_copy(a, zz, side).wait_recv()

                    @pl.when((z < lines - 1) if side == 0 else (z > 0))
                    def _():
                        for a in arrays(group):
                            z_copy(a, zz, side).start()

                    if group == 0:
                        for s in range(2):
                            y_start(zz, y, s)
                    for a in arrays(group):
                        spread(a, zz, y)
        if group == 0:
            for m in range(1, wide):
                for side in range(2):
                    yy = y - m if side == 0 else y + m

                    @pl.when((yy >= 0) if side == 0 else (yy < wide))
                    def _():
                        for zz in range(lines):
                            for a in range(n_attn):
                                y_copy(a, zz, yy, side).wait_recv()
                            if m < wide - 1:
                                y_start(zz, yy, side)
                            for a in range(n_attn):
                                spread(a, zz, yy)
    def others(group, body):
        for zz in range(lines):
            for yy in range(wide) if group == 0 else [y]:
                @pl.when((zz != z) | (yy != y))
                def _():
                    body(zz, yy)

    for group in range(2):
        def pass_on(zz, yy):
            for a in arrays(group):
                x_copy(a, zz, yy, quad ^ 2).wait_recv()
                c_copy(a, zz, yy, quad ^ 2, 1).start()

        others(group, pass_on)
    for group in range(2):
        def settle(zz, yy):
            for a in arrays(group):
                for hop in range(2):
                    c_copy(a, zz, yy, quad ^ (1 + 2 * hop), hop).wait_recv()
                    c_copy(a, zz, yy, quad ^ (2 * hop), hop).wait_send()
                x_copy(a, zz, yy, quad).wait_send()

        others(group, settle)
        for side in range(2):
            @pl.when((z < lines - 1) if side == 0 else (z > 0))
            def _():
                for k in range(lines):
                    zz = z - k if side == 0 else z + k

                    @pl.when((zz >= 0) if side == 0 else (zz < lines))
                    def _():
                        for a in arrays(group):
                            z_copy(a, zz, side).wait_send()
    for side in range(2):
        @pl.when((y < wide - 1) if side == 0 else (y > 0))
        def _():
            for zz in range(lines):
                for m in range(wide):
                    yy = y - m if side == 0 else y + m

                    @pl.when((yy >= 0) if side == 0 else (yy < wide))
                    def _():
                        for a in range(n_attn):
                            y_copy(a, zz, yy, side).wait_send()
    for c in local:
        c.wait()


def gather_weights(n_tensor, attn, mlp):
    lines, wide = grid_of(n_tensor)
    n = len(attn) + len(mlp)
    arrays = list(attn) + list(mlp)
    outs = [
        jax.ShapeDtypeStruct(((n_tensor if i < len(attn) else lines),) + a.shape, a.dtype) for i, a in enumerate(arrays)
    ]
    dma = pltpu.SemaphoreType.DMA
    return pl.pallas_call(
        functools.partial(gather_kernel, n_tensor, len(attn), len(mlp)),
        out_shape=outs,
        in_specs=[ANY] * n,
        out_specs=[ANY] * n,
        scratch_shapes=[dma((2, n, lines))] * 2
        + [dma((2, len(attn), lines, wide))] * 2
        + [dma((n, lines, wide))] * 2
        + [dma((2, n, lines, wide))] * 2
        + [dma((n,))],
        compiler_params=pltpu.CompilerParams(collective_id=0, has_side_effects=True),
        name="gather_weights",
    )(*arrays)


def add_rows(dst, terms):
    rows = dst.shape[0]
    step = 32 if rows % 32 == 0 else rows

    @pl.loop(0, rows // step)
    def _(i):
        part = pl.ds(pl.multiple_of(i * step, step), step)
        total = terms[0][part].astype(jnp.float32)
        for term in terms[1:]:
            total = total + term[part].astype(jnp.float32)
        dst[part] = total.astype(dst.dtype)


def reduce_kernel(n_tensor, n_attn, n_mlp, *refs):
    lines, wide = grid_of(n_tensor)
    dp, t, z, y = where_am_i(n_tensor)
    n = n_attn + n_mlp
    terms, final = refs[:n], refs[n : 2 * n]
    from_c, from_x, to_x, acc, from_y, from_z = (refs[(2 + i) * n : (3 + i) * n] for i in range(6))
    c_send, c_recv, x_send, x_recv, y_send, y_recv, z_send, z_recv, q_send, q_recv = refs[8 * n :]
    quad = dp % 4
    side_x = quad // 2
    core = quad % 2
    core_peer, x_peer = (dp ^ 1, t), (dp ^ 2, t)

    def copy(src, dst, send, recv, peer):
        return pltpu.make_async_remote_copy(
            src_ref=src, dst_ref=dst, send_sem=send, recv_sem=recv, device_id=peer, device_id_type=MESH
        )

    def slots(a):
        return [(zz, yy) for zz in range(lines) for yy in (range(wide) if a < n_attn else [0])]

    def index(a, zz, yy):
        return zz * wide + yy if a < n_attn else zz

    def quarter(ref, a, q):
        rows = final[a].shape[0] // 4
        return ref.at[pl.ds(pl.multiple_of(q * rows, rows), rows)]

    greet(neighbours(n_tensor))

    def c_copy(a, s, h):
        return copy(
            quarter(terms[a].at[s], a, h * 2 + 1 - core), from_c[a].at[s, h], c_send.at[a, s, h], c_recv.at[a, s, h],
            core_peer,
        )

    def x_copy(a, s):
        return copy(to_x[a].at[s], from_x[a].at[s], x_send.at[a, s], x_recv.at[a, s], x_peer)

    def y_copy(a, zz, yy, side):
        peer = ((dp, t + 1), (dp, t - 1))[side]
        return copy(
            acc[a].at[index(a, zz, yy)], from_y[a].at[side, zz * wide + yy], y_send.at[side, a, zz * wide + yy],
            y_recv.at[side, a, zz * wide + yy], peer,
        )

    def z_copy(a, zz, side):
        peer = ((dp, t + wide), (dp, t - wide))[side]
        return copy(
            acc[a].at[index(a, zz, y)], from_z[a].at[side, zz], z_send.at[side, a, zz], z_recv.at[side, a, zz], peer
        )

    order = list(range(n_attn, n)) + list(range(n_attn))
    for a in order:
        for zz, yy in slots(a):
            for h in range(2):
                c_copy(a, index(a, zz, yy), h).start()
    for a in order:
        for zz, yy in slots(a):
            s = index(a, zz, yy)
            for h in range(2):
                c_copy(a, s, h).wait_recv()
            add_rows(to_x[a].at[s], [quarter(terms[a].at[s], a, (1 - side_x) * 2 + core), from_c[a].at[s, 1 - side_x]])
            x_copy(a, s).start()
            add_rows(acc[a].at[s], [quarter(terms[a].at[s], a, quad), from_c[a].at[s, side_x]])
    for a in order:
        for zz, yy in slots(a):
            s = index(a, zz, yy)
            x_copy(a, s).wait_recv()
            add_rows(acc[a].at[s], [acc[a].at[s], from_x[a].at[s]])

            if a < n_attn:
                @pl.when((y == 0) & (yy > y))
                def _():
                    y_copy(a, zz, yy, 0).start()

                @pl.when((y == wide - 1) & (yy < y))
                def _():
                    y_copy(a, zz, yy, 1).start()
        if a >= n_attn:
            z_stage(a, lines, wide, z, y, z_copy, acc, from_z, index)
    for a in range(n_attn):
        for side in range(2):
            for m in range(1, wide):
                @pl.when((y >= 1) if side == 0 else (y < wide - 1))
                def _():
                    for zz in range(lines):
                        for yy in range(wide):
                            if m > 1:
                                continue

                            @pl.when((yy >= y) if side == 0 else (yy <= y))
                            def _():
                                s = index(a, zz, yy)
                                y_copy(a, zz, yy, side).wait_recv()
                                add_rows(acc[a].at[s], [acc[a].at[s], from_y[a].at[side, zz * wide + yy]])

                                @pl.when(yy != y)
                                def _():
                                    y_copy(a, zz, yy, side).start()

        z_stage(a, lines, wide, z, y, z_copy, acc, from_z, index)

    def q_copy(a, q, hop, peer):
        return copy(quarter(final[a], a, q), quarter(final[a], a, q), q_send.at[hop, a], q_recv.at[hop, a], peer)

    for a in order:
        add_rows(quarter(final[a], a, quad), [acc[a].at[index(a, z, y)]])
        q_copy(a, quad, 0, x_peer).start()
        q_copy(a, quad, 1, core_peer).start()
    for a in order:
        q_copy(a, quad ^ 2, 0, x_peer).wait_recv()
        q_copy(a, quad ^ 2, 2, core_peer).start()
    for a in order:
        q_copy(a, quad ^ 1, 1, core_peer).wait_recv()
        q_copy(a, quad ^ 3, 2, core_peer).wait_recv()
        q_copy(a, quad, 0, x_peer).wait_send()
        q_copy(a, quad, 1, core_peer).wait_send()
        q_copy(a, quad ^ 2, 2, core_peer).wait_send()
        for zz, yy in slots(a):
            s = index(a, zz, yy)
            for h in range(2):
                c_copy(a, s, h).wait_send()
            x_copy(a, s).wait_send()
            if a < n_attn:
                @pl.when((yy > y))
                def _():
                    y_copy(a, zz, yy, 0).wait_send()

                @pl.when((yy < y))
                def _():
                    y_copy(a, zz, yy, 1).wait_send()
        for zz in range(lines):
            @pl.when(zz > z)
            def _():
                z_copy(a, zz, 0).wait_send()

            @pl.when(zz < z)
            def _():
                z_copy(a, zz, 1).wait_send()


def z_stage(a, lines, wide, z, y, z_copy, acc, from_z, index):
    for k in range(lines - 1):
        far = lines - 1 - k
        for side, zz in ((0, far), (1, k)):
            @pl.when((z < zz) if side == 0 else (z > zz))
            def _():
                s = index(a, zz, y)

                @pl.when((z > 0) if side == 0 else (z < lines - 1))
                def _():
                    z_copy(a, zz, side).wait_recv()
                    add_rows(acc[a].at[s], [acc[a].at[s], from_z[a].at[side, zz]])

                z_copy(a, zz, side).start()
    s = index(a, z, y)
    for side in range(2):
        @pl.when((z > 0) if side == 0 else (z < lines - 1))
        def _():
            z_copy(a, z, side).wait_recv()
            add_rows(acc[a].at[s], [acc[a].at[s], from_z[a].at[side, z]])


def reduce_weights(n_tensor, attn, mlp):
    lines, wide = grid_of(n_tensor)
    arrays = list(attn) + list(mlp)
    n = len(arrays)
    vm, dma = pltpu.VMEM, pltpu.SemaphoreType.DMA
    quarters = [(a.shape[1] // 4, a.shape[2]) for a in arrays]
    outs = [jax.ShapeDtypeStruct(a.shape[1:], a.dtype) for a in arrays]
    low = jnp.bfloat16
    scratch = (
        [vm((a.shape[0], 2) + q, low) for a, q in zip(arrays, quarters)]
        + [vm((a.shape[0],) + q, low) for a, q in zip(arrays, quarters)]
        + [vm((a.shape[0],) + q, low) for a, q in zip(arrays, quarters)]
        + [vm((a.shape[0],) + q, low) for a, q in zip(arrays, quarters)]
        + [vm(((2, n_tensor) if i < len(attn) else (1, 1)) + q, low) for i, q in enumerate(quarters)]
        + [vm((2, lines) + q, low) for q in quarters]
    )
    sems = (
        [dma((n, n_tensor, 2))] * 2
        + [dma((n, n_tensor))] * 2
        + [dma((2, len(attn), n_tensor))] * 2
        + [dma((2, n, lines))] * 2
        + [dma((3, n))] * 2
    )
    sums = pl.pallas_call(
        functools.partial(reduce_kernel, n_tensor, len(attn), len(mlp)),
        out_shape=outs,
        in_specs=[VM] * n,
        out_specs=[VM] * n,
        scratch_shapes=scratch + sems,
        compiler_params=pltpu.CompilerParams(collective_id=1, has_side_effects=True, vmem_limit_bytes=60 * 2**20),
        name="reduce_weights",
    )(*arrays)
    if lax.axis_size("dp") > 4:
        sums = [lax.psum(s, "dp").astype(jnp.float32) * 0.25 for s in sums]
    return sums


def group_kernel(n_tensor, scatter, own, full, send, recv, l_sem):
    lines, wide = grid_of(n_tensor)
    dp, t, z, y = where_am_i(n_tensor)
    peers = [(y != yy, (dp, z * wide + yy)) for yy in range(wide)]
    greet(peers)
    local = pltpu.make_async_copy(own.at[y] if scatter else own, full.at[y], l_sem)
    local.start()

    def step(yy, slot):
        return pltpu.make_async_remote_copy(
            src_ref=own.at[yy] if scatter else own, dst_ref=full.at[slot], send_sem=send.at[yy], recv_sem=recv.at[slot],
            device_id=peers[yy][1], device_id_type=MESH,
        )

    for yy in range(wide):
        @pl.when(peers[yy][0])
        def _():
            step(yy, y).start()
    for yy in range(wide):
        @pl.when(peers[yy][0])
        def _():
            step(yy, yy).wait_recv()
            step(yy, y).wait_send()
    local.wait()


def group_exchange(n_tensor, own, scatter, cid, name):
    lines, wide = grid_of(n_tensor)
    dma = pltpu.SemaphoreType.DMA
    shape = own.shape if scatter else (wide,) + own.shape
    return pl.pallas_call(
        functools.partial(group_kernel, n_tensor, scatter),
        out_shape=jax.ShapeDtypeStruct(shape, own.dtype),
        in_specs=[ANY],
        out_specs=ANY,
        scratch_shapes=[dma((wide,)), dma((wide,)), dma],
        compiler_params=pltpu.CompilerParams(collective_id=cid, has_side_effects=True),
        name=name,
    )(own)


def halo_kernel(n_tensor, halo, own, got, send, recv):
    dp, t, z, y = where_am_i(n_tensor)
    ahead = [(t + 1 + m < n_tensor, (dp, t + 1 + m)) for m in range(halo)]
    greet(ahead + [(t - 1 - m >= 0, (dp, t - 1 - m)) for m in range(halo)])

    def step(m):
        return pltpu.make_async_remote_copy(
            src_ref=own.at[halo - 1 - m], dst_ref=got.at[m], send_sem=send.at[m], recv_sem=recv.at[m],
            device_id=(dp, t - 1 - m), device_id_type=MESH,
        )

    for m in range(halo):
        @pl.when(t - 1 - m >= 0)
        def _():
            step(m).start()
    for m in range(halo):
        @pl.when(t + 1 + m < n_tensor)
        def _():
            step(m).wait_recv()

        @pl.when(t - 1 - m >= 0)
        def _():
            step(m).wait_send()


def halo_exchange(n_tensor, own):
    halo = own.shape[0]
    dma = pltpu.SemaphoreType.DMA
    return pl.pallas_call(
        functools.partial(halo_kernel, n_tensor, halo),
        out_shape=jax.ShapeDtypeStruct(own.shape, own.dtype),
        in_specs=[ANY],
        out_specs=ANY,
        scratch_shapes=[dma((halo,)), dma((halo,))],
        compiler_params=pltpu.CompilerParams(collective_id=2, has_side_effects=True),
        name="halo_exchange",
    )(own)


def rows_kernel(n_tensor, n, *refs):
    lines, wide = grid_of(n_tensor)
    dp, t, z, y = where_am_i(n_tensor)
    own, full = refs[:n], refs[n : 2 * n]
    z_send, z_recv, y_send, y_recv, l_sem = refs[2 * n :]
    greet(neighbours(n_tensor, True, False, False))

    def copy(src, dst, send, recv, peer):
        return pltpu.make_async_remote_copy(
            src_ref=src, dst_ref=dst, send_sem=send, recv_sem=recv, device_id=peer, device_id_type=MESH
        )

    def z_copy(a, zz, side, mine=False):
        dst = full[a].at[zz * wide + y]
        peer = ((dp, t + wide), (dp, t - wide))[side]
        return copy(own[a] if mine else dst, dst, z_send.at[side, a, zz], z_recv.at[side, a, zz], peer)

    def y_copy(a, zz, yy, side, mine=False):
        dst = full[a].at[zz * wide + yy]
        peer = ((dp, t + 1), (dp, t - 1))[side]
        return copy(own[a] if mine else dst, dst, y_send.at[side, a, zz, yy], y_recv.at[side, a, zz, yy], peer)

    z_has = ((z < lines - 1), (z > 0))
    y_has = ((y < wide - 1), (y > 0))

    def when(condition, body):
        pl.when(condition)(body)

    local = [pltpu.make_async_copy(own[a], full[a].at[t], l_sem.at[a]) for a in range(n)]
    for side in range(2):
        for a in range(n):
            when(z_has[side], lambda: z_copy(a, z, side, True).start())
            when(y_has[side], lambda: y_copy(a, z, y, side, True).start())
    for c in local:
        c.start()
    for k in range(1, lines):
        for side in range(2):
            zz = z - k if side == 0 else z + k

            @pl.when((zz >= 0) & (zz < lines))
            def _():
                for a in range(n):
                    z_copy(a, zz, side).wait_recv()
                    when(z_has[side], lambda: z_copy(a, zz, side).start())
                    for s in range(2):
                        when(y_has[s], lambda: y_copy(a, zz, y, s).start())
    for m in range(1, wide):
        for side in range(2):
            yy = y - m if side == 0 else y + m

            @pl.when((yy >= 0) & (yy < wide))
            def _():
                for zz in range(lines):
                    for a in range(n):
                        y_copy(a, zz, yy, side).wait_recv()
                        if m < wide - 1:
                            when(y_has[side], lambda: y_copy(a, zz, yy, side).start())
    for side in range(2):
        for k in range(lines):
            zz = z - k if side == 0 else z + k

            @pl.when(z_has[side] & (zz >= 0) & (zz < lines))
            def _():
                for a in range(n):
                    z_copy(a, zz, side).wait_send()
        for m in range(wide):
            yy = y - m if side == 0 else y + m

            @pl.when(y_has[side] & (yy >= 0) & (yy < wide))
            def _():
                for zz in range(lines):
                    for a in range(n):
                        y_copy(a, zz, yy, side).wait_send()
    for c in local:
        c.wait()


def gather_rows(n_tensor, arrays, cid):
    lines, wide = grid_of(n_tensor)
    n = len(arrays)
    dma = pltpu.SemaphoreType.DMA
    return pl.pallas_call(
        functools.partial(rows_kernel, n_tensor, n),
        out_shape=[jax.ShapeDtypeStruct((n_tensor,) + a.shape, a.dtype) for a in arrays],
        in_specs=[ANY] * n,
        out_specs=[ANY] * n,
        scratch_shapes=[dma((2, n, lines))] * 2 + [dma((2, n, lines, wide))] * 2 + [dma((n,))],
        compiler_params=pltpu.CompilerParams(collective_id=cid, has_side_effects=True),
        name="gather_rows",
    )(*arrays)


def dot(a, b, contract, **kwargs):
    return lax.dot_general(a, b, (contract, ((), ())), preferred_element_type=jnp.float32, **kwargs)


NN, NT, TN = ((1,), (0,)), ((1,), (1,)), ((0,), (0,))


def head_of_lane(shape, heads):
    return lax.broadcasted_iota(jnp.int32, shape, 1) // (shape[1] // heads)


def attend_kernel(heads, slopes, dist, q, k, v, ctx):
    pair = pl.program_id(0)
    lanes = q.shape[2]
    scale = 1.0 / math.sqrt(lanes // heads)
    query, keys, values = q[0], k[0], v[0]
    head = head_of_lane(query.shape, heads)
    out = jnp.zeros(query.shape, jnp.float32)
    for h in range(heads):
        masked = jnp.where(head == h, query * jnp.bfloat16(scale), jnp.bfloat16(0))
        scores = dot(masked, keys, NT) - slopes[pair * heads + h] * dist[...]
        peak = jnp.max(scores, axis=1, keepdims=True)
        expo = jnp.exp(scores - peak)
        total = jnp.sum(expo, axis=1, keepdims=True)
        part = dot(expo.astype(jnp.bfloat16), values, NN) / total
        out = jnp.where(head == h, part, out)
    ctx[0] = out.astype(jnp.bfloat16)


def attend_pull_kernel(heads, slopes, dist, q, k, v, g, dq, dk, dv):
    pair = pl.program_id(0)
    lanes = q.shape[2]
    scale = 1.0 / math.sqrt(lanes // heads)
    query, keys, values, grad = q[0], k[0], v[0], g[0]
    head = head_of_lane(query.shape, heads)
    head_rows = lax.broadcasted_iota(jnp.int32, (lanes, query.shape[0]), 0) // (lanes // heads)
    low = jnp.bfloat16
    grad_q = jnp.zeros((lanes, query.shape[0]), jnp.float32)
    grad_k = jnp.zeros(keys.shape, jnp.float32)
    grad_v = jnp.zeros(keys.shape, jnp.float32)
    for h in range(heads):
        masked = jnp.where(head == h, query * low(scale), low(0))
        masked_grad = jnp.where(head == h, grad, low(0))
        scores = dot(keys, masked, NT) - slopes[pair * heads + h] * dist[...]
        peak = jnp.max(scores, axis=0, keepdims=True)
        expo = jnp.exp(scores - peak)
        probs = expo * (1.0 / jnp.sum(expo, axis=0, keepdims=True))
        grad_probs = dot(values, masked_grad, NT)
        inner = jnp.sum(probs * grad_probs, axis=0, keepdims=True)
        grad_scores = (probs * (grad_probs - inner)).astype(low)
        grad_v = grad_v + dot(probs.astype(low), masked_grad, NN)
        grad_k = grad_k + dot(grad_scores, masked, NN)
        grad_q = jnp.where(head_rows == h, dot(keys, grad_scores, TN), grad_q)
    dq[0] = (jnp.transpose(grad_q) * scale).astype(low)
    dk[0] = grad_k.astype(low)
    dv[0] = grad_v.astype(low)


def by_shard(array):
    return pl.BlockSpec((1,) + array.shape[1:], lambda p: (p, 0, 0))


def attend(slopes, dist, q, k, v):
    heads = slopes.shape[0] // q.shape[0]
    return pl.pallas_call(
        functools.partial(attend_kernel, heads),
        grid=(q.shape[0],),
        out_shape=jax.ShapeDtypeStruct(q.shape, jnp.bfloat16),
        in_specs=[pl.BlockSpec(memory_space=pltpu.SMEM), pl.BlockSpec(dist.shape, lambda p: (0, 0))]
        + [by_shard(a) for a in (q, k, v)],
        out_specs=by_shard(q),
        compiler_params=pltpu.CompilerParams(vmem_limit_bytes=50 * 2**20),
        name="attend",
    )(slopes, dist, q, k, v)


def attend_pull(slopes, dist, q, k, v, g):
    heads = slopes.shape[0] // q.shape[0]
    return pl.pallas_call(
        functools.partial(attend_pull_kernel, heads),
        grid=(q.shape[0],),
        out_shape=[jax.ShapeDtypeStruct(a.shape, jnp.bfloat16) for a in (q, k, v)],
        in_specs=[pl.BlockSpec(memory_space=pltpu.SMEM), pl.BlockSpec(dist.shape, lambda p: (0, 0))]
        + [by_shard(a) for a in (q, k, v, g)],
        out_specs=[by_shard(a) for a in (q, k, v)],
        compiler_params=pltpu.CompilerParams(vmem_limit_bytes=50 * 2**20),
        name="attend_pull",
    )(slopes, dist, q, k, v, g)


norm_eps = 1e-05


def normalized(values):
    offset = values - jnp.mean(values, axis=-1, keepdims=True)
    rate = lax.rsqrt(jnp.mean(offset * offset, axis=-1, keepdims=True) + norm_eps)
    return offset * rate, rate


def norm_input_term(xhat, rate, gain, grad):
    e = grad * gain
    return rate * (e - jnp.mean(e, axis=-1, keepdims=True) - xhat * jnp.mean(e * xhat, axis=-1, keepdims=True))


def gelu_and_slope(u):
    c, a = 0.7978845608028654, 0.044715
    th = jnp.tanh(c * (u + a * u * u * u))
    slope = 0.5 * (1.0 + th) + 0.5 * u * (1.0 - th * th) * (c * (1.0 + 3.0 * a * u * u))
    return 0.5 * u * (1.0 + th), slope


far_off = 1e33
longest = 512


def per_device(
    tokens, segment_ids, first_gain, first_shift, qkv_weight, qv_bias, out_weight, out_bias, second_gain, second_shift,
    up_weight, up_bias, down_weight, down_bias, cotangent,
):
    low, f32 = jnp.bfloat16, jnp.float32
    nt = lax.axis_size("tensor")
    lines, wide = grid_of(nt)
    t = lax.axis_index("tensor")
    z, y = t // wide, t % wide
    length, d = tokens.shape
    chunk = length // nt
    halo = -(-(longest - 1) // chunk)
    behind = halo * chunk
    span = behind + chunk
    heads_here, width = qkv_weight.shape[1], qkv_weight.shape[2] // 3
    lanes = heads_here * width
    hidden_here = up_weight.shape[1]

    qkv_own = qkv_weight.reshape(d, heads_here, 3, width).transpose(0, 2, 1, 3).reshape(d, 3 * lanes)
    bias_own = qv_bias.reshape(heads_here, 2, width).transpose(1, 0, 2).reshape(2 * lanes)
    small = jnp.concatenate([bias_own, up_bias])
    small = jnp.concatenate([small, jnp.zeros((64 * 128 - small.shape[0],), low)]).reshape(64, 128)
    qkv_all, out_all, small_all, up_all, down_all = gather_weights(
        nt, [qkv_own, out_weight, small], [up_weight, down_weight]
    )
    small_all = small_all.reshape(nt, 64 * 128).astype(f32)
    q_bias, v_bias = small_all[:, :lanes], small_all[:, lanes : 2 * lanes]
    up_bias_all = lax.dynamic_index_in_dim(
        small_all[:, 2 * lanes : 2 * lanes + hidden_here].reshape(lines, wide, hidden_here), y, 1, keepdims=False
    )

    padded = jnp.concatenate([jnp.zeros((behind, d), low), tokens])
    near = lax.dynamic_slice_in_dim(padded, t * chunk, span, 0).astype(f32)
    seg_row = jnp.concatenate([jnp.full((behind,), -1, jnp.int32), segment_ids[0]])
    seg_near = lax.dynamic_slice_in_dim(seg_row, t * chunk, span, 0)
    seg_mine = seg_near[behind:]
    distance = (behind + jnp.arange(chunk)[:, None]) - jnp.arange(span)[None, :]
    allowed = (seg_mine[:, None] == seg_near[None, :]) & (distance >= 0)
    dist = jnp.where(allowed, distance.astype(f32), far_off)
    total_heads = heads_here * nt
    slopes = jnp.exp2(-8.0 * (jnp.arange(total_heads, dtype=jnp.int32) + 1).astype(f32) / total_heads)

    gain1, shift1 = first_gain.astype(f32), first_shift.astype(f32)
    gain2, shift2 = second_gain.astype(f32), second_shift.astype(f32)
    xhat1, rate1 = normalized(near)
    normed = (xhat1 * gain1 + shift1).astype(low)
    mine = normed[behind:]
    query = (jnp.einsum("td,gde->gte", mine, qkv_all[:, :, :lanes], preferred_element_type=f32) + q_bias[:, None]).astype(low)
    keys = jnp.einsum("td,gde->gte", normed, qkv_all[:, :, lanes : 2 * lanes], preferred_element_type=f32).astype(low)
    values = (
        jnp.einsum("td,gde->gte", normed, qkv_all[:, :, 2 * lanes :], preferred_element_type=f32) + v_bias[:, None]
    ).astype(low)
    context = attend(slopes, dist, query, keys, values)
    context = context.transpose(1, 0, 2).reshape(chunk, d)
    out_full = out_all.reshape(d, d)
    mixed = jnp.dot(context, out_full, preferred_element_type=f32)
    middle = near[behind:] + mixed + out_bias.astype(f32)
    xhat2, rate2 = normalized(middle)
    second = (xhat2 * gain2 + shift2).astype(low)

    second_pair = group_exchange(nt, second, False, 3, "share_second").reshape(wide * chunk, d)
    cot_pair = lax.dynamic_slice_in_dim(cotangent, z * (wide * chunk), wide * chunk, 0)
    upper = jnp.einsum("td,zdf->ztf", second_pair, up_all, preferred_element_type=f32) + up_bias_all[:, None]
    hidden, slope = gelu_and_slope(upper)
    hidden = hidden.astype(low)
    feed_part = jnp.einsum("ztf,zfd->td", hidden, down_all, preferred_element_type=f32)
    grad_hidden = jnp.einsum("td,zfd->ztf", cot_pair, down_all, preferred_element_type=f32)
    grad_upper = (grad_hidden * slope).astype(low)
    grad_up_bias = jnp.sum(grad_upper.astype(f32), axis=1)
    grad_down = jnp.einsum("ztf,td->zfd", hidden, cot_pair, preferred_element_type=f32).astype(low)
    grad_up = jnp.einsum("td,ztf->zdf", second_pair, grad_upper, preferred_element_type=f32).astype(low)
    second_part = jnp.einsum("ztf,zdf->td", grad_upper, up_all, preferred_element_type=f32)
    parts = jnp.stack([second_part.reshape(wide, chunk, d), feed_part.reshape(wide, chunk, d)], axis=1).astype(low)
    sums = jnp.sum(group_exchange(nt, parts, True, 4, "sum_parts").astype(f32), axis=0)
    grad_second, feed = sums[0], sums[1]
    output_mine = (middle + feed + down_bias.astype(f32)).astype(low)

    cot_mine = lax.dynamic_slice_in_dim(cotangent, t * chunk, chunk, 0).astype(f32)
    grad_middle = cot_mine + norm_input_term(xhat2, rate2, gain2, grad_second)
    grad_middle_low = grad_middle.astype(low)
    grad_out = jnp.dot(context.T, grad_middle_low, preferred_element_type=f32).astype(low).reshape(out_all.shape)
    grad_context = jnp.einsum("td,gcd->gtc", grad_middle_low, out_all, preferred_element_type=f32).astype(low)
    grad_q, grad_k, grad_v = attend_pull(slopes, dist.T, query, keys, values, grad_context)
    grad_kv = jnp.concatenate([grad_k, grad_v], axis=2)
    grad_qkv = jnp.concatenate(
        [
            jnp.einsum("td,gte->gde", mine, grad_q, preferred_element_type=f32),
            jnp.einsum("td,gte->gde", normed, grad_kv, preferred_element_type=f32),
        ],
        axis=2,
    ).astype(low)
    first_part = jnp.einsum("gte,gde->td", grad_kv, qkv_all[:, :, lanes:], preferred_element_type=f32)
    first_mine = first_part[behind:] + jnp.einsum("gte,gde->td", grad_q, qkv_all[:, :, :lanes], preferred_element_type=f32)
    got = halo_exchange(nt, first_part[:behind].astype(low).reshape(halo, chunk, d)).astype(f32)
    there = (t + 1 + jnp.arange(halo)) < nt
    grad_first = first_mine + jnp.sum(jnp.where(there[:, None, None], got, 0.0), axis=0)
    xhat_mine = xhat1[behind:]
    grad_tokens = (grad_middle + norm_input_term(xhat_mine, rate1[behind:], gain1, grad_first)).astype(low)

    g_qkv, g_out, g_up, g_down = reduce_weights(nt, [grad_qkv, grad_out], [grad_up, grad_down])
    output_all, grad_tokens_all = gather_rows(nt, [output_mine, grad_tokens], 5)

    def rows_sum(v):
        return jnp.sum(v, axis=0)

    up_slots = jnp.where(jnp.arange(wide)[None, :, None] == y, grad_up_bias[:, None, :], 0.0)
    q_sum, v_sum = jnp.sum(grad_q.astype(f32), axis=1), jnp.sum(grad_v.astype(f32), axis=1)
    vectors = jnp.concatenate(
        [
            rows_sum(grad_first * xhat_mine), rows_sum(grad_first), rows_sum(grad_middle),
            rows_sum(grad_second * xhat2), rows_sum(grad_second), rows_sum(cot_mine),
            q_sum.reshape(-1), v_sum.reshape(-1), up_slots.reshape(-1),
        ]
    )
    vectors = lax.psum(vectors, ("dp", "tensor"))
    g_first_gain, g_first_shift, g_out_bias, g_second_gain, g_second_shift, g_down_bias = (
        vectors[i * d : (i + 1) * d] for i in range(6)
    )
    rest = vectors[6 * d :]
    g_q = lax.dynamic_index_in_dim(rest[:d].reshape(nt, heads_here, width), t, 0, keepdims=False)
    g_v = lax.dynamic_index_in_dim(rest[d : 2 * d].reshape(nt, heads_here, width), t, 0, keepdims=False)
    g_up_bias = lax.dynamic_index_in_dim(rest[2 * d :].reshape(nt, hidden_here), t, 0, keepdims=False)
    g_qkv = g_qkv.astype(f32).reshape(d, 3, heads_here, width).transpose(0, 2, 1, 3).reshape(d, heads_here, 3 * width)
    return (
        output_all.reshape(length, d), grad_tokens_all.reshape(length, d), g_first_gain, g_first_shift, g_qkv,
        jnp.concatenate([g_q, g_v], axis=1), g_out.astype(f32), g_out_bias, g_second_gain, g_second_shift,
        g_up.astype(f32), g_up_bias, g_down.astype(f32), g_down_bias,
    )


def solution(mesh):
    rows, cols, both = P("dp", None), P(None, "tensor"), P("tensor", None)
    return jax.shard_map(
        per_device,
        mesh=mesh,
        in_specs=(
            rows, rows, P(), P(), P(None, "tensor", None), both, both, P(), P(), P(), cols, P("tensor"), both, P(), rows,
        ),
        out_specs=(
            rows, rows, P(), P(), P(None, "tensor", None), both, both, P(), P(), P(), cols, P("tensor"), both, P(),
        ),
        check_vma=False,
    )
```

```python
import functools
import math

import jax
import jax.numpy as jnp
from jax import lax
from jax.experimental import pallas as pl
from jax.experimental.pallas import tpu as pltpu
from jax.sharding import PartitionSpec as P

MESH = pl.DeviceIdType.MESH
ANY = pl.BlockSpec(memory_space=pl.ANY)
VM = pl.BlockSpec(memory_space=pltpu.VMEM)


def grid_of(n_tensor):
    lines = min(4, n_tensor)
    return lines, n_tensor // lines


def where_am_i(n_tensor):
    lines, wide = grid_of(n_tensor)
    dp, t = lax.axis_index("dp"), lax.axis_index("tensor")
    return dp, t, t // wide, t % wide


def remote(src, dst, send, recv, peer):
    return pltpu.make_async_remote_copy(
        src_ref=src, dst_ref=dst, send_sem=send, recv_sem=recv, device_id=peer, device_id_type=MESH
    )


def when(condition, body):
    pl.when(condition)(body)


def greet(peers):
    barrier = pltpu.get_barrier_semaphore()
    for ok, peer in peers:
        @pl.when(ok)
        def _():
            pl.semaphore_signal(barrier, inc=1, device_id=peer, device_id_type=MESH)
    pl.semaphore_wait(barrier, sum(jnp.int32(ok) for ok, peer in peers))


def neighbours(n_tensor, use_y=True, use_x=True, use_core=True):
    lines, wide = grid_of(n_tensor)
    dp, t, z, y = where_am_i(n_tensor)
    out = [(z > 0, (dp, t - wide)), (z < lines - 1, (dp, t + wide))]
    if use_y:
        out += [(y > 0, (dp, t - 1)), (y < wide - 1, (dp, t + 1))]
    if use_x:
        out.append((dp >= 0, (dp ^ 2, t)))
    if use_core:
        out.append((dp >= 0, (dp ^ 1, t)))
    return out


def gather_kernel(n_tensor, n_attn, n_mlp, *refs):
    lines, wide = grid_of(n_tensor)
    dp, t, z, y = where_am_i(n_tensor)
    n = n_attn + n_mlp
    own, full = refs[:n], refs[n : 2 * n]
    z_send, z_recv, y_send, y_recv, x_send, x_recv, c_send, c_recv, l_sem = refs[2 * n :]
    quad = dp % 4

    def slot(a, zz, yy):
        return zz * wide + yy if a < n_attn else zz

    def piece(ref, a, q):
        rows = own[a].shape[0] // 4
        return ref.at[pl.ds(pl.multiple_of(q * rows, rows), rows)]

    def block(a, zz, yy, q):
        return piece(full[a].at[slot(a, zz, yy)], a, q)

    def copy(src, dst, send, recv, peer):
        return pltpu.make_async_remote_copy(
            src_ref=src, dst_ref=dst, send_sem=send, recv_sem=recv, device_id=peer, device_id_type=MESH
        )

    greet(neighbours(n_tensor))
    local = [pltpu.make_async_copy(own[a], full[a].at[slot(a, z, y)], l_sem.at[a]) for a in range(n)]
    for c in local:
        c.start()
    up, down = (dp, t + wide), (dp, t - wide)

    def z_copy(a, zz, side, mine=False):
        src = piece(own[a], a, quad) if mine else block(a, zz, y, quad)
        return copy(src, block(a, zz, y, quad), z_send.at[side, a, zz], z_recv.at[side, a, zz], (up, down)[side])

    def y_copy(a, zz, yy, side, mine=False):
        src = piece(own[a], a, quad) if mine else block(a, zz, yy, quad)
        peer = ((dp, t + 1), (dp, t - 1))[side]
        return copy(src, block(a, zz, yy, quad), y_send.at[side, a, zz, yy], y_recv.at[side, a, zz, yy], peer)

    def x_copy(a, zz, yy, q):
        return copy(block(a, zz, yy, q), block(a, zz, yy, q), x_send.at[a, zz, yy], x_recv.at[a, zz, yy], (dp ^ 2, t))

    def c_copy(a, zz, yy, q, hop):
        return copy(
            block(a, zz, yy, q), block(a, zz, yy, q), c_send.at[hop, a, zz, yy], c_recv.at[hop, a, zz, yy], (dp ^ 1, t)
        )

    def spread(a, zz, yy):
        x_copy(a, zz, yy, quad).start()
        c_copy(a, zz, yy, quad, 0).start()

    def arrays(group):
        return range(n_attn) if group == 0 else range(n_attn, n)

    def y_start(zz, yy, side, mine=False):
        @pl.when((y < wide - 1) if side == 0 else (y > 0))
        def _():
            for a in range(n_attn):
                y_copy(a, zz, yy, side, mine).start()

    for group in range(2):
        for side in range(2):
            @pl.when((z < lines - 1) if side == 0 else (z > 0))
            def _():
                for a in arrays(group):
                    z_copy(a, z, side, True).start()
        if group == 0:
            for side in range(2):
                y_start(z, y, side, True)
    for group in range(2):
        for k in range(1, lines):
            for side in range(2):
                zz = z - k if side == 0 else z + k

                @pl.when((zz >= 0) if side == 0 else (zz < lines))
                def _():
                    for a in arrays(group):
                        z_copy(a, zz, side).wait_recv()

                    @pl.when((z < lines - 1) if side == 0 else (z > 0))
                    def _():
                        for a in arrays(group):
                            z_copy(a, zz, side).start()

                    if group == 0:
                        for s in range(2):
                            y_start(zz, y, s)
                    for a in arrays(group):
                        spread(a, zz, y)
        if group == 0:
            for m in range(1, wide):
                for side in range(2):
                    yy = y - m if side == 0 else y + m

                    @pl.when((yy >= 0) if side == 0 else (yy < wide))
                    def _():
                        for zz in range(lines):
                            for a in range(n_attn):
                                y_copy(a, zz, yy, side).wait_recv()
                            if m < wide - 1:
                                y_start(zz, yy, side)
                            for a in range(n_attn):
                                spread(a, zz, yy)
    def others(group, body):
        for zz in range(lines):
            for yy in range(wide) if group == 0 else [y]:
                @pl.when((zz != z) | (yy != y))
                def _():
                    body(zz, yy)

    for group in range(2):
        def pass_on(zz, yy):
            for a in arrays(group):
                x_copy(a, zz, yy, quad ^ 2).wait_recv()
                c_copy(a, zz, yy, quad ^ 2, 1).start()

        others(group, pass_on)
    for group in range(2):
        def settle(zz, yy):
            for a in arrays(group):
                for hop in range(2):
                    c_copy(a, zz, yy, quad ^ (1 + 2 * hop), hop).wait_recv()
                    c_copy(a, zz, yy, quad ^ (2 * hop), hop).wait_send()
                x_copy(a, zz, yy, quad).wait_send()

        others(group, settle)
        for side in range(2):
            @pl.when((z < lines - 1) if side == 0 else (z > 0))
            def _():
                for k in range(lines):
                    zz = z - k if side == 0 else z + k

                    @pl.when((zz >= 0) if side == 0 else (zz < lines))
                    def _():
                        for a in arrays(group):
                            z_copy(a, zz, side).wait_send()
    for side in range(2):
        @pl.when((y < wide - 1) if side == 0 else (y > 0))
        def _():
            for zz in range(lines):
                for m in range(wide):
                    yy = y - m if side == 0 else y + m

                    @pl.when((yy >= 0) if side == 0 else (yy < wide))
                    def _():
                        for a in range(n_attn):
                            y_copy(a, zz, yy, side).wait_send()
    for c in local:
        c.wait()


def gather_weights(n_tensor, attn, mlp):
    lines, wide = grid_of(n_tensor)
    n = len(attn) + len(mlp)
    arrays = list(attn) + list(mlp)
    outs = [
        jax.ShapeDtypeStruct(((n_tensor if i < len(attn) else lines),) + a.shape, a.dtype) for i, a in enumerate(arrays)
    ]
    dma = pltpu.SemaphoreType.DMA
    return pl.pallas_call(
        functools.partial(gather_kernel, n_tensor, len(attn), len(mlp)),
        out_shape=outs,
        in_specs=[ANY] * n,
        out_specs=[ANY] * n,
        scratch_shapes=[dma((2, n, lines))] * 2
        + [dma((2, len(attn), lines, wide))] * 2
        + [dma((n, lines, wide))] * 2
        + [dma((2, n, lines, wide))] * 2
        + [dma((n,))],
        compiler_params=pltpu.CompilerParams(collective_id=0, has_side_effects=True),
        name="gather_weights",
    )(*arrays)


def add_rows(dst, terms):
    rows = dst.shape[0]
    step = 32 if rows % 32 == 0 else rows

    @pl.loop(0, rows // step)
    def _(i):
        part = pl.ds(pl.multiple_of(i * step, step), step)
        total = terms[0][part].astype(jnp.float32)
        for term in terms[1:]:
            total = total + term[part].astype(jnp.float32)
        dst[part] = total.astype(dst.dtype)


def doubling_peers(n_tensor):
    dp, t, z, y = where_am_i(n_tensor)
    bits = lambda size: [1 << i for i in range((size - 1).bit_length())]
    return [(dp ^ b, t) for b in bits(lax.axis_size("dp"))] + [(dp, t ^ b) for b in bits(n_tensor)]


def doubling_program(n_tensor, own, out, total, got, send, recv):
    peers = doubling_peers(n_tensor)

    def step(i):
        return remote(total.at[i], got.at[i], send.at[i], recv.at[i], peers[i])

    def begin():
        total[0] = own[...]
        step(0).start()

    def advance(i):
        step(i).wait_recv()
        if i + 1 < len(peers):
            total[i + 1] = total[i] + got[i]
            step(i + 1).start()
        else:
            out[...] = total[i] + got[i]

    def settle():
        for i in range(len(peers)):
            step(i).wait_send()

    return [begin] + [functools.partial(advance, i) for i in range(len(peers))] + [settle]


def finish_kernel(n_tensor, n_attn, n_mlp, with_feed, with_vectors, *refs):
    lines, wide = grid_of(n_tensor)
    dp, t, z, y = where_am_i(n_tensor)
    n = n_attn + n_mlp
    refs = list(refs)

    def take(count):
        got, refs[:] = refs[:count], refs[count:]
        return got

    terms, rows_own = take(n), take(1)
    feed_base = take(1)[0] if with_feed else None
    vec_own = take(1)[0] if with_vectors else None
    final, rows_full = take(n), take(1)
    vec_out = take(1)[0] if with_vectors else None
    from_c, from_x, to_x, acc, from_y, from_z = (take(n) for i in range(6))
    c_send, c_recv, x_send, x_recv, y_send, y_recv, z_send, z_recv, q_send, q_recv = take(10)
    rows_sems = take(5)
    if with_feed:
        feed_parts, (feed_got, feed_sum), (f_send, f_recv) = rows_own[0], take(2), take(2)
        rows_own = [feed_sum]
    rows_steps = rows_program(n_tensor, rows_own, rows_full, *rows_sems)
    vec_steps = doubling_program(n_tensor, vec_own, vec_out, *take(4)) if with_vectors else []
    quad = dp % 4
    side_x = quad // 2
    core = quad % 2
    core_peer, x_peer = (dp ^ 1, t), (dp ^ 2, t)

    def slots(a):
        order = [0, lines - 1] + list(range(1, lines - 1))
        return [(zz, yy) for zz in order for yy in (range(wide) if a < n_attn else [0])]

    def index(a, zz, yy):
        return zz * wide + yy if a < n_attn else zz

    def quarter(ref, a, q):
        rows = final[a].shape[0] // 4
        return ref.at[pl.ds(pl.multiple_of(q * rows, rows), rows)]

    def c_copy(a, s, h):
        return remote(
            quarter(terms[a].at[s], a, h * 2 + 1 - core), from_c[a].at[s, h], c_send.at[a, s, h], c_recv.at[a, s, h],
            core_peer,
        )

    def x_copy(a, s):
        return remote(to_x[a].at[s], from_x[a].at[s], x_send.at[a, s], x_recv.at[a, s], x_peer)

    def y_copy(a, zz, yy, side):
        peer = ((dp, t + 1), (dp, t - 1))[side]
        lane = zz * wide + yy
        return remote(acc[a].at[lane], from_y[a].at[side, lane], y_send.at[side, a, lane], y_recv.at[side, a, lane], peer)

    def z_copy(a, zz, side):
        peer = ((dp, t + wide), (dp, t - wide))[side]
        return remote(
            acc[a].at[index(a, zz, y)], from_z[a].at[side, zz], z_send.at[side, a, zz], z_recv.at[side, a, zz], peer
        )

    def core_stage(a, zz, yy):
        s = index(a, zz, yy)
        for h in range(2):
            c_copy(a, s, h).wait_recv()
        add_rows(to_x[a].at[s], [quarter(terms[a].at[s], a, (1 - side_x) * 2 + core), from_c[a].at[s, 1 - side_x]])
        x_copy(a, s).start()
        add_rows(acc[a].at[s], [quarter(terms[a].at[s], a, quad), from_c[a].at[s, side_x]])

    def x_stage(a, zz, yy):
        s = index(a, zz, yy)
        x_copy(a, s).wait_recv()
        add_rows(acc[a].at[s], [acc[a].at[s], from_x[a].at[s]])
        if a < n_attn:
            when((y == 0) & (yy > y), lambda: y_copy(a, zz, yy, 0).start())
            when((y == wide - 1) & (yy < y), lambda: y_copy(a, zz, yy, 1).start())

    def y_stage(a, zz):
        for k in range(wide):
            for side, yy in ((0, wide - 1 - k), (1, k)):
                @pl.when(((yy >= y) & (y > 0)) if side == 0 else ((yy <= y) & (y < wide - 1)))
                def _():
                    lane = zz * wide + yy
                    y_copy(a, zz, yy, side).wait_recv()
                    add_rows(acc[a].at[lane], [acc[a].at[lane], from_y[a].at[side, lane]])
                    when(yy != y, lambda: y_copy(a, zz, yy, side).start())

    def z_stage(a, zz):
        for side in range(2):
            @pl.when((z <= zz) if side == 0 else (z >= zz))
            def _():
                @pl.when((z > 0) if side == 0 else (z < lines - 1))
                def _():
                    s = index(a, zz, y)
                    z_copy(a, zz, side).wait_recv()
                    add_rows(acc[a].at[s], [acc[a].at[s], from_z[a].at[side, zz]])

                when(z != zz, lambda: z_copy(a, zz, side).start())

    def q_copy(a, q, hop, peer):
        return remote(quarter(final[a], a, q), quarter(final[a], a, q), q_send.at[hop, a], q_recv.at[hop, a], peer)

    def home(a):
        add_rows(quarter(final[a], a, quad), [acc[a].at[index(a, z, y)]])
        q_copy(a, quad, 0, x_peer).start()
        q_copy(a, quad, 1, core_peer).start()

    def feed_copy(yy, slot):
        return remote(feed_parts.at[yy], feed_got.at[slot], f_send.at[yy], f_recv.at[slot], (dp, z * wide + yy))

    def feed_start():
        for yy in range(wide):
            when(yy != y, lambda: feed_copy(yy, y).start())

    def feed_end():
        feed_got[y] = jnp.zeros(feed_got.shape[1:], feed_got.dtype)
        for yy in range(wide):
            when(yy != y, lambda: feed_copy(yy, yy).wait_recv())
        add_rows(feed_sum, [feed_base] + [feed_got.at[yy] for yy in range(wide)])
        for yy in range(wide):
            when(yy != y, lambda: feed_copy(yy, y).wait_send())

    peers = neighbours(n_tensor)
    if with_feed and wide > 2:
        peers += [(yy != y, (dp, z * wide + yy)) for yy in range(wide)]
    if with_vectors:
        peers += [(dp >= 0, peer) for peer in doubling_peers(n_tensor)]
    greet(peers)
    attn, mlp = list(range(n_attn)), list(range(n_attn, n))
    order = attn + mlp
    lines_order = [0, lines - 1] + list(range(1, lines - 1))
    if with_feed:
        feed_start()
    else:
        rows_steps.pop(0)()
    for a in order:
        for zz, yy in slots(a):
            for h in range(2):
                c_copy(a, index(a, zz, yy), h).start()
    if with_vectors:
        vec_steps.pop(0)()
    for zz, yy in slots(0):
        for a in order:
            core_stage(a, zz, yy)
    if with_feed:
        feed_end()
        rows_steps.pop(0)()

    def aside():
        if len(rows_steps) > 1:
            rows_steps.pop(0)()
        if len(vec_steps) > 1:
            vec_steps.pop(0)()

    for i in range(lines + 2):
        if i < lines:
            for a in order:
                for yy in range(wide) if a < n_attn else [0]:
                    x_stage(a, lines_order[i], yy)
        if 0 <= i - 1 < lines:
            for a in attn:
                y_stage(a, lines_order[i - 1])
        lag = 2 if n_attn else 1
        if 0 <= i - lag < lines:
            for a in order:
                z_stage(a, lines_order[i - lag])
        aside()
    for a in order:
        home(a)
    aside()
    for a in order:
        q_copy(a, quad ^ 2, 0, x_peer).wait_recv()
        q_copy(a, quad ^ 2, 2, core_peer).start()
    while rows_steps:
        rows_steps.pop(0)()
    while vec_steps:
        vec_steps.pop(0)()
    for a in order:
        q_copy(a, quad ^ 1, 1, core_peer).wait_recv()
        q_copy(a, quad ^ 3, 2, core_peer).wait_recv()
        q_copy(a, quad, 0, x_peer).wait_send()
        q_copy(a, quad, 1, core_peer).wait_send()
        q_copy(a, quad ^ 2, 2, core_peer).wait_send()
        for zz, yy in slots(a):
            s = index(a, zz, yy)
            for h in range(2):
                c_copy(a, s, h).wait_send()
            x_copy(a, s).wait_send()
            if a < n_attn:
                when(yy > y, lambda: y_copy(a, zz, yy, 0).wait_send())
                when(yy < y, lambda: y_copy(a, zz, yy, 1).wait_send())
        for zz in range(lines):
            when(zz > z, lambda: z_copy(a, zz, 0).wait_send())
            when(zz < z, lambda: z_copy(a, zz, 1).wait_send())


def finish(n_tensor, attn, mlp, rows, base, vectors, cid, name):
    lines, wide = grid_of(n_tensor)
    arrays = list(attn) + list(mlp)
    n = len(arrays)
    vm, dma = pltpu.VMEM, pltpu.SemaphoreType.DMA
    quarters = [(a.shape[1] // 4, a.shape[2]) for a in arrays]
    low = jnp.bfloat16
    each = lambda lead: [vm(lead(a, i) + q, low) for i, (a, q) in enumerate(zip(arrays, quarters))]
    slots = lambda a, i: (a.shape[0],)
    steps = (lax.axis_size("dp") - 1).bit_length() + (n_tensor - 1).bit_length()
    scratch = (
        each(lambda a, i: (a.shape[0], 2))
        + each(slots) + each(slots) + each(slots)
        + each(lambda a, i: (2, n_tensor) if i < len(attn) else (1, 1))
        + each(lambda a, i: (2, lines))
    )
    sems = (
        [dma((n, n_tensor, 2))] * 2 + [dma((n, n_tensor))] * 2 + [dma((2, max(1, len(attn)), n_tensor))] * 2
        + [dma((2, n, lines))] * 2 + [dma((3, n))] * 2
        + [dma((2, 1, lines))] * 2 + [dma((2, 1, lines, wide))] * 2 + [dma((1,))]
    )
    inputs, in_specs = arrays + [rows], [VM] * n + [ANY]
    chunk = rows.shape[-2:]
    out_shape = [jax.ShapeDtypeStruct(a.shape[1:], a.dtype) for a in arrays]
    out_shape.append(jax.ShapeDtypeStruct((n_tensor,) + chunk, low))
    out_specs = [VM] * n + [ANY]
    if base is not None:
        inputs, in_specs = inputs + [base], in_specs + [VM]
        sems += [vm((wide,) + chunk, low), vm(chunk, low), dma((wide,)), dma((wide,))]
    if vectors is not None:
        inputs, in_specs = inputs + [vectors], in_specs + [VM]
        out_shape.append(jax.ShapeDtypeStruct(vectors.shape, vectors.dtype))
        out_specs.append(VM)
        sems += [vm((steps,) + vectors.shape, jnp.float32)] * 2 + [dma((steps,))] * 2
    out = pl.pallas_call(
        functools.partial(finish_kernel, n_tensor, len(attn), len(mlp), base is not None, vectors is not None),
        out_shape=out_shape,
        in_specs=in_specs,
        out_specs=out_specs,
        scratch_shapes=scratch + sems,
        compiler_params=pltpu.CompilerParams(collective_id=cid, has_side_effects=True, vmem_limit_bytes=60 * 2**20),
        name=name,
    )(*inputs)
    sums = out[:n]
    if lax.axis_size("dp") > 4:
        sums = [lax.psum(s, "dp").astype(jnp.float32) * 0.25 for s in sums]
    return list(sums) + list(out[n:])


def group_kernel(n_tensor, scatter, own, full, send, recv, l_sem):
    lines, wide = grid_of(n_tensor)
    dp, t, z, y = where_am_i(n_tensor)
    peers = [(y != yy, (dp, z * wide + yy)) for yy in range(wide)]
    greet(peers)
    local = pltpu.make_async_copy(own.at[y] if scatter else own, full.at[y], l_sem)
    local.start()

    def step(yy, slot):
        return pltpu.make_async_remote_copy(
            src_ref=own.at[yy] if scatter else own, dst_ref=full.at[slot], send_sem=send.at[yy], recv_sem=recv.at[slot],
            device_id=peers[yy][1], device_id_type=MESH,
        )

    for yy in range(wide):
        @pl.when(peers[yy][0])
        def _():
            step(yy, y).start()
    for yy in range(wide):
        @pl.when(peers[yy][0])
        def _():
            step(yy, yy).wait_recv()
            step(yy, y).wait_send()
    local.wait()


def group_exchange(n_tensor, own, scatter, cid, name):
    lines, wide = grid_of(n_tensor)
    dma = pltpu.SemaphoreType.DMA
    shape = own.shape if scatter else (wide,) + own.shape
    return pl.pallas_call(
        functools.partial(group_kernel, n_tensor, scatter),
        out_shape=jax.ShapeDtypeStruct(shape, own.dtype),
        in_specs=[ANY],
        out_specs=ANY,
        scratch_shapes=[dma((wide,)), dma((wide,)), dma],
        compiler_params=pltpu.CompilerParams(collective_id=cid, has_side_effects=True),
        name=name,
    )(own)


def halo_kernel(n_tensor, halo, own, got, send, recv):
    dp, t, z, y = where_am_i(n_tensor)
    ahead = [(t + 1 + m < n_tensor, (dp, t + 1 + m)) for m in range(halo)]
    greet(ahead + [(t - 1 - m >= 0, (dp, t - 1 - m)) for m in range(halo)])

    def step(m):
        return pltpu.make_async_remote_copy(
            src_ref=own.at[halo - 1 - m], dst_ref=got.at[m], send_sem=send.at[m], recv_sem=recv.at[m],
            device_id=(dp, t - 1 - m), device_id_type=MESH,
        )

    for m in range(halo):
        @pl.when(t - 1 - m >= 0)
        def _():
            step(m).start()
    for m in range(halo):
        @pl.when(t + 1 + m < n_tensor)
        def _():
            step(m).wait_recv()

        @pl.when(t - 1 - m >= 0)
        def _():
            step(m).wait_send()


def halo_exchange(n_tensor, own):
    halo = own.shape[0]
    dma = pltpu.SemaphoreType.DMA
    return pl.pallas_call(
        functools.partial(halo_kernel, n_tensor, halo),
        out_shape=jax.ShapeDtypeStruct(own.shape, own.dtype),
        in_specs=[ANY],
        out_specs=ANY,
        scratch_shapes=[dma((halo,)), dma((halo,))],
        compiler_params=pltpu.CompilerParams(collective_id=2, has_side_effects=True),
        name="halo_exchange",
    )(own)


def rows_program(n_tensor, own, full, z_send, z_recv, y_send, y_recv, l_sem):
    lines, wide = grid_of(n_tensor)
    dp, t, z, y = where_am_i(n_tensor)
    n = len(own)

    def z_copy(a, zz, side, mine=False):
        dst = full[a].at[zz * wide + y]
        peer = ((dp, t + wide), (dp, t - wide))[side]
        return remote(own[a] if mine else dst, dst, z_send.at[side, a, zz], z_recv.at[side, a, zz], peer)

    def y_copy(a, zz, yy, side, mine=False):
        dst = full[a].at[zz * wide + yy]
        peer = ((dp, t + 1), (dp, t - 1))[side]
        return remote(own[a] if mine else dst, dst, y_send.at[side, a, zz, yy], y_recv.at[side, a, zz, yy], peer)

    z_has = ((z < lines - 1), (z > 0))
    y_has = ((y < wide - 1), (y > 0))
    local = [pltpu.make_async_copy(own[a], full[a].at[t], l_sem.at[a]) for a in range(n)]

    def begin():
        for side in range(2):
            for a in range(n):
                when(z_has[side], lambda: z_copy(a, z, side, True).start())
                when(y_has[side], lambda: y_copy(a, z, y, side, True).start())
        for c in local:
            c.start()

    def along_z(k):
        for side in range(2):
            zz = z - k if side == 0 else z + k

            @pl.when((zz >= 0) & (zz < lines))
            def _():
                for a in range(n):
                    z_copy(a, zz, side).wait_recv()
                    when(z_has[side], lambda: z_copy(a, zz, side).start())
                    for s in range(2):
                        when(y_has[s], lambda: y_copy(a, zz, y, s).start())

    def along_y(m):
        for side in range(2):
            yy = y - m if side == 0 else y + m

            @pl.when((yy >= 0) & (yy < wide))
            def _():
                for zz in range(lines):
                    for a in range(n):
                        y_copy(a, zz, yy, side).wait_recv()
                        if m < wide - 1:
                            when(y_has[side], lambda: y_copy(a, zz, yy, side).start())

    def settle():
        for side in range(2):
            for k in range(lines):
                zz = z - k if side == 0 else z + k

                @pl.when(z_has[side] & (zz >= 0) & (zz < lines))
                def _():
                    for a in range(n):
                        z_copy(a, zz, side).wait_send()
            for m in range(wide):
                yy = y - m if side == 0 else y + m

                @pl.when(y_has[side] & (yy >= 0) & (yy < wide))
                def _():
                    for zz in range(lines):
                        for a in range(n):
                            y_copy(a, zz, yy, side).wait_send()
        for c in local:
            c.wait()

    return (
        [begin]
        + [functools.partial(along_z, k) for k in range(1, lines)]
        + [functools.partial(along_y, m) for m in range(1, wide)]
        + [settle]
    )


def dot(a, b, contract, **kwargs):
    return lax.dot_general(a, b, (contract, ((), ())), preferred_element_type=jnp.float32, **kwargs)


NN, NT, TN = ((1,), (0,)), ((1,), (1,)), ((0,), (0,))


def head_of_lane(shape, heads):
    return lax.broadcasted_iota(jnp.int32, shape, 1) // (shape[1] // heads)


def attend_kernel(heads, slopes, dist, q, k, v, ctx):
    pair = pl.program_id(0)
    lanes = q.shape[2]
    scale = 1.0 / math.sqrt(lanes // heads)
    query, keys, values = q[0], k[0], v[0]
    head = head_of_lane(query.shape, heads)
    out = jnp.zeros(query.shape, jnp.float32)
    for h in range(heads):
        masked = jnp.where(head == h, query * jnp.bfloat16(scale), jnp.bfloat16(0))
        scores = dot(masked, keys, NT) - slopes[pair * heads + h] * dist[...]
        peak = jnp.max(scores, axis=1, keepdims=True)
        expo = jnp.exp(scores - peak)
        total = jnp.sum(expo, axis=1, keepdims=True)
        part = dot(expo.astype(jnp.bfloat16), values, NN) / total
        out = jnp.where(head == h, part, out)
    ctx[0] = out.astype(jnp.bfloat16)


def attend_pull_kernel(heads, slopes, dist, q, k, v, g, dq, dk, dv):
    pair = pl.program_id(0)
    lanes = q.shape[2]
    scale = 1.0 / math.sqrt(lanes // heads)
    query, keys, values, grad = q[0], k[0], v[0], g[0]
    head = head_of_lane(query.shape, heads)
    head_rows = lax.broadcasted_iota(jnp.int32, (lanes, query.shape[0]), 0) // (lanes // heads)
    low = jnp.bfloat16
    grad_q = jnp.zeros((lanes, query.shape[0]), jnp.float32)
    grad_k = jnp.zeros(keys.shape, jnp.float32)
    grad_v = jnp.zeros(keys.shape, jnp.float32)
    for h in range(heads):
        masked = jnp.where(head == h, query * low(scale), low(0))
        masked_grad = jnp.where(head == h, grad, low(0))
        scores = dot(keys, masked, NT) - slopes[pair * heads + h] * dist[...]
        peak = jnp.max(scores, axis=0, keepdims=True)
        expo = jnp.exp(scores - peak)
        probs = expo * (1.0 / jnp.sum(expo, axis=0, keepdims=True))
        grad_probs = dot(values, masked_grad, NT)
        inner = jnp.sum(probs * grad_probs, axis=0, keepdims=True)
        grad_scores = (probs * (grad_probs - inner)).astype(low)
        grad_v = grad_v + dot(probs.astype(low), masked_grad, NN)
        grad_k = grad_k + dot(grad_scores, masked, NN)
        grad_q = jnp.where(head_rows == h, dot(keys, grad_scores, TN), grad_q)
    dq[0] = (jnp.transpose(grad_q) * scale).astype(low)
    dk[0] = grad_k.astype(low)
    dv[0] = grad_v.astype(low)


def by_shard(array):
    return pl.BlockSpec((1,) + array.shape[1:], lambda p: (p, 0, 0))


def attend(slopes, dist, q, k, v):
    heads = slopes.shape[0] // q.shape[0]
    return pl.pallas_call(
        functools.partial(attend_kernel, heads),
        grid=(q.shape[0],),
        out_shape=jax.ShapeDtypeStruct(q.shape, jnp.bfloat16),
        in_specs=[pl.BlockSpec(memory_space=pltpu.SMEM), pl.BlockSpec(dist.shape, lambda p: (0, 0))]
        + [by_shard(a) for a in (q, k, v)],
        out_specs=by_shard(q),
        compiler_params=pltpu.CompilerParams(vmem_limit_bytes=50 * 2**20),
        name="attend",
    )(slopes, dist, q, k, v)


def attend_pull(slopes, dist, q, k, v, g):
    heads = slopes.shape[0] // q.shape[0]
    return pl.pallas_call(
        functools.partial(attend_pull_kernel, heads),
        grid=(q.shape[0],),
        out_shape=[jax.ShapeDtypeStruct(a.shape, jnp.bfloat16) for a in (q, k, v)],
        in_specs=[pl.BlockSpec(memory_space=pltpu.SMEM), pl.BlockSpec(dist.shape, lambda p: (0, 0))]
        + [by_shard(a) for a in (q, k, v, g)],
        out_specs=[by_shard(a) for a in (q, k, v)],
        compiler_params=pltpu.CompilerParams(vmem_limit_bytes=50 * 2**20),
        name="attend_pull",
    )(slopes, dist, q, k, v, g)


norm_eps = 1e-05


def normalized(values):
    offset = values - jnp.mean(values, axis=-1, keepdims=True)
    rate = lax.rsqrt(jnp.mean(offset * offset, axis=-1, keepdims=True) + norm_eps)
    return offset * rate, rate


def norm_input_term(xhat, rate, gain, grad):
    e = grad * gain
    return rate * (e - jnp.mean(e, axis=-1, keepdims=True) - xhat * jnp.mean(e * xhat, axis=-1, keepdims=True))


def gelu_and_slope(u):
    c, a = 0.7978845608028654, 0.044715
    th = jnp.tanh(c * (u + a * u * u * u))
    slope = 0.5 * (1.0 + th) + 0.5 * u * (1.0 - th * th) * (c * (1.0 + 3.0 * a * u * u))
    return 0.5 * u * (1.0 + th), slope


far_off = 1e33
longest = 512


def rows_sum(v):
    return jnp.sum(v, axis=0)


def per_device(
    tokens, segment_ids, first_gain, first_shift, qkv_weight, qv_bias, out_weight, out_bias, second_gain, second_shift,
    up_weight, up_bias, down_weight, down_bias, cotangent,
):
    low, f32 = jnp.bfloat16, jnp.float32
    nt = lax.axis_size("tensor")
    lines, wide = grid_of(nt)
    t = lax.axis_index("tensor")
    z, y = t // wide, t % wide
    length, d = tokens.shape
    chunk = length // nt
    halo = -(-(longest - 1) // chunk)
    behind = halo * chunk
    span = behind + chunk
    heads_here, width = qkv_weight.shape[1], qkv_weight.shape[2] // 3
    lanes = heads_here * width
    hidden_here = up_weight.shape[1]

    qkv_own = qkv_weight.reshape(d, heads_here, 3, width).transpose(0, 2, 1, 3).reshape(d, 3 * lanes)
    bias_own = qv_bias.reshape(heads_here, 2, width).transpose(1, 0, 2).reshape(2 * lanes)
    small = jnp.concatenate([bias_own, up_bias])
    small = jnp.concatenate([small, jnp.zeros((64 * 128 - small.shape[0],), low)]).reshape(64, 128)
    qkv_all, out_all, small_all, up_all, down_all = gather_weights(
        nt, [qkv_own, out_weight, small], [up_weight, down_weight]
    )
    small_all = small_all.reshape(nt, 64 * 128).astype(f32)
    q_bias, v_bias = small_all[:, :lanes], small_all[:, lanes : 2 * lanes]
    up_bias_all = lax.dynamic_index_in_dim(
        small_all[:, 2 * lanes : 2 * lanes + hidden_here].reshape(lines, wide, hidden_here), y, 1, keepdims=False
    )

    padded = jnp.concatenate([jnp.zeros((behind, d), low), tokens])
    near = lax.dynamic_slice_in_dim(padded, t * chunk, span, 0).astype(f32)
    seg_row = jnp.concatenate([jnp.full((behind,), -1, jnp.int32), segment_ids[0]])
    seg_near = lax.dynamic_slice_in_dim(seg_row, t * chunk, span, 0)
    seg_mine = seg_near[behind:]
    distance = (behind + jnp.arange(chunk)[:, None]) - jnp.arange(span)[None, :]
    allowed = (seg_mine[:, None] == seg_near[None, :]) & (distance >= 0)
    dist = jnp.where(allowed, distance.astype(f32), far_off)
    total_heads = heads_here * nt
    slopes = jnp.exp2(-8.0 * (jnp.arange(total_heads, dtype=jnp.int32) + 1).astype(f32) / total_heads)

    gain1, shift1 = first_gain.astype(f32), first_shift.astype(f32)
    gain2, shift2 = second_gain.astype(f32), second_shift.astype(f32)
    xhat1, rate1 = normalized(near)
    normed = (xhat1 * gain1 + shift1).astype(low)
    mine = normed[behind:]
    query = (jnp.einsum("td,gde->gte", mine, qkv_all[:, :, :lanes], preferred_element_type=f32) + q_bias[:, None]).astype(low)
    keys = jnp.einsum("td,gde->gte", normed, qkv_all[:, :, lanes : 2 * lanes], preferred_element_type=f32).astype(low)
    values = (
        jnp.einsum("td,gde->gte", normed, qkv_all[:, :, 2 * lanes :], preferred_element_type=f32) + v_bias[:, None]
    ).astype(low)
    context = attend(slopes, dist, query, keys, values)
    context = context.transpose(1, 0, 2).reshape(chunk, d)
    out_full = out_all.reshape(d, d)
    mixed = jnp.dot(context, out_full, preferred_element_type=f32)
    middle = near[behind:] + mixed + out_bias.astype(f32)
    xhat2, rate2 = normalized(middle)
    second = (xhat2 * gain2 + shift2).astype(low)

    second_pair = group_exchange(nt, second, False, 3, "share_second").reshape(wide * chunk, d)
    cot_pair = lax.dynamic_slice_in_dim(cotangent, z * (wide * chunk), wide * chunk, 0)
    upper = jnp.einsum("td,zdf->ztf", second_pair, up_all, preferred_element_type=f32) + up_bias_all[:, None]
    hidden, slope = gelu_and_slope(upper)
    hidden = hidden.astype(low)
    feed_part = jnp.einsum("ztf,zfd->td", hidden, down_all, preferred_element_type=f32)
    grad_hidden = jnp.einsum("td,zfd->ztf", cot_pair, down_all, preferred_element_type=f32)
    grad_upper = (grad_hidden * slope).astype(low)
    grad_up_bias = jnp.sum(grad_upper.astype(f32), axis=1)
    grad_down = jnp.einsum("ztf,td->zfd", hidden, cot_pair, preferred_element_type=f32).astype(low)
    grad_up = jnp.einsum("td,ztf->zdf", second_pair, grad_upper, preferred_element_type=f32).astype(low)
    second_part = jnp.einsum("ztf,zdf->td", grad_upper, up_all, preferred_element_type=f32)
    terms = group_exchange(nt, second_part.reshape(wide, chunk, d).astype(low), True, 4, "sum_second")
    grad_second = jnp.sum(terms.astype(f32), axis=0)
    feed_part = feed_part.reshape(wide, chunk, d)
    feed_mine = lax.dynamic_index_in_dim(feed_part, y, 0, keepdims=False)
    g_up, g_down, output_all = finish(
        nt, [], [grad_up, grad_down], feed_part.astype(low), middle + down_bias.astype(f32) + feed_mine, None, 1, "finish_mlp"
    )

    cot_mine = lax.dynamic_slice_in_dim(cotangent, t * chunk, chunk, 0).astype(f32)
    grad_middle = cot_mine + norm_input_term(xhat2, rate2, gain2, grad_second)
    grad_middle_low = grad_middle.astype(low)
    grad_out = jnp.dot(context.T, grad_middle_low, preferred_element_type=f32).astype(low).reshape(out_all.shape)
    grad_context = jnp.einsum("td,gcd->gtc", grad_middle_low, out_all, preferred_element_type=f32).astype(low)
    grad_q, grad_k, grad_v = attend_pull(slopes, dist.T, query, keys, values, grad_context)
    grad_kv = jnp.concatenate([grad_k, grad_v], axis=2)
    grad_qkv = jnp.concatenate(
        [
            jnp.einsum("td,gte->gde", mine, grad_q, preferred_element_type=f32),
            jnp.einsum("td,gte->gde", normed, grad_kv, preferred_element_type=f32),
        ],
        axis=2,
    ).astype(low)
    first_part = jnp.einsum("gte,gde->td", grad_kv, qkv_all[:, :, lanes:], preferred_element_type=f32)
    first_mine = first_part[behind:] + jnp.einsum("gte,gde->td", grad_q, qkv_all[:, :, :lanes], preferred_element_type=f32)
    got = halo_exchange(nt, first_part[:behind].astype(low).reshape(halo, chunk, d)).astype(f32)
    there = (t + 1 + jnp.arange(halo)) < nt
    grad_first = first_mine + jnp.sum(jnp.where(there[:, None, None], got, 0.0), axis=0)
    xhat_mine = xhat1[behind:]
    grad_tokens = (grad_middle + norm_input_term(xhat_mine, rate1[behind:], gain1, grad_first)).astype(low)

    up_slots = jnp.where(jnp.arange(wide)[None, :, None] == y, grad_up_bias[:, None, :], 0.0)
    vectors = jnp.concatenate(
        [
            rows_sum(grad_first * xhat_mine), rows_sum(grad_first), rows_sum(grad_middle),
            rows_sum(grad_second * xhat2), rows_sum(grad_second), rows_sum(cot_mine),
            rows_sum(grad_q.astype(f32).transpose(1, 0, 2)).reshape(-1),
            rows_sum(grad_v.astype(f32).transpose(1, 0, 2)).reshape(-1), up_slots.reshape(-1),
        ]
    )
    g_qkv, g_out, grad_tokens_all, vectors = finish(
        nt, [grad_qkv, grad_out], [], grad_tokens, None, vectors.reshape(-1, 128), 5, "finish_attn"
    )
    vectors = vectors.reshape(-1)
    g_first_gain, g_first_shift, g_out_bias, g_second_gain, g_second_shift, g_down_bias = (
        vectors[i * d : (i + 1) * d] for i in range(6)
    )
    rest = vectors[6 * d :]
    g_q = lax.dynamic_index_in_dim(rest[:d].reshape(nt, heads_here, width), t, 0, keepdims=False)
    g_v = lax.dynamic_index_in_dim(rest[d : 2 * d].reshape(nt, heads_here, width), t, 0, keepdims=False)
    g_up_bias = lax.dynamic_index_in_dim(rest[2 * d :].reshape(nt, hidden_here), t, 0, keepdims=False)
    g_qkv = g_qkv.astype(f32).reshape(d, 3, heads_here, width).transpose(0, 2, 1, 3).reshape(d, heads_here, 3 * width)
    return (
        output_all.reshape(length, d), grad_tokens_all.reshape(length, d), g_first_gain, g_first_shift, g_qkv,
        jnp.concatenate([g_q, g_v], axis=1), g_out.astype(f32), g_out_bias, g_second_gain, g_second_shift,
        g_up.astype(f32), g_up_bias, g_down.astype(f32), g_down_bias,
    )


def solution(mesh):
    rows, cols, both = P("dp", None), P(None, "tensor"), P("tensor", None)
    return jax.shard_map(
        per_device,
        mesh=mesh,
        in_specs=(
            rows, rows, P(), P(), P(None, "tensor", None), both, both, P(), P(), P(), cols, P("tensor"), both, P(), rows,
        ),
        out_specs=(
            rows, rows, P(), P(), P(None, "tensor", None), both, both, P(), P(), P(), cols, P("tensor"), both, P(),
        ),
        check_vma=False,
    )
```

```python
import functools
import math

import jax
import jax.numpy as jnp
from jax import lax
from jax.experimental import pallas as pl
from jax.experimental.pallas import tpu as pltpu
from jax.sharding import PartitionSpec as P

MESH = pl.DeviceIdType.MESH
ANY = pl.BlockSpec(memory_space=pl.ANY)
VM = pl.BlockSpec(memory_space=pltpu.VMEM)


def grid_of(n_tensor):
    lines = min(4, n_tensor)
    return lines, n_tensor // lines


def where_am_i(n_tensor):
    lines, wide = grid_of(n_tensor)
    dp, t = lax.axis_index("dp"), lax.axis_index("tensor")
    return dp, t, t // wide, t % wide


def remote(src, dst, send, recv, peer):
    return pltpu.make_async_remote_copy(
        src_ref=src, dst_ref=dst, send_sem=send, recv_sem=recv, device_id=peer, device_id_type=MESH
    )


def when(condition, body):
    pl.when(condition)(body)


def greet(peers):
    barrier = pltpu.get_barrier_semaphore()
    for ok, peer in peers:
        @pl.when(ok)
        def _():
            pl.semaphore_signal(barrier, inc=1, device_id=peer, device_id_type=MESH)
    pl.semaphore_wait(barrier, sum(jnp.int32(ok) for ok, peer in peers))


def neighbours(n_tensor, use_y=True, use_x=True, use_core=True):
    lines, wide = grid_of(n_tensor)
    dp, t, z, y = where_am_i(n_tensor)
    out = [(z > 0, (dp, t - wide)), (z < lines - 1, (dp, t + wide))]
    if use_y:
        out += [(y > 0, (dp, t - 1)), (y < wide - 1, (dp, t + 1))]
    if use_x:
        out.append((dp >= 0, (dp ^ 2, t)))
    if use_core:
        out.append((dp >= 0, (dp ^ 1, t)))
    return out


def gather_kernel(n_tensor, n_attn, n_mlp, *refs):
    lines, wide = grid_of(n_tensor)
    dp, t, z, y = where_am_i(n_tensor)
    n = n_attn + n_mlp
    own, full = refs[:n], refs[n : 2 * n]
    z_send, z_recv, y_send, y_recv, x_send, x_recv, c_send, c_recv, l_sem = refs[2 * n :]
    quad = dp % 4

    def slot(a, zz, yy):
        return zz * wide + yy if a < n_attn else zz

    def piece(ref, a, q):
        rows = own[a].shape[0] // 4
        return ref.at[pl.ds(pl.multiple_of(q * rows, rows), rows)]

    def block(a, zz, yy, q):
        return piece(full[a].at[slot(a, zz, yy)], a, q)

    def copy(src, dst, send, recv, peer):
        return pltpu.make_async_remote_copy(
            src_ref=src, dst_ref=dst, send_sem=send, recv_sem=recv, device_id=peer, device_id_type=MESH
        )

    greet(neighbours(n_tensor))
    local = [pltpu.make_async_copy(own[a], full[a].at[slot(a, z, y)], l_sem.at[a]) for a in range(n)]
    for c in local:
        c.start()
    up, down = (dp, t + wide), (dp, t - wide)

    def z_copy(a, zz, side, mine=False):
        src = piece(own[a], a, quad) if mine else block(a, zz, y, quad)
        return copy(src, block(a, zz, y, quad), z_send.at[side, a, zz], z_recv.at[side, a, zz], (up, down)[side])

    def y_copy(a, zz, yy, side, mine=False):
        src = piece(own[a], a, quad) if mine else block(a, zz, yy, quad)
        peer = ((dp, t + 1), (dp, t - 1))[side]
        return copy(src, block(a, zz, yy, quad), y_send.at[side, a, zz, yy], y_recv.at[side, a, zz, yy], peer)

    def x_copy(a, zz, yy, q):
        return copy(block(a, zz, yy, q), block(a, zz, yy, q), x_send.at[a, zz, yy], x_recv.at[a, zz, yy], (dp ^ 2, t))

    def c_copy(a, zz, yy, q, hop):
        return copy(
            block(a, zz, yy, q), block(a, zz, yy, q), c_send.at[hop, a, zz, yy], c_recv.at[hop, a, zz, yy], (dp ^ 1, t)
        )

    def spread(a, zz, yy):
        x_copy(a, zz, yy, quad).start()
        c_copy(a, zz, yy, quad, 0).start()

    def arrays(group):
        return range(n_attn) if group == 0 else range(n_attn, n)

    def y_start(zz, yy, side, mine=False):
        @pl.when((y < wide - 1) if side == 0 else (y > 0))
        def _():
            for a in range(n_attn):
                y_copy(a, zz, yy, side, mine).start()

    for group in range(2):
        for side in range(2):
            @pl.when((z < lines - 1) if side == 0 else (z > 0))
            def _():
                for a in arrays(group):
                    z_copy(a, z, side, True).start()
        if group == 0:
            for side in range(2):
                y_start(z, y, side, True)
    for group in range(2):
        for k in range(1, lines):
            for side in range(2):
                zz = z - k if side == 0 else z + k

                @pl.when((zz >= 0) if side == 0 else (zz < lines))
                def _():
                    for a in arrays(group):
                        z_copy(a, zz, side).wait_recv()

                    @pl.when((z < lines - 1) if side == 0 else (z > 0))
                    def _():
                        for a in arrays(group):
                            z_copy(a, zz, side).start()

                    if group == 0:
                        for s in range(2):
                            y_start(zz, y, s)
                    for a in arrays(group):
                        spread(a, zz, y)
        if group == 0:
            for m in range(1, wide):
                for side in range(2):
                    yy = y - m if side == 0 else y + m

                    @pl.when((yy >= 0) if side == 0 else (yy < wide))
                    def _():
                        for zz in range(lines):
                            for a in range(n_attn):
                                y_copy(a, zz, yy, side).wait_recv()
                            if m < wide - 1:
                                y_start(zz, yy, side)
                            for a in range(n_attn):
                                spread(a, zz, yy)
    def others(group, body):
        for zz in range(lines):
            for yy in range(wide) if group == 0 else [y]:
                @pl.when((zz != z) | (yy != y))
                def _():
                    body(zz, yy)

    for group in range(2):
        def pass_on(zz, yy):
            for a in arrays(group):
                x_copy(a, zz, yy, quad ^ 2).wait_recv()
                c_copy(a, zz, yy, quad ^ 2, 1).start()

        others(group, pass_on)
    for group in range(2):
        def settle(zz, yy):
            for a in arrays(group):
                for hop in range(2):
                    c_copy(a, zz, yy, quad ^ (1 + 2 * hop), hop).wait_recv()
                    c_copy(a, zz, yy, quad ^ (2 * hop), hop).wait_send()
                x_copy(a, zz, yy, quad).wait_send()

        others(group, settle)
        for side in range(2):
            @pl.when((z < lines - 1) if side == 0 else (z > 0))
            def _():
                for k in range(lines):
                    zz = z - k if side == 0 else z + k

                    @pl.when((zz >= 0) if side == 0 else (zz < lines))
                    def _():
                        for a in arrays(group):
                            z_copy(a, zz, side).wait_send()
    for side in range(2):
        @pl.when((y < wide - 1) if side == 0 else (y > 0))
        def _():
            for zz in range(lines):
                for m in range(wide):
                    yy = y - m if side == 0 else y + m

                    @pl.when((yy >= 0) if side == 0 else (yy < wide))
                    def _():
                        for a in range(n_attn):
                            y_copy(a, zz, yy, side).wait_send()
    for c in local:
        c.wait()


def gather_weights(n_tensor, attn, mlp):
    lines, wide = grid_of(n_tensor)
    n = len(attn) + len(mlp)
    arrays = list(attn) + list(mlp)
    outs = [
        jax.ShapeDtypeStruct(((n_tensor if i < len(attn) else lines),) + a.shape, a.dtype) for i, a in enumerate(arrays)
    ]
    dma = pltpu.SemaphoreType.DMA
    return pl.pallas_call(
        functools.partial(gather_kernel, n_tensor, len(attn), len(mlp)),
        out_shape=outs,
        in_specs=[ANY] * n,
        out_specs=[ANY] * n,
        scratch_shapes=[dma((2, n, lines))] * 2
        + [dma((2, len(attn), lines, wide))] * 2
        + [dma((n, lines, wide))] * 2
        + [dma((2, n, lines, wide))] * 2
        + [dma((n,))],
        compiler_params=pltpu.CompilerParams(collective_id=0, has_side_effects=True),
        name="gather_weights",
    )(*arrays)


def add_rows(dst, terms):
    rows = dst.shape[0]
    step = 32 if rows % 32 == 0 else rows

    @pl.loop(0, rows // step)
    def _(i):
        part = pl.ds(pl.multiple_of(i * step, step), step)
        total = terms[0][part].astype(jnp.float32)
        for term in terms[1:]:
            total = total + term[part].astype(jnp.float32)
        dst[part] = total.astype(dst.dtype)


def doubling_peers(n_tensor):
    dp, t, z, y = where_am_i(n_tensor)
    bits = lambda size: [1 << i for i in range((size - 1).bit_length())]
    return [(dp ^ b, t) for b in bits(lax.axis_size("dp"))] + [(dp, t ^ b) for b in bits(n_tensor)]


def doubling_program(n_tensor, own, out, total, got, send, recv):
    peers = doubling_peers(n_tensor)

    def step(i):
        return remote(total.at[i], got.at[i], send.at[i], recv.at[i], peers[i])

    def begin():
        total[0] = own[...]
        step(0).start()

    def advance(i):
        step(i).wait_recv()
        if i + 1 < len(peers):
            total[i + 1] = total[i] + got[i]
            step(i + 1).start()
        else:
            out[...] = total[i] + got[i]

    def settle():
        for i in range(len(peers)):
            step(i).wait_send()

    return [begin] + [functools.partial(advance, i) for i in range(len(peers))] + [settle]


def finish_kernel(n_tensor, n_attn, n_mlp, with_feed, with_vectors, pull, *refs):
    lines, wide = grid_of(n_tensor)
    dp, t, z, y = where_am_i(n_tensor)
    n = n_attn + n_mlp
    refs = list(refs)

    def take(count):
        got, refs[:] = refs[:count], refs[count:]
        return got

    terms, rows_own = take(n), take(1)
    feed_base = take(1)[0] if with_feed else None
    vec_own = take(1)[0] if with_vectors else None
    pull_in = take(pull_inputs) if pull else []
    final, rows_full = take(n), take(1)
    vec_out = take(1)[0] if with_vectors else None
    pull_out = take(pull_outputs) if pull else []
    from_c, from_x, to_x, acc, from_y, from_z = (take(n) for i in range(6))
    c_send, c_recv, x_send, x_recv, y_send, y_recv, z_send, z_recv, q_send, q_recv = take(10)
    rows_sems = take(5)
    if with_feed:
        feed_parts, (feed_got, feed_sum), (f_send, f_recv) = rows_own[0], take(2), take(2)
        rows_own = [feed_sum]
    rows_steps = rows_program(n_tensor, rows_own, rows_full, *rows_sems)
    vec_steps = doubling_program(n_tensor, vec_own, vec_out, *take(4)) if with_vectors else []
    work, pull_peers, pull_end = pull_program(n_tensor, pull, pull_in, pull_out, refs) if pull else (None, [], None)
    quad = dp % 4
    side_x = quad // 2
    core = quad % 2
    core_peer, x_peer = (dp ^ 1, t), (dp ^ 2, t)

    lines_order = [i // 2 if i % 2 else lines - 1 - i // 2 for i in range(lines)]

    def across(a):
        return [(y + 1 + m) % wide for m in range(wide)] if a < n_attn else [0]

    def slots(a):
        return [(zz, yy) for zz in lines_order for yy in across(a)]

    def index(a, zz, yy):
        return zz * wide + yy if a < n_attn else zz

    def quarter(ref, a, q):
        rows = final[a].shape[0] // 4
        return ref.at[pl.ds(pl.multiple_of(q * rows, rows), rows)]

    def c_copy(a, s, h):
        return remote(
            quarter(terms[a].at[s], a, h * 2 + 1 - core), from_c[a].at[s, h], c_send.at[a, s, h], c_recv.at[a, s, h],
            core_peer,
        )

    def x_copy(a, s):
        return remote(to_x[a].at[s], from_x[a].at[s], x_send.at[a, s], x_recv.at[a, s], x_peer)

    def y_copy(a, zz, yy, side):
        peer = ((dp, t + 1), (dp, t - 1))[side]
        lane = zz * wide + yy
        return remote(acc[a].at[lane], from_y[a].at[side, lane], y_send.at[side, a, lane], y_recv.at[side, a, lane], peer)

    def z_copy(a, zz, side):
        peer = ((dp, t + wide), (dp, t - wide))[side]
        return remote(
            acc[a].at[index(a, zz, y)], from_z[a].at[side, zz], z_send.at[side, a, zz], z_recv.at[side, a, zz], peer
        )

    def core_stage(a, zz, yy):
        s = index(a, zz, yy)
        for h in range(2):
            c_copy(a, s, h).wait_recv()
        add_rows(to_x[a].at[s], [quarter(terms[a].at[s], a, (1 - side_x) * 2 + core), from_c[a].at[s, 1 - side_x]])
        x_copy(a, s).start()
        add_rows(acc[a].at[s], [quarter(terms[a].at[s], a, quad), from_c[a].at[s, side_x]])

    def x_stage(a, zz, yy):
        s = index(a, zz, yy)
        x_copy(a, s).wait_recv()
        add_rows(acc[a].at[s], [acc[a].at[s], from_x[a].at[s]])
        if a < n_attn:
            when((y == 0) & (yy > y), lambda: y_copy(a, zz, yy, 0).start())
            when((y == wide - 1) & (yy < y), lambda: y_copy(a, zz, yy, 1).start())

    def y_stage(a, zz):
        for k in range(wide):
            for side, yy in ((0, wide - 1 - k), (1, k)):
                @pl.when(((yy >= y) & (y > 0)) if side == 0 else ((yy <= y) & (y < wide - 1)))
                def _():
                    lane = zz * wide + yy
                    y_copy(a, zz, yy, side).wait_recv()
                    add_rows(acc[a].at[lane], [acc[a].at[lane], from_y[a].at[side, lane]])
                    when(yy != y, lambda: y_copy(a, zz, yy, side).start())

    def z_round(r):
        for side in range(2):
            zz = lines - 1 - r + z if side == 0 else z - (lines - 1 - r)

            @pl.when((zz < lines) & (zz >= 0))
            def _():
                @pl.when((z > 0) if side == 0 else (z < lines - 1))
                def _():
                    for a in order:
                        s = index(a, zz, y)
                        z_copy(a, zz, side).wait_recv()
                        add_rows(acc[a].at[s], [acc[a].at[s], from_z[a].at[side, zz]])

                if r < lines - 1:
                    for a in order:
                        z_copy(a, zz, side).start()

    def q_copy(a, q, hop, peer):
        return remote(quarter(final[a], a, q), quarter(final[a], a, q), q_send.at[hop, a], q_recv.at[hop, a], peer)

    def home(a):
        add_rows(quarter(final[a], a, quad), [acc[a].at[index(a, z, y)]])
        q_copy(a, quad, 0, x_peer).start()
        q_copy(a, quad, 1, core_peer).start()

    def feed_copy(yy, slot):
        return remote(feed_parts.at[yy], feed_got.at[slot], f_send.at[yy], f_recv.at[slot], (dp, z * wide + yy))

    def feed_start():
        for yy in range(wide):
            when(yy != y, lambda: feed_copy(yy, y).start())

    def feed_end():
        feed_got[y] = jnp.zeros(feed_got.shape[1:], feed_got.dtype)
        for yy in range(wide):
            when(yy != y, lambda: feed_copy(yy, yy).wait_recv())
        add_rows(feed_sum, [feed_base] + [feed_got.at[yy] for yy in range(wide)])
        for yy in range(wide):
            when(yy != y, lambda: feed_copy(yy, y).wait_send())

    peers = neighbours(n_tensor) + pull_peers
    if with_feed and wide > 2:
        peers += [(yy != y, (dp, z * wide + yy)) for yy in range(wide)]
    if with_vectors:
        peers += [(dp >= 0, peer) for peer in doubling_peers(n_tensor)]
    greet(peers)
    attn, mlp = list(range(n_attn)), list(range(n_attn, n))
    order = attn + mlp
    if with_feed:
        feed_start()
    else:
        rows_steps.pop(0)()
    for a in order:
        for zz, yy in slots(a):
            for h in range(2):
                c_copy(a, index(a, zz, yy), h).start()
    if with_vectors:
        vec_steps.pop(0)()
    for zz, yy in slots(0):
        for a in order:
            core_stage(a, zz, yy)
    if with_feed:
        feed_end()
        rows_steps.pop(0)()

    def aside():
        if len(rows_steps) > 1:
            rows_steps.pop(0)()
        if len(vec_steps) > 1:
            vec_steps.pop(0)()

    def x_part(zz):
        for a in order:
            for yy in across(a):
                x_stage(a, zz, yy)

    def turn(i, r):
        for zz in lines_order[i : i + 2]:
            for a in attn:
                y_stage(a, zz)
        aside()
        z_round(r)

    def late(r):
        aside()
        z_round(r)

    steps = []
    for i in range(0, lines, 2):
        steps += [functools.partial(x_part, zz) for zz in lines_order[i : i + 2]]
        steps.append(functools.partial(turn, i, i // 2))
    steps += [functools.partial(late, r) for r in range((lines + 1) // 2, lines)]
    if work:
        @pl.loop(0, n_tensor)
        def _(p):
            work(p)
            for k in range(1, n_tensor):
                if steps:
                    when(p == k, steps.pop(0))

        pull_end[0]()
    for step in steps:
        step()
    for a in order:
        home(a)
    aside()
    for a in order:
        q_copy(a, quad ^ 2, 0, x_peer).wait_recv()
        q_copy(a, quad ^ 2, 2, core_peer).start()
    if work:
        pull_end[1]()
    while rows_steps:
        rows_steps.pop(0)()
    while vec_steps:
        vec_steps.pop(0)()
    for a in order:
        q_copy(a, quad ^ 1, 1, core_peer).wait_recv()
        q_copy(a, quad ^ 3, 2, core_peer).wait_recv()
        q_copy(a, quad, 0, x_peer).wait_send()
        q_copy(a, quad, 1, core_peer).wait_send()
        q_copy(a, quad ^ 2, 2, core_peer).wait_send()
        for zz, yy in slots(a):
            s = index(a, zz, yy)
            for h in range(2):
                c_copy(a, s, h).wait_send()
            x_copy(a, s).wait_send()
            if a < n_attn:
                when(yy > y, lambda: y_copy(a, zz, yy, 0).wait_send())
                when(yy < y, lambda: y_copy(a, zz, yy, 1).wait_send())
        for zz in range(lines):
            when(zz > z, lambda: z_copy(a, zz, 0).wait_send())
            when(zz < z, lambda: z_copy(a, zz, 1).wait_send())


def finish(n_tensor, attn, mlp, rows, base, vectors, cid, name, pull=None):
    lines, wide = grid_of(n_tensor)
    arrays = list(attn) + list(mlp)
    n = len(arrays)
    vm, dma = pltpu.VMEM, pltpu.SemaphoreType.DMA
    quarters = [(a.shape[1] // 4, a.shape[2]) for a in arrays]
    low = jnp.bfloat16
    each = lambda lead: [vm(lead(a, i) + q, low) for i, (a, q) in enumerate(zip(arrays, quarters))]
    slots = lambda a, i: (a.shape[0],)
    steps = (lax.axis_size("dp") - 1).bit_length() + (n_tensor - 1).bit_length()
    scratch = (
        each(lambda a, i: (a.shape[0], 2))
        + each(slots) + each(slots) + each(slots)
        + each(lambda a, i: (2, n_tensor) if i < len(attn) else (1, 1))
        + each(lambda a, i: (2, lines))
    )
    sems = (
        [dma((n, n_tensor, 2))] * 2 + [dma((n, n_tensor))] * 2 + [dma((2, max(1, len(attn)), n_tensor))] * 2
        + [dma((2, n, lines))] * 2 + [dma((3, n))] * 2
        + [dma((2, 1, lines))] * 2 + [dma((2, 1, lines, wide))] * 2 + [dma((1,))]
    )
    inputs, in_specs = arrays + [rows], [VM] * n + [ANY]
    chunk = rows.shape[-2:]
    out_shape = [jax.ShapeDtypeStruct(a.shape[1:], a.dtype) for a in arrays]
    out_shape.append(jax.ShapeDtypeStruct((n_tensor,) + chunk, low))
    out_specs = [VM] * n + [ANY]
    if base is not None:
        inputs, in_specs = inputs + [base], in_specs + [VM]
        sems += [vm((wide,) + chunk, low), vm(chunk, low), dma((wide,)), dma((wide,))]
    if vectors is not None:
        inputs, in_specs = inputs + [vectors], in_specs + [VM]
        out_shape.append(jax.ShapeDtypeStruct(vectors.shape, vectors.dtype))
        out_specs.append(VM)
        sems += [vm((steps,) + vectors.shape, jnp.float32)] * 2 + [dma((steps,))] * 2
    heads = 0
    if pull is not None:
        heads = pull[0].shape[0] // n_tensor
        inputs, in_specs = inputs + list(pull), in_specs + [pl.BlockSpec(memory_space=pltpu.SMEM)] + [VM] * (pull_inputs - 1)
        shapes, more = pull_shapes(n_tensor, pull)
        out_shape += shapes
        out_specs += [VM] * pull_outputs
        sems += more
    out = pl.pallas_call(
        functools.partial(
            finish_kernel, n_tensor, len(attn), len(mlp), base is not None, vectors is not None, heads
        ),
        out_shape=out_shape,
        in_specs=in_specs,
        out_specs=out_specs,
        scratch_shapes=scratch + sems,
        compiler_params=pltpu.CompilerParams(collective_id=cid, has_side_effects=True, vmem_limit_bytes=60 * 2**20),
        name=name,
    )(*inputs)
    sums = out[:n]
    if lax.axis_size("dp") > 4:
        sums = [lax.psum(s, "dp").astype(jnp.float32) * 0.25 for s in sums]
    return list(sums) + list(out[n:])


def group_kernel(n_tensor, scatter, own, full, send, recv, l_sem):
    lines, wide = grid_of(n_tensor)
    dp, t, z, y = where_am_i(n_tensor)
    peers = [(y != yy, (dp, z * wide + yy)) for yy in range(wide)]
    greet(peers)
    local = pltpu.make_async_copy(own.at[y] if scatter else own, full.at[y], l_sem)
    local.start()

    def step(yy, slot):
        return pltpu.make_async_remote_copy(
            src_ref=own.at[yy] if scatter else own, dst_ref=full.at[slot], send_sem=send.at[yy], recv_sem=recv.at[slot],
            device_id=peers[yy][1], device_id_type=MESH,
        )

    for yy in range(wide):
        @pl.when(peers[yy][0])
        def _():
            step(yy, y).start()
    for yy in range(wide):
        @pl.when(peers[yy][0])
        def _():
            step(yy, yy).wait_recv()
            step(yy, y).wait_send()
    local.wait()


def group_exchange(n_tensor, own, scatter, cid, name):
    lines, wide = grid_of(n_tensor)
    dma = pltpu.SemaphoreType.DMA
    shape = own.shape if scatter else (wide,) + own.shape
    return pl.pallas_call(
        functools.partial(group_kernel, n_tensor, scatter),
        out_shape=jax.ShapeDtypeStruct(shape, own.dtype),
        in_specs=[ANY],
        out_specs=ANY,
        scratch_shapes=[dma((wide,)), dma((wide,)), dma],
        compiler_params=pltpu.CompilerParams(collective_id=cid, has_side_effects=True),
        name=name,
    )(own)


def rows_program(n_tensor, own, full, z_send, z_recv, y_send, y_recv, l_sem):
    lines, wide = grid_of(n_tensor)
    dp, t, z, y = where_am_i(n_tensor)
    n = len(own)

    def z_copy(a, zz, side, mine=False):
        dst = full[a].at[zz * wide + y]
        peer = ((dp, t + wide), (dp, t - wide))[side]
        return remote(own[a] if mine else dst, dst, z_send.at[side, a, zz], z_recv.at[side, a, zz], peer)

    def y_copy(a, zz, yy, side, mine=False):
        dst = full[a].at[zz * wide + yy]
        peer = ((dp, t + 1), (dp, t - 1))[side]
        return remote(own[a] if mine else dst, dst, y_send.at[side, a, zz, yy], y_recv.at[side, a, zz, yy], peer)

    z_has = ((z < lines - 1), (z > 0))
    y_has = ((y < wide - 1), (y > 0))
    local = [pltpu.make_async_copy(own[a], full[a].at[t], l_sem.at[a]) for a in range(n)]

    def begin():
        for side in range(2):
            for a in range(n):
                when(z_has[side], lambda: z_copy(a, z, side, True).start())
                when(y_has[side], lambda: y_copy(a, z, y, side, True).start())
        for c in local:
            c.start()

    def along_z(k):
        for side in range(2):
            zz = z - k if side == 0 else z + k

            @pl.when((zz >= 0) & (zz < lines))
            def _():
                for a in range(n):
                    z_copy(a, zz, side).wait_recv()
                    when(z_has[side], lambda: z_copy(a, zz, side).start())
                    for s in range(2):
                        when(y_has[s], lambda: y_copy(a, zz, y, s).start())

    def along_y(m):
        for side in range(2):
            yy = y - m if side == 0 else y + m

            @pl.when((yy >= 0) & (yy < wide))
            def _():
                for zz in range(lines):
                    for a in range(n):
                        y_copy(a, zz, yy, side).wait_recv()
                        if m < wide - 1:
                            when(y_has[side], lambda: y_copy(a, zz, yy, side).start())

    def settle():
        for side in range(2):
            for k in range(lines):
                zz = z - k if side == 0 else z + k

                @pl.when(z_has[side] & (zz >= 0) & (zz < lines))
                def _():
                    for a in range(n):
                        z_copy(a, zz, side).wait_send()
            for m in range(wide):
                yy = y - m if side == 0 else y + m

                @pl.when(y_has[side] & (yy >= 0) & (yy < wide))
                def _():
                    for zz in range(lines):
                        for a in range(n):
                            y_copy(a, zz, yy, side).wait_send()
        for c in local:
            c.wait()

    return (
        [begin]
        + [functools.partial(along_z, k) for k in range(1, lines)]
        + [functools.partial(along_y, m) for m in range(1, wide)]
        + [settle]
    )


def dot(a, b, contract, **kwargs):
    return lax.dot_general(a, b, (contract, ((), ())), preferred_element_type=jnp.float32, **kwargs)


NN, NT, TN = ((1,), (0,)), ((1,), (1,)), ((0,), (0,))


def head_of_lane(shape, heads):
    return lax.broadcasted_iota(jnp.int32, shape, 1) // (shape[1] // heads)


def attend_kernel(heads, slopes, dist, q, k, v, ctx):
    pair = pl.program_id(0)
    lanes = q.shape[2]
    scale = 1.0 / math.sqrt(lanes // heads)
    query, keys, values = q[0], k[0], v[0]
    head = head_of_lane(query.shape, heads)
    out = jnp.zeros(query.shape, jnp.float32)
    for h in range(heads):
        masked = jnp.where(head == h, query * jnp.bfloat16(scale), jnp.bfloat16(0))
        scores = dot(masked, keys, NT) - slopes[pair * heads + h] * dist[...]
        peak = jnp.max(scores, axis=1, keepdims=True)
        expo = jnp.exp(scores - peak)
        total = jnp.sum(expo, axis=1, keepdims=True)
        part = dot(expo.astype(jnp.bfloat16), values, NN) / total
        out = jnp.where(head == h, part, out)
    ctx[0] = out.astype(jnp.bfloat16)


def pull_scores(heads, slope_of, dist, query, keys, values, grad):
    lanes = query.shape[1]
    scale = 1.0 / math.sqrt(lanes // heads)
    head = head_of_lane(query.shape, heads)
    head_rows = lax.broadcasted_iota(jnp.int32, (lanes, query.shape[0]), 0) // (lanes // heads)
    low = jnp.bfloat16
    grad_q = jnp.zeros((lanes, query.shape[0]), jnp.float32)
    grad_k = jnp.zeros(keys.shape, jnp.float32)
    grad_v = jnp.zeros(keys.shape, jnp.float32)
    for h in range(heads):
        masked = jnp.where(head == h, query * low(scale), low(0))
        masked_grad = jnp.where(head == h, grad, low(0))
        scores = dot(keys, masked, NT) - slope_of(h) * dist[...]
        peak = jnp.max(scores, axis=0, keepdims=True)
        expo = jnp.exp(scores - peak)
        probs = expo * (1.0 / jnp.sum(expo, axis=0, keepdims=True))
        grad_probs = dot(values, masked_grad, NT)
        inner = jnp.sum(probs * grad_probs, axis=0, keepdims=True)
        grad_scores = (probs * (grad_probs - inner)).astype(low)
        grad_v = grad_v + dot(probs.astype(low), masked_grad, NN)
        grad_k = grad_k + dot(grad_scores, masked, NN)
        grad_q = jnp.where(head_rows == h, dot(keys, grad_scores, TN), grad_q)
    return (jnp.transpose(grad_q) * scale).astype(low), grad_k.astype(low), grad_v.astype(low)


pull_inputs, pull_outputs = 10, 5


def pull_shapes(n_tensor, pull):
    slopes, dist, q, k, v, grad, context, out_all, qkv_all, normed_t = pull
    span, chunk, lanes, d = k.shape[1], q.shape[1], q.shape[2], normed_t.shape[0]
    halo = (span - chunk) // chunk
    low, f32 = jnp.bfloat16, jnp.float32
    shape = jax.ShapeDtypeStruct
    vm, dma = pltpu.VMEM, pltpu.SemaphoreType.DMA
    outs = [
        shape(qkv_all.shape, low), shape(out_all.shape, low), shape((chunk, d), f32),
        shape((n_tensor, 8, lanes), f32), shape((n_tensor, 8, lanes), f32),
    ]
    scratch = [
        vm(q.shape, low), vm((n_tensor, span, 2 * lanes), low), vm((halo, chunk, d), low), vm((halo, chunk, d), low),
        dma((halo,)), dma((halo,)),
    ]
    return outs, scratch


def pull_program(n_tensor, heads, ins, outs, scratch):
    dp, t, z, y = where_am_i(n_tensor)
    slopes, dist, q, k, v, grad, context, out_all, qkv_all, normed_t = ins
    grad_qkv, grad_out, first, q_sum, v_sum = outs
    grad_q, grad_kv, halo_own, halo_got, h_send, h_recv = scratch
    halo, chunk, d = halo_own.shape
    span, lanes = k.shape[1], q.shape[2]
    behind = span - chunk
    low, f32 = jnp.bfloat16, jnp.float32

    def work(p):
        grad_context = dot(grad[...], out_all[p], NT).astype(low)
        grad_out[p] = dot(context[p], grad[...], TN).astype(low)
        gq, gk, gv = pull_scores(heads, lambda h: slopes[p * heads + h], dist, q[p], k[p], v[p], grad_context)
        grad_q[p] = gq
        grad_kv[p, :, :lanes] = gk
        grad_kv[p, :, lanes:] = gv
        q_sum[p] = jnp.broadcast_to(jnp.sum(gq.astype(f32), axis=0, keepdims=True), (8, lanes))
        v_sum[p] = jnp.broadcast_to(jnp.sum(gv.astype(f32), axis=0, keepdims=True), (8, lanes))
        grad_qkv[p, :, :lanes] = dot(normed_t[:, behind:], gq, NN).astype(low)
        grad_qkv[p, :, lanes:] = dot(normed_t[...], grad_kv[p], NN).astype(low)

    def step(m):
        return remote(halo_own.at[halo - 1 - m], halo_got.at[m], h_send.at[m], h_recv.at[m], (dp, t - 1 - m))

    ahead = [(t + 1 + m < n_tensor, (dp, t + 1 + m)) for m in range(halo)]
    back = [(t - 1 - m >= 0, (dp, t - 1 - m)) for m in range(halo)]
    tile = min(128, chunk)

    def rows_first():
        for j in range(halo):
            @pl.loop(0, chunk // tile)
            def _(i):
                here = pl.multiple_of(i * tile, tile)
                total = jnp.zeros((tile, d), f32)
                for p in range(n_tensor):
                    total = total + dot(grad_kv[p, pl.ds(j * chunk + here, tile)], qkv_all[p, :, lanes:], NT)
                halo_own[j, pl.ds(here, tile)] = total.astype(low)

        for m in range(halo):
            when(back[m][0], lambda: step(m).start())

        @pl.loop(0, chunk // tile)
        def _(i):
            here = pl.multiple_of(i * tile, tile)
            total = jnp.zeros((tile, d), f32)
            for p in range(n_tensor):
                total = total + dot(grad_kv[p, pl.ds(behind + here, tile)], qkv_all[p, :, lanes:], NT)
                total = total + dot(grad_q[p, pl.ds(here, tile)], qkv_all[p, :, :lanes], NT)
            first[pl.ds(here, tile)] = total

    def rows_last():
        for m in range(halo):
            @pl.when(ahead[m][0])
            def _():
                step(m).wait_recv()
                add_rows(first, [first, halo_got.at[m]])

            when(back[m][0], lambda: step(m).wait_send())

    return work, ahead + back, (rows_first, rows_last)


def by_shard(array):
    return pl.BlockSpec((1,) + array.shape[1:], lambda p: (p, 0, 0))


def attend(slopes, dist, q, k, v):
    heads = slopes.shape[0] // q.shape[0]
    return pl.pallas_call(
        functools.partial(attend_kernel, heads),
        grid=(q.shape[0],),
        out_shape=jax.ShapeDtypeStruct(q.shape, jnp.bfloat16),
        in_specs=[pl.BlockSpec(memory_space=pltpu.SMEM), pl.BlockSpec(dist.shape, lambda p: (0, 0))]
        + [by_shard(a) for a in (q, k, v)],
        out_specs=by_shard(q),
        compiler_params=pltpu.CompilerParams(vmem_limit_bytes=50 * 2**20),
        name="attend",
    )(slopes, dist, q, k, v)


norm_eps = 1e-05


def normalized(values):
    offset = values - jnp.mean(values, axis=-1, keepdims=True)
    rate = lax.rsqrt(jnp.mean(offset * offset, axis=-1, keepdims=True) + norm_eps)
    return offset * rate, rate


def norm_input_term(xhat, rate, gain, grad):
    e = grad * gain
    return rate * (e - jnp.mean(e, axis=-1, keepdims=True) - xhat * jnp.mean(e * xhat, axis=-1, keepdims=True))


def gelu_and_slope(u):
    c, a = 0.7978845608028654, 0.044715
    th = jnp.tanh(c * (u + a * u * u * u))
    slope = 0.5 * (1.0 + th) + 0.5 * u * (1.0 - th * th) * (c * (1.0 + 3.0 * a * u * u))
    return 0.5 * u * (1.0 + th), slope


far_off = 1e33
longest = 512


def rows_sum(v):
    return jnp.sum(v, axis=0)


def per_device(
    tokens, segment_ids, first_gain, first_shift, qkv_weight, qv_bias, out_weight, out_bias, second_gain, second_shift,
    up_weight, up_bias, down_weight, down_bias, cotangent,
):
    low, f32 = jnp.bfloat16, jnp.float32
    nt = lax.axis_size("tensor")
    lines, wide = grid_of(nt)
    t = lax.axis_index("tensor")
    z, y = t // wide, t % wide
    length, d = tokens.shape
    chunk = length // nt
    halo = -(-(longest - 1) // chunk)
    behind = halo * chunk
    span = behind + chunk
    heads_here, width = qkv_weight.shape[1], qkv_weight.shape[2] // 3
    lanes = heads_here * width
    hidden_here = up_weight.shape[1]

    qkv_own = qkv_weight.reshape(d, heads_here, 3, width).transpose(0, 2, 1, 3).reshape(d, 3 * lanes)
    bias_own = qv_bias.reshape(heads_here, 2, width).transpose(1, 0, 2).reshape(2 * lanes)
    small = jnp.concatenate([bias_own, up_bias])
    small = jnp.concatenate([small, jnp.zeros((64 * 128 - small.shape[0],), low)]).reshape(64, 128)
    qkv_all, out_all, small_all, up_all, down_all = gather_weights(
        nt, [qkv_own, out_weight, small], [up_weight, down_weight]
    )
    small_all = small_all.reshape(nt, 64 * 128).astype(f32)
    q_bias, v_bias = small_all[:, :lanes], small_all[:, lanes : 2 * lanes]
    up_bias_all = lax.dynamic_index_in_dim(
        small_all[:, 2 * lanes : 2 * lanes + hidden_here].reshape(lines, wide, hidden_here), y, 1, keepdims=False
    )

    padded = jnp.concatenate([jnp.zeros((behind, d), low), tokens])
    near = lax.dynamic_slice_in_dim(padded, t * chunk, span, 0).astype(f32)
    seg_row = jnp.concatenate([jnp.full((behind,), -1, jnp.int32), segment_ids[0]])
    seg_near = lax.dynamic_slice_in_dim(seg_row, t * chunk, span, 0)
    seg_mine = seg_near[behind:]
    distance = (behind + jnp.arange(chunk)[:, None]) - jnp.arange(span)[None, :]
    allowed = (seg_mine[:, None] == seg_near[None, :]) & (distance >= 0)
    dist = jnp.where(allowed, distance.astype(f32), far_off)
    total_heads = heads_here * nt
    slopes = jnp.exp2(-8.0 * (jnp.arange(total_heads, dtype=jnp.int32) + 1).astype(f32) / total_heads)

    gain1, shift1 = first_gain.astype(f32), first_shift.astype(f32)
    gain2, shift2 = second_gain.astype(f32), second_shift.astype(f32)
    xhat1, rate1 = normalized(near)
    normed = (xhat1 * gain1 + shift1).astype(low)
    mine = normed[behind:]
    query = (jnp.einsum("td,gde->gte", mine, qkv_all[:, :, :lanes], preferred_element_type=f32) + q_bias[:, None]).astype(low)
    keys = jnp.einsum("td,gde->gte", normed, qkv_all[:, :, lanes : 2 * lanes], preferred_element_type=f32).astype(low)
    values = (
        jnp.einsum("td,gde->gte", normed, qkv_all[:, :, 2 * lanes :], preferred_element_type=f32) + v_bias[:, None]
    ).astype(low)
    context_by_shard = attend(slopes, dist, query, keys, values)
    context = context_by_shard.transpose(1, 0, 2).reshape(chunk, d)
    out_full = out_all.reshape(d, d)
    mixed = jnp.dot(context, out_full, preferred_element_type=f32)
    middle = near[behind:] + mixed + out_bias.astype(f32)
    xhat2, rate2 = normalized(middle)
    second = (xhat2 * gain2 + shift2).astype(low)

    second_pair = group_exchange(nt, second, False, 3, "share_second").reshape(wide * chunk, d)
    cot_pair = lax.dynamic_slice_in_dim(cotangent, z * (wide * chunk), wide * chunk, 0)
    upper = jnp.einsum("td,zdf->ztf", second_pair, up_all, preferred_element_type=f32) + up_bias_all[:, None]
    hidden, slope = gelu_and_slope(upper)
    hidden = hidden.astype(low)
    feed_part = jnp.einsum("ztf,zfd->td", hidden, down_all, preferred_element_type=f32)
    grad_hidden = jnp.einsum("td,zfd->ztf", cot_pair, down_all, preferred_element_type=f32)
    grad_upper = (grad_hidden * slope).astype(low)
    grad_up_bias = jnp.sum(grad_upper.astype(f32), axis=1)
    grad_down = jnp.einsum("ztf,td->zfd", hidden, cot_pair, preferred_element_type=f32).astype(low)
    grad_up = jnp.einsum("td,ztf->zdf", second_pair, grad_upper, preferred_element_type=f32).astype(low)
    second_part = jnp.einsum("ztf,zdf->td", grad_upper, up_all, preferred_element_type=f32)
    terms = group_exchange(nt, second_part.reshape(wide, chunk, d).astype(low), True, 4, "sum_second")
    grad_second = jnp.sum(terms.astype(f32), axis=0)
    feed_part = feed_part.reshape(wide, chunk, d)
    feed_mine = lax.dynamic_index_in_dim(feed_part, y, 0, keepdims=False)
    cot_mine = lax.dynamic_slice_in_dim(cotangent, t * chunk, chunk, 0).astype(f32)
    grad_middle = cot_mine + norm_input_term(xhat2, rate2, gain2, grad_second)
    pull = [
        slopes, dist.T, query, keys, values, grad_middle.astype(low), context_by_shard, out_all, qkv_all, normed.T,
    ]
    g_up, g_down, output_all, grad_qkv, grad_out, grad_first, q_sum, v_sum = finish(
        nt, [], [grad_up, grad_down], feed_part.astype(low), middle + down_bias.astype(f32) + feed_mine, None, 1,
        "finish_mlp", pull,
    )
    xhat_mine = xhat1[behind:]
    grad_tokens = (grad_middle + norm_input_term(xhat_mine, rate1[behind:], gain1, grad_first)).astype(low)

    up_slots = jnp.where(jnp.arange(wide)[None, :, None] == y, grad_up_bias[:, None, :], 0.0)
    vectors = jnp.concatenate(
        [
            rows_sum(grad_first * xhat_mine), rows_sum(grad_first), rows_sum(grad_middle),
            rows_sum(grad_second * xhat2), rows_sum(grad_second), rows_sum(cot_mine),
            q_sum[:, 0].reshape(-1), v_sum[:, 0].reshape(-1), up_slots.reshape(-1),
        ]
    )
    g_qkv, g_out, grad_tokens_all, vectors = finish(
        nt, [grad_qkv, grad_out], [], grad_tokens, None, vectors.reshape(-1, 128), 5, "finish_attn"
    )
    vectors = vectors.reshape(-1)
    g_first_gain, g_first_shift, g_out_bias, g_second_gain, g_second_shift, g_down_bias = (
        vectors[i * d : (i + 1) * d] for i in range(6)
    )
    rest = vectors[6 * d :]
    g_q = lax.dynamic_index_in_dim(rest[:d].reshape(nt, heads_here, width), t, 0, keepdims=False)
    g_v = lax.dynamic_index_in_dim(rest[d : 2 * d].reshape(nt, heads_here, width), t, 0, keepdims=False)
    g_up_bias = lax.dynamic_index_in_dim(rest[2 * d :].reshape(nt, hidden_here), t, 0, keepdims=False)
    g_qkv = g_qkv.astype(f32).reshape(d, 3, heads_here, width).transpose(0, 2, 1, 3).reshape(d, heads_here, 3 * width)
    return (
        output_all.reshape(length, d), grad_tokens_all.reshape(length, d), g_first_gain, g_first_shift, g_qkv,
        jnp.concatenate([g_q, g_v], axis=1), g_out.astype(f32), g_out_bias, g_second_gain, g_second_shift,
        g_up.astype(f32), g_up_bias, g_down.astype(f32), g_down_bias,
    )


def solution(mesh):
    rows, cols, both = P("dp", None), P(None, "tensor"), P("tensor", None)
    return jax.shard_map(
        per_device,
        mesh=mesh,
        in_specs=(
            rows, rows, P(), P(), P(None, "tensor", None), both, both, P(), P(), P(), cols, P("tensor"), both, P(), rows,
        ),
        out_specs=(
            rows, rows, P(), P(), P(None, "tensor", None), both, both, P(), P(), P(), cols, P("tensor"), both, P(),
        ),
        check_vma=False,
    )
```

```python
import functools
import math

import jax
import jax.numpy as jnp
from jax import lax
from jax.experimental import pallas as pl
from jax.experimental.pallas import tpu as pltpu
from jax.sharding import PartitionSpec as P

MESH = pl.DeviceIdType.MESH
ANY = pl.BlockSpec(memory_space=pl.ANY)
VM = pl.BlockSpec(memory_space=pltpu.VMEM)


def grid_of(n_tensor):
    lines = min(4, n_tensor)
    return lines, n_tensor // lines


def where_am_i(n_tensor):
    lines, wide = grid_of(n_tensor)
    dp, t = lax.axis_index("dp"), lax.axis_index("tensor")
    return dp, t, t // wide, t % wide


def remote(src, dst, send, recv, peer):
    return pltpu.make_async_remote_copy(
        src_ref=src, dst_ref=dst, send_sem=send, recv_sem=recv, device_id=peer, device_id_type=MESH
    )


def when(condition, body):
    pl.when(condition)(body)


def greet(peers):
    barrier = pltpu.get_barrier_semaphore()
    for ok, peer in peers:
        @pl.when(ok)
        def _():
            pl.semaphore_signal(barrier, inc=1, device_id=peer, device_id_type=MESH)
    pl.semaphore_wait(barrier, sum(jnp.int32(ok) for ok, peer in peers))


def neighbours(n_tensor, use_y=True, use_x=True, use_core=True):
    lines, wide = grid_of(n_tensor)
    dp, t, z, y = where_am_i(n_tensor)
    out = [(z > 0, (dp, t - wide)), (z < lines - 1, (dp, t + wide))]
    if use_y:
        out += [(y > 0, (dp, t - 1)), (y < wide - 1, (dp, t + 1))]
    if use_x:
        out.append((dp >= 0, (dp ^ 2, t)))
    if use_core:
        out.append((dp >= 0, (dp ^ 1, t)))
    return out


def front_kernel(n_tensor, heads, n_attn, n_mlp, *refs):
    lines, wide = grid_of(n_tensor)
    dp, t, z, y = where_am_i(n_tensor)
    n = n_attn + n_mlp
    refs = list(refs)

    def take(count):
        got, refs[:] = refs[:count], refs[count:]
        return got

    own, inputs = take(n), take(front_inputs)
    full, outputs = take(n), take(front_outputs)
    z_send, z_recv, y_send, y_recv, x_send, x_recv, c_send, c_recv, l_sem = take(9)
    before, work, after, share, share_end = front_program(n_tensor, heads, inputs, full[:n_attn], outputs, refs)
    quad = dp % 4

    items, group_of = [], ([], [])
    for a in range(n):
        size = own[a].shape[0]
        split = a < n_attn and size % 128 == 0
        for item in [(a, 0, size // 8, True), (a, size // 2, size // 4, False)] if split else [(a, 0, size // 4, True)]:
            group_of[a >= n_attn].append(len(items))
            items.append(item)

    def slot(i, zz, yy):
        return zz * wide + yy if items[i][0] < n_attn else zz

    def piece(ref, i, q):
        a, first, size, by_x = items[i]
        return ref.at[pl.ds(pl.multiple_of(first + (q if by_x else q % 2) * size, size), size)]

    def block(i, zz, yy, q):
        return piece(full[items[i][0]].at[slot(i, zz, yy)], i, q)

    peers = neighbours(n_tensor)
    if wide > 2:
        peers += [(yy != y, (dp, z * wide + yy)) for yy in range(wide)]
    greet(peers)
    local = [pltpu.make_async_copy(own[a], full[a].at[z * wide + y if a < n_attn else z], l_sem.at[a]) for a in range(n)]
    for c in local:
        c.start()
    up, down = (dp, t + wide), (dp, t - wide)
    z_has = ((z < lines - 1), (z > 0))
    y_has = ((y < wide - 1), (y > 0))

    def z_copy(a, zz, side, mine=False):
        src = piece(own[items[a][0]], a, quad) if mine else block(a, zz, y, quad)
        return remote(src, block(a, zz, y, quad), z_send.at[side, a, zz], z_recv.at[side, a, zz], (up, down)[side])

    def y_copy(a, zz, yy, side, mine=False):
        src = piece(own[items[a][0]], a, quad) if mine else block(a, zz, yy, quad)
        peer = ((dp, t + 1), (dp, t - 1))[side]
        return remote(src, block(a, zz, yy, quad), y_send.at[side, a, zz, yy], y_recv.at[side, a, zz, yy], peer)

    def x_copy(a, zz, yy, q):
        return remote(block(a, zz, yy, q), block(a, zz, yy, q), x_send.at[a, zz, yy], x_recv.at[a, zz, yy], (dp ^ 2, t))

    def c_copy(a, zz, yy, q, hop):
        return remote(
            block(a, zz, yy, q), block(a, zz, yy, q), c_send.at[hop, a, zz, yy], c_recv.at[hop, a, zz, yy], (dp ^ 1, t)
        )

    def spread(a, zz, yy):
        if items[a][3]:
            x_copy(a, zz, yy, quad).start()
        c_copy(a, zz, yy, quad, 0).start()

    def arrays(group):
        return group_of[group]

    def y_start(zz, yy, side, mine=False):
        @pl.when(y_has[side])
        def _():
            for a in arrays(0):
                y_copy(a, zz, yy, side, mine).start()

    def z_begin(group):
        for side in range(2):
            @pl.when(z_has[side])
            def _():
                for a in arrays(group):
                    z_copy(a, z, side, True).start()

    def z_step(group, k):
        for side in range(2):
            zz = z - k if side == 0 else z + k

            @pl.when((zz >= 0) if side == 0 else (zz < lines))
            def _():
                for a in arrays(group):
                    z_copy(a, zz, side).wait_recv()

                @pl.when(z_has[side])
                def _():
                    for a in arrays(group):
                        z_copy(a, zz, side).start()

                if group == 0:
                    for s in range(2):
                        y_start(zz, y, s)
                for a in arrays(group):
                    spread(a, zz, y)

    def others(group, zs, body):
        for zz in zs:
            for yy in range(wide) if group == 0 else [y]:
                @pl.when((zz != z) | (yy != y))
                def _():
                    body(zz, yy)

    def pass_on(group, zs):
        def body(zz, yy):
            for a in arrays(group):
                if items[a][3]:
                    x_copy(a, zz, yy, quad ^ 2).wait_recv()
                    c_copy(a, zz, yy, quad ^ 2, 1).start()

        others(group, zs, body)

    def arrived(group):
        def body(zz, yy):
            for a in arrays(group):
                for hop in range(1 + items[a][3]):
                    c_copy(a, zz, yy, quad ^ (1 + 2 * hop), hop).wait_recv()

        others(group, range(lines), body)

    def settle(group):
        def body(zz, yy):
            for a in arrays(group):
                for hop in range(1 + items[a][3]):
                    c_copy(a, zz, yy, quad ^ (2 * hop), hop).wait_send()
                if items[a][3]:
                    x_copy(a, zz, yy, quad).wait_send()

        others(group, range(lines), body)
        for side in range(2):
            for k in range(lines):
                zz = z - k if side == 0 else z + k

                @pl.when(z_has[side] & (zz >= 0) & (zz < lines))
                def _():
                    for a in arrays(group):
                        z_copy(a, zz, side).wait_send()

    z_begin(0)
    for side in range(2):
        y_start(z, y, side, True)
    before()
    for k in range(1, lines):
        z_step(0, k)
    z_begin(1)
    for m in range(1, wide):
        for side in range(2):
            yy = y - m if side == 0 else y + m

            @pl.when((yy >= 0) if side == 0 else (yy < wide))
            def _():
                for zz in range(lines):
                    for a in arrays(0):
                        y_copy(a, zz, yy, side).wait_recv()
                    if m < wide - 1:
                        y_start(zz, yy, side)
                    for a in arrays(0):
                        spread(a, zz, yy)
    z_step(1, 1)
    for zz in range(lines):
        pass_on(0, [zz])
        if zz == lines // 2:
            z_step(1, 2)
    arrived(0)
    for c in local:
        c.wait()
    steps = [functools.partial(z_step, 1, k) for k in range(3, lines)]
    steps += [functools.partial(pass_on, 1, [zz]) for zz in range(lines)]

    @pl.loop(0, n_tensor)
    def _(p):
        work(p)
        for k in range(n_tensor):
            if steps:
                when(p == k, steps.pop(0))

    after()
    share()
    for step in steps:
        step()
    share_end()
    arrived(1)
    settle(0)
    settle(1)
    for side in range(2):
        @pl.when(y_has[side])
        def _():
            for zz in range(lines):
                for m in range(wide):
                    yy = y - m if side == 0 else y + m

                    @pl.when((yy >= 0) if side == 0 else (yy < wide))
                    def _():
                        for a in arrays(0):
                            y_copy(a, zz, yy, side).wait_send()


def front(n_tensor, attn, mlp, slopes, dist, near, rows):
    lines, wide = grid_of(n_tensor)
    n = len(attn) + len(mlp)
    arrays = list(attn) + list(mlp)
    span, d = near.shape
    chunk = dist.shape[0]
    lanes = attn[0].shape[1] // 3
    shape, low, f32 = jax.ShapeDtypeStruct, jnp.bfloat16, jnp.float32
    outs = [shape(((n_tensor if i < len(attn) else lines),) + a.shape, a.dtype) for i, a in enumerate(arrays)]
    outs += [
        shape((n_tensor, chunk, lanes), low), shape((n_tensor, span, lanes), low), shape((n_tensor, span, lanes), low),
        shape((n_tensor, chunk, lanes), low), shape((chunk, d), f32), shape((wide, chunk, d), low), shape((d, span), low),
    ]
    dma = pltpu.SemaphoreType.DMA
    return pl.pallas_call(
        functools.partial(front_kernel, n_tensor, slopes.shape[0] // n_tensor, len(attn), len(mlp)),
        out_shape=outs,
        in_specs=[VM] * n + [pl.BlockSpec(memory_space=pltpu.SMEM)] + [VM] * (front_inputs - 1),
        out_specs=[VM] * len(attn) + [ANY] * len(mlp) + [VM] * front_outputs,
        scratch_shapes=[dma((2, 2 * n, lines))] * 2
        + [dma((2, 2 * n, lines, wide))] * 2
        + [dma((2 * n, lines, wide))] * 2
        + [dma((2, 2 * n, lines, wide))] * 2
        + [dma((n,))]
        + [pltpu.VMEM((span, d), low), dma((wide,)), dma((wide,))],
        compiler_params=pltpu.CompilerParams(collective_id=0, has_side_effects=True, vmem_limit_bytes=60 * 2**20),
        name="front",
    )(*arrays, slopes, dist, near, rows)


def add_rows(dst, terms):
    rows = dst.shape[0]
    step = 32 if rows % 32 == 0 else rows

    @pl.loop(0, rows // step)
    def _(i):
        part = pl.ds(pl.multiple_of(i * step, step), step)
        total = terms[0][part].astype(jnp.float32)
        for term in terms[1:]:
            total = total + term[part].astype(jnp.float32)
        dst[part] = total.astype(dst.dtype)


def pair_sums(n_tensor, terms, sums, from_c, to_x, from_x, c_send, c_recv, x_send, x_recv):
    dp, t, z, y = where_am_i(n_tensor)
    quad = dp % 4
    side_x, core = quad // 2, quad % 2
    arrays = range(len(terms))

    def quarter(a, s, q):
        rows = terms[a].shape[1] // 4
        return terms[a].at[s, pl.ds(pl.multiple_of(q * rows, rows), rows)]

    def c_copy(a, s, h):
        return remote(
            quarter(a, s, h * 2 + 1 - core), from_c[a].at[s, h], c_send.at[a, s, h], c_recv.at[a, s, h], (dp ^ 1, t)
        )

    def x_copy(a, s):
        return remote(to_x[a].at[s], from_x[a].at[s], x_send.at[a, s], x_recv.at[a, s], (dp ^ 2, t))

    def start(s):
        for a in arrays:
            for h in range(2):
                c_copy(a, s, h).start()

    def core_stage(s):
        for a in arrays:
            for h in range(2):
                c_copy(a, s, h).wait_recv()
            add_rows(to_x[a].at[s], [quarter(a, s, (1 - side_x) * 2 + core), from_c[a].at[s, 1 - side_x]])
            x_copy(a, s).start()
            add_rows(sums[a].at[s], [quarter(a, s, quad), from_c[a].at[s, side_x]])

    def x_stage(s):
        for a in arrays:
            x_copy(a, s).wait_recv()
            add_rows(sums[a].at[s], [sums[a].at[s], from_x[a].at[s]])

    def settle(s):
        for a in arrays:
            for h in range(2):
                c_copy(a, s, h).wait_send()
            x_copy(a, s).wait_send()

    return start, core_stage, x_stage, settle


def pair_scratch(shapes, slots):
    low, dma = jnp.bfloat16, pltpu.SemaphoreType.DMA
    n = len(shapes)
    quarters = [(r // 4, c) for r, c in shapes]
    return (
        [pltpu.VMEM((slots, 2) + q, low) for q in quarters]
        + [pltpu.VMEM((slots,) + q, low) for q in quarters] * 2
        + [dma((n, slots, 2))] * 2 + [dma((n, slots))] * 2
    )


def doubling_peers(n_tensor):
    dp, t, z, y = where_am_i(n_tensor)
    bits = lambda size: [1 << i for i in range((size - 1).bit_length())]
    return [(dp ^ b, t) for b in bits(lax.axis_size("dp"))] + [(dp, t ^ b) for b in bits(n_tensor)]


def doubling_program(n_tensor, own, out, total, got, send, recv):
    peers = doubling_peers(n_tensor)

    def step(i):
        return remote(total.at[i], got.at[i], send.at[i], recv.at[i], peers[i])

    def begin():
        total[0] = own[...]
        step(0).start()

    def advance(i):
        step(i).wait_recv()
        if i + 1 < len(peers):
            total[i + 1] = total[i] + got[i]
            step(i + 1).start()
        else:
            out[...] = total[i] + got[i]

    def settle():
        for i in range(len(peers)):
            step(i).wait_send()

    return [begin] + [functools.partial(advance, i) for i in range(len(peers))] + [settle]


def finish_kernel(n_tensor, n_attn, n_mlp, with_vectors, pull, *refs):
    lines, wide = grid_of(n_tensor)
    dp, t, z, y = where_am_i(n_tensor)
    n = n_attn + n_mlp
    refs = list(refs)

    def take(count):
        got, refs[:] = refs[:count], refs[count:]
        return got

    terms, rows_own = take(n), take(1)
    vec_own = take(1)[0] if with_vectors else None
    pull_in = take(pull_inputs) if pull else []
    final, rows_full = take(n), take(1)
    vec_out = take(1)[0] if with_vectors else None
    pull_out = take(pull_outputs) if pull else []
    acc, from_y, from_z, whole = (take(n) for i in range(4))
    y_send, y_recv, z_send, z_recv, q_send, q_recv = take(6)
    rows_steps = rows_program(n_tensor, rows_own, rows_full, *take(5))
    vec_steps = doubling_program(n_tensor, vec_own, vec_out, *take(4)) if with_vectors else []
    if pull:
        work, pull_peers, pull_first, pull_last = pull_program(n_tensor, pull, pull_in, pull_out, refs)
    quad = dp % 4
    core_peer, x_peer = (dp ^ 1, t), (dp ^ 2, t)
    lines_order = [i // 2 if i % 2 else lines - 1 - i // 2 for i in range(lines)]
    attn, order = list(range(n_attn)), list(range(n))

    def index(a, zz, yy):
        return zz * wide + yy if a < n_attn else zz

    def quarter(ref, q):
        rows = ref.shape[0] // 4
        return ref.at[pl.ds(pl.multiple_of(q * rows, rows), rows)]

    def y_copy(a, zz, yy, side):
        peer = ((dp, t + 1), (dp, t - 1))[side]
        lane = zz * wide + yy
        return remote(acc[a].at[lane], from_y[a].at[side, lane], y_send.at[side, a, lane], y_recv.at[side, a, lane], peer)

    def z_copy(a, zz, side):
        peer = ((dp, t + wide), (dp, t - wide))[side]
        return remote(
            acc[a].at[index(a, zz, y)], from_z[a].at[side, zz], z_send.at[side, a, zz], z_recv.at[side, a, zz], peer
        )

    def y_begin(zz):
        for m in range(wide):
            yy = (y + 1 + m) % wide
            for a in attn:
                lane = zz * wide + yy
                add_rows(acc[a].at[lane], [terms[a].at[lane]])
                when((y == 0) & (yy > y), lambda: y_copy(a, zz, yy, 0).start())
                when((y == wide - 1) & (yy < y), lambda: y_copy(a, zz, yy, 1).start())

    def y_stage(zz):
        for a in attn:
            for k in range(wide):
                for side, yy in ((0, wide - 1 - k), (1, k)):
                    @pl.when(((yy >= y) & (y > 0)) if side == 0 else ((yy <= y) & (y < wide - 1)))
                    def _():
                        lane = zz * wide + yy
                        y_copy(a, zz, yy, side).wait_recv()
                        add_rows(acc[a].at[lane], [acc[a].at[lane], from_y[a].at[side, lane]])
                        when(yy != y, lambda: y_copy(a, zz, yy, side).start())

    def z_round(r):
        for side in range(2):
            zz = lines - 1 - r + z if side == 0 else z - (lines - 1 - r)

            @pl.when((zz < lines) & (zz >= 0))
            def _():
                @pl.when((z > 0) if side == 0 else (z < lines - 1))
                def _():
                    for a in order:
                        s = index(a, zz, y)
                        z_copy(a, zz, side).wait_recv()
                        add_rows(acc[a].at[s], [acc[a].at[s], from_z[a].at[side, zz]])

                if r < lines - 1:
                    for a in order:
                        z_copy(a, zz, side).start()

    def q_copy(a, q, hop, peer):
        return remote(quarter(whole[a], q), quarter(whole[a], q), q_send.at[hop, a], q_recv.at[hop, a], peer)

    def home(a):
        add_rows(quarter(whole[a], quad), [acc[a].at[index(a, z, y)]])
        q_copy(a, quad, 0, x_peer).start()
        q_copy(a, quad, 1, core_peer).start()

    def widen(a, q):
        add_rows(quarter(final[a], q), [quarter(whole[a], q)])

    def aside():
        if len(rows_steps) > 1:
            rows_steps.pop(0)()
        if len(vec_steps) > 1:
            vec_steps.pop(0)()

    def late(r):
        aside()
        z_round(r)

    peers = neighbours(n_tensor)
    if pull:
        peers += pull_peers
    if with_vectors:
        peers += [(dp >= 0, peer) for peer in doubling_peers(n_tensor)]
    greet(peers)
    for zz in lines_order:
        y_begin(zz)
        for a in order[n_attn:]:
            add_rows(acc[a].at[zz], [terms[a].at[zz]])
    if not attn:
        z_round(0)
    rows_steps.pop(0)()
    if with_vectors:
        vec_steps.pop(0)()
    if attn:
        for zz in lines_order:
            y_stage(zz)
            if with_vectors:
                vec_steps.pop(0)()
        z_round(0)
    steps = [functools.partial(late, r) for r in range(1, lines)]
    if pull:
        @pl.loop(0, n_tensor)
        def _(p):
            work(p)
            for k in (n_tensor // 2, n_tensor - 1):
                when(p == k, steps.pop(0))

        pull_first()
    for step in steps:
        step()
    for a in order:
        home(a)
    aside()
    for a in order:
        widen(a, quad)
        q_copy(a, quad ^ 2, 0, x_peer).wait_recv()
        q_copy(a, quad ^ 2, 2, core_peer).start()
        widen(a, quad ^ 2)
    if pull:
        pull_last()
    while rows_steps:
        rows_steps.pop(0)()
    while vec_steps:
        vec_steps.pop(0)()
    for a in order:
        q_copy(a, quad ^ 1, 1, core_peer).wait_recv()
        widen(a, quad ^ 1)
        q_copy(a, quad ^ 3, 2, core_peer).wait_recv()
        widen(a, quad ^ 3)
        q_copy(a, quad, 0, x_peer).wait_send()
        q_copy(a, quad, 1, core_peer).wait_send()
        q_copy(a, quad ^ 2, 2, core_peer).wait_send()
        if a < n_attn:
            for zz in range(lines):
                for yy in range(wide):
                    when(yy > y, lambda: y_copy(a, zz, yy, 0).wait_send())
                    when(yy < y, lambda: y_copy(a, zz, yy, 1).wait_send())
        for zz in range(lines):
            when(zz > z, lambda: z_copy(a, zz, 0).wait_send())
            when(zz < z, lambda: z_copy(a, zz, 1).wait_send())


def finish(n_tensor, attn, mlp, rows, vectors, cid, name, pull=None):
    lines, wide = grid_of(n_tensor)
    arrays = list(attn) + list(mlp)
    n = len(arrays)
    vm, dma = pltpu.VMEM, pltpu.SemaphoreType.DMA
    low, f32 = jnp.bfloat16, jnp.float32
    quarters = [a.shape[1:] for a in arrays]
    each = lambda lead: [vm(lead(a, i) + q, low) for i, (a, q) in enumerate(zip(arrays, quarters))]
    steps = (lax.axis_size("dp") - 1).bit_length() + (n_tensor - 1).bit_length()
    scratch = (
        each(lambda a, i: (a.shape[0],))
        + each(lambda a, i: (2, n_tensor) if i < len(attn) else (1, 1))
        + each(lambda a, i: (2, lines))
        + [vm((4 * q[0], q[1]), low) for q in quarters]
    )
    sems = (
        [dma((2, max(1, len(attn)), n_tensor))] * 2 + [dma((2, n, lines))] * 2 + [dma((3, n))] * 2
        + [dma((2, 1, lines))] * 2 + [dma((2, 1, lines, wide))] * 2 + [dma((1,))]
    )
    inputs, in_specs = arrays + [rows], [VM] * n + [VM]
    out_shape = [jax.ShapeDtypeStruct((4 * q[0], q[1]), f32) for q in quarters]
    out_shape.append(jax.ShapeDtypeStruct((n_tensor,) + rows.shape, low))
    out_specs = [VM] * n + [ANY]
    if vectors is not None:
        inputs, in_specs = inputs + [vectors], in_specs + [VM]
        out_shape.append(jax.ShapeDtypeStruct(vectors.shape, vectors.dtype))
        out_specs.append(VM)
        sems += [vm((steps,) + vectors.shape, jnp.float32)] * 2 + [dma((steps,))] * 2
    heads = 0
    if pull is not None:
        heads = pull[0].shape[0] // n_tensor
        inputs, in_specs = inputs + list(pull), in_specs + [pl.BlockSpec(memory_space=pltpu.SMEM)] + [VM] * (pull_inputs - 1)
        shapes, more = pull_shapes(n_tensor, pull)
        out_shape += shapes
        out_specs += [VM] * pull_outputs
        sems += more
    out = pl.pallas_call(
        functools.partial(
            finish_kernel, n_tensor, len(attn), len(mlp), vectors is not None, heads
        ),
        out_shape=out_shape,
        in_specs=in_specs,
        out_specs=out_specs,
        scratch_shapes=scratch + sems,
        compiler_params=pltpu.CompilerParams(collective_id=cid, has_side_effects=True, vmem_limit_bytes=63 * 2**20),
        name=name,
    )(*inputs)
    sums = out[:n]
    if lax.axis_size("dp") > 4:
        sums = [lax.psum(s, "dp") * 0.25 for s in sums]
    return list(sums) + list(out[n:])


def mlp_kernel(n_tensor, *refs):
    lines, wide = grid_of(n_tensor)
    dp, t, z, y = where_am_i(n_tensor)
    second, cot, up, down, bias, base = refs[:6]
    sum_up, sum_down, up_sum, grad_second, output = refs[6:11]
    terms_up, terms_down = refs[11:13]
    pair, (feed, grad, second_t, share_own, share_got, s_send, s_recv) = refs[13:23], refs[23:]
    sums, terms = (sum_up, sum_down), (terms_up, terms_down)
    pair_start, core_stage, x_stage, pair_settle = pair_sums(
        n_tensor, terms, sums, pair[0:2], pair[2:4], pair[4:6], *pair[6:]
    )
    low, f32 = jnp.bfloat16, jnp.float32
    chunk = output.shape[0]
    tile = min(128, chunk)

    def share(kind, yy, slot):
        return remote(
            share_own.at[kind, yy], share_got.at[kind, slot], s_send.at[kind, yy], s_recv.at[kind, slot],
            (dp, z * wide + yy),
        )

    peers = [(dp >= 0, (dp ^ 1, t)), (dp >= 0, (dp ^ 2, t))]
    peers += [(yy != y, (dp, z * wide + yy)) for yy in range(wide)]
    greet(peers)
    feed[...] = jnp.zeros(feed.shape, f32)
    grad[...] = jnp.zeros(grad.shape, f32)

    @pl.loop(0, second.shape[0] // tile)
    def _(i):
        here = pl.ds(pl.multiple_of(i * tile, tile), tile)
        second_t[:, here] = second[here].T

    @pl.loop(0, lines)
    def _(s):
        upper = dot(second[...], up[s], NN) + bias[s, 0:1]
        hidden, slope = gelu_and_slope(upper)
        hidden = hidden.astype(low)
        grad_upper = (dot(cot[...], down[s], NT) * slope).astype(low)
        up_sum[s] = jnp.broadcast_to(jnp.sum(grad_upper.astype(f32), axis=0, keepdims=True), up_sum.shape[1:])
        terms_down[s] = dot(hidden, cot[...], TN).astype(low)
        terms_up[s] = dot(second_t[...], grad_upper, NN).astype(low)
        pair_start(s)
        feed[...] += dot(hidden, down[s], NN)
        grad[...] += dot(grad_upper, up[s], NT)
        when(s >= 1, lambda: core_stage(jnp.maximum(s - 1, 0)))

    for kind, whole in ((0, grad), (1, feed)):
        for yy in range(wide):
            @pl.when(yy != y)
            def _():
                add_rows(share_own.at[kind, yy], [whole.at[pl.ds(yy * chunk, chunk)]])
                share(kind, yy, y).start()
    core_stage(lines - 1)
    for s in range(lines - 1):
        x_stage(s)
    for kind, whole, out in ((0, grad, grad_second), (1, feed, output)):
        share_got[kind, y] = jnp.zeros((chunk, second.shape[1]), low)
        for yy in range(wide):
            when(yy != y, lambda: share(kind, yy, yy).wait_recv())
        mine = whole.at[pl.ds(pl.multiple_of(y * chunk, chunk), chunk)]
        add_rows(out, [mine] + [share_got.at[kind, yy] for yy in range(wide)] + ([base] if kind else []))
    x_stage(lines - 1)
    for yy in range(wide):
        for kind in range(2):
            when(yy != y, lambda: share(kind, yy, y).wait_send())
    for s in range(lines):
        pair_settle(s)


def mlp(n_tensor, second, cot, up, down, bias, base):
    lines, wide = grid_of(n_tensor)
    shape, vm, dma = jax.ShapeDtypeStruct, pltpu.VMEM, pltpu.SemaphoreType.DMA
    low, f32 = jnp.bfloat16, jnp.float32
    d, hidden = up.shape[1:]
    chunk = base.shape[0]
    quarters = [(d // 4, hidden), (hidden // 4, d)]
    return pl.pallas_call(
        functools.partial(mlp_kernel, n_tensor),
        out_shape=[shape((lines,) + q, low) for q in quarters]
        + [shape((lines, 8, hidden), f32), shape((chunk, d), f32), shape((chunk, d), low)],
        in_specs=[VM] * 6,
        out_specs=[VM] * 5,
        scratch_shapes=[vm(up.shape, low), vm(down.shape, low)] + pair_scratch([up.shape[1:], down.shape[1:]], lines)
        + [vm(second.shape, f32)] * 2 + [vm((d, second.shape[0]), low)] + [vm((2, wide, chunk, d), low)] * 2
        + [dma((2, wide))] * 2,
        compiler_params=pltpu.CompilerParams(collective_id=3, has_side_effects=True, vmem_limit_bytes=60 * 2**20),
        name="mlp",
    )(second, cot, up, down, bias, base)


def rows_program(n_tensor, own, full, z_send, z_recv, y_send, y_recv, l_sem):
    lines, wide = grid_of(n_tensor)
    dp, t, z, y = where_am_i(n_tensor)
    n = len(own)

    def z_copy(a, zz, side, mine=False):
        dst = full[a].at[zz * wide + y]
        peer = ((dp, t + wide), (dp, t - wide))[side]
        return remote(own[a] if mine else dst, dst, z_send.at[side, a, zz], z_recv.at[side, a, zz], peer)

    def y_copy(a, zz, yy, side, mine=False):
        dst = full[a].at[zz * wide + yy]
        peer = ((dp, t + 1), (dp, t - 1))[side]
        return remote(own[a] if mine else dst, dst, y_send.at[side, a, zz, yy], y_recv.at[side, a, zz, yy], peer)

    z_has = ((z < lines - 1), (z > 0))
    y_has = ((y < wide - 1), (y > 0))
    local = [pltpu.make_async_copy(own[a], full[a].at[t], l_sem.at[a]) for a in range(n)]

    def begin():
        for side in range(2):
            for a in range(n):
                when(z_has[side], lambda: z_copy(a, z, side, True).start())
                when(y_has[side], lambda: y_copy(a, z, y, side, True).start())
        for c in local:
            c.start()

    def along_z(k):
        for side in range(2):
            zz = z - k if side == 0 else z + k

            @pl.when((zz >= 0) & (zz < lines))
            def _():
                for a in range(n):
                    z_copy(a, zz, side).wait_recv()
                    when(z_has[side], lambda: z_copy(a, zz, side).start())
                    for s in range(2):
                        when(y_has[s], lambda: y_copy(a, zz, y, s).start())

    def along_y(m):
        for side in range(2):
            yy = y - m if side == 0 else y + m

            @pl.when((yy >= 0) & (yy < wide))
            def _():
                for zz in range(lines):
                    for a in range(n):
                        y_copy(a, zz, yy, side).wait_recv()
                        if m < wide - 1:
                            when(y_has[side], lambda: y_copy(a, zz, yy, side).start())

    def settle():
        for side in range(2):
            for k in range(lines):
                zz = z - k if side == 0 else z + k

                @pl.when(z_has[side] & (zz >= 0) & (zz < lines))
                def _():
                    for a in range(n):
                        z_copy(a, zz, side).wait_send()
            for m in range(wide):
                yy = y - m if side == 0 else y + m

                @pl.when(y_has[side] & (yy >= 0) & (yy < wide))
                def _():
                    for zz in range(lines):
                        for a in range(n):
                            y_copy(a, zz, yy, side).wait_send()
        for c in local:
            c.wait()

    return (
        [begin]
        + [functools.partial(along_z, k) for k in range(1, lines)]
        + [functools.partial(along_y, m) for m in range(1, wide)]
        + [settle]
    )


def dot(a, b, contract, **kwargs):
    return lax.dot_general(a, b, (contract, ((), ())), preferred_element_type=jnp.float32, **kwargs)


NN, NT, TN = ((1,), (0,)), ((1,), (1,)), ((0,), (0,))


def head_of_lane(shape, heads):
    return lax.broadcasted_iota(jnp.int32, shape, 1) // (shape[1] // heads)


def attend(heads, slope_of, dist, query, keys, values):
    scale = 1.0 / math.sqrt(query.shape[1] // heads)
    head = head_of_lane(query.shape, heads)
    out = jnp.zeros(query.shape, jnp.float32)
    for h in range(heads):
        masked = jnp.where(head == h, query * jnp.bfloat16(scale), jnp.bfloat16(0))
        scores = dot(masked, keys, NT) - slope_of(h) * dist[...]
        peak = jnp.max(scores, axis=1, keepdims=True)
        expo = jnp.exp(scores - peak)
        total = jnp.sum(expo, axis=1, keepdims=True)
        part = dot(expo.astype(jnp.bfloat16), values, NN) / total
        out = jnp.where(head == h, part, out)
    return out.astype(jnp.bfloat16)


front_inputs, front_outputs = 4, 7


def front_program(n_tensor, heads, ins, weights, outs, scratch):
    lines, wide = grid_of(n_tensor)
    dp, t, z, y = where_am_i(n_tensor)
    slopes, dist, near, rows = ins
    qkv_all, out_all, small_all = weights
    q, k, v, context, middle, second, normed_t = outs
    normed, s_send, s_recv = scratch
    chunk, lanes = q.shape[1:]
    span, d = near.shape
    behind = span - chunk
    low, f32 = jnp.bfloat16, jnp.float32
    tile = min(128, chunk)

    def before():
        @pl.loop(0, span // tile)
        def _(i):
            here = pl.ds(pl.multiple_of(i * tile, tile), tile)
            xhat, rate = normalized(near[here].astype(f32))
            value = (xhat * rows[0:1] + rows[1:2]).astype(low)
            normed[here] = value
            normed_t[:, here] = value.T

    def work(p):
        bias = small_all[p, 0:16, :].astype(f32)
        query = (dot(normed[behind:], qkv_all[p, :, :lanes], NN) + bias[0:1, :lanes]).astype(low)
        both = dot(normed[...], qkv_all[p, :, lanes:], NN)
        keys = both[:, :lanes].astype(low)
        values = (both[:, lanes:] + bias[1:2, :lanes]).astype(low)
        q[p], k[p], v[p] = query, keys, values
        context[p] = attend(heads, lambda h: slopes[p * heads + h], dist, query, keys, values)

    def after():
        @pl.loop(0, chunk // tile)
        def _(i):
            start = pl.multiple_of(i * tile, tile)
            here = pl.ds(start, tile)
            total = near[pl.ds(behind + start, tile)].astype(f32) + rows[4:5]
            for p in range(n_tensor):
                total = total + dot(context[p, here], out_all[p], NN)
            middle[here] = total
            xhat, rate = normalized(total)
            second[y, here] = (xhat * rows[2:3] + rows[3:4]).astype(low)

    def step(yy, slot):
        return remote(second.at[slot], second.at[slot], s_send.at[yy], s_recv.at[slot], (dp, z * wide + yy))

    def share():
        for yy in range(wide):
            when(yy != y, lambda: step(yy, y).start())

    def share_end():
        for yy in range(wide):
            @pl.when(yy != y)
            def _():
                step(yy, yy).wait_recv()
                step(yy, y).wait_send()

    return before, work, after, share, share_end


def pull_scores(heads, slope_of, dist, query, keys, values, grad):
    lanes = query.shape[1]
    scale = 1.0 / math.sqrt(lanes // heads)
    head = head_of_lane(query.shape, heads)
    head_rows = lax.broadcasted_iota(jnp.int32, (lanes, query.shape[0]), 0) // (lanes // heads)
    low = jnp.bfloat16
    grad_q = jnp.zeros((lanes, query.shape[0]), jnp.float32)
    grad_k = jnp.zeros(keys.shape, jnp.float32)
    grad_v = jnp.zeros(keys.shape, jnp.float32)
    for h in range(heads):
        masked = jnp.where(head == h, query * low(scale), low(0))
        masked_grad = jnp.where(head == h, grad, low(0))
        scores = dot(keys, masked, NT) - slope_of(h) * dist[...]
        peak = jnp.max(scores, axis=0, keepdims=True)
        expo = jnp.exp(scores - peak)
        probs = expo * (1.0 / jnp.sum(expo, axis=0, keepdims=True))
        grad_probs = dot(values, masked_grad, NT)
        inner = jnp.sum(probs * grad_probs, axis=0, keepdims=True)
        grad_scores = (probs * (grad_probs - inner)).astype(low)
        grad_v = grad_v + dot(probs.astype(low), masked_grad, NN)
        grad_k = grad_k + dot(grad_scores, masked, NN)
        grad_q = jnp.where(head_rows == h, dot(keys, grad_scores, TN), grad_q)
    return (jnp.transpose(grad_q) * scale).astype(low), grad_k.astype(low), grad_v.astype(low)


pull_inputs, pull_outputs = 10, 5


def pull_shapes(n_tensor, pull):
    slopes, dist, q, k, v, grad, context, out_all, qkv_all, normed_t = pull
    span, chunk, lanes, d = k.shape[1], q.shape[1], q.shape[2], normed_t.shape[0]
    halo = (span - chunk) // chunk
    low, f32 = jnp.bfloat16, jnp.float32
    shape = jax.ShapeDtypeStruct
    vm, dma = pltpu.VMEM, pltpu.SemaphoreType.DMA
    outs = [
        shape((n_tensor, d // 4, 3 * lanes), low), shape((n_tensor, lanes // 4, d), low), shape((chunk, d), f32),
        shape((n_tensor, 8, lanes), f32), shape((n_tensor, 8, lanes), f32),
    ]
    scratch = [vm(qkv_all.shape, low), vm(out_all.shape, low)]
    scratch += pair_scratch([qkv_all.shape[1:], out_all.shape[1:]], n_tensor) + [
        vm(q.shape, low), vm((n_tensor, span, 2 * lanes), low), vm((halo, chunk, d), low), vm((halo, chunk, d), low),
        dma((halo,)), dma((halo,)),
    ]
    return outs, scratch


def pull_program(n_tensor, heads, ins, outs, scratch):
    dp, t, z, y = where_am_i(n_tensor)
    slopes, dist, q, k, v, grad, context, out_all, qkv_all, normed_t = ins
    sum_qkv, sum_out, first, q_sum, v_sum = outs
    (grad_qkv, grad_out), pair = scratch[:2], scratch[2:12]
    grad_q, grad_kv, halo_own, halo_got, h_send, h_recv = scratch[12:]
    pair_start, core_stage, x_stage, pair_settle = pair_sums(
        n_tensor, (grad_qkv, grad_out), (sum_qkv, sum_out), pair[0:2], pair[2:4], pair[4:6], *pair[6:]
    )
    halo, chunk, d = halo_own.shape
    span, lanes = k.shape[1], q.shape[2]
    behind = span - chunk
    low, f32 = jnp.bfloat16, jnp.float32

    def work(p):
        grad_context = dot(grad[...], out_all[p], NT).astype(low)
        grad_out[p] = dot(context[p], grad[...], TN).astype(low)
        gq, gk, gv = pull_scores(heads, lambda h: slopes[p * heads + h], dist, q[p], k[p], v[p], grad_context)
        grad_q[p] = gq
        grad_kv[p, :, :lanes] = gk
        grad_kv[p, :, lanes:] = gv
        q_sum[p] = jnp.broadcast_to(jnp.sum(gq.astype(f32), axis=0, keepdims=True), (8, lanes))
        v_sum[p] = jnp.broadcast_to(jnp.sum(gv.astype(f32), axis=0, keepdims=True), (8, lanes))
        grad_qkv[p, :, :lanes] = dot(normed_t[:, behind:], gq, NN).astype(low)
        grad_qkv[p, :, lanes:] = dot(normed_t[...], grad_kv[p], NN).astype(low)
        pair_start(p)
        when(p >= 1, lambda: core_stage(jnp.maximum(p - 1, 0)))

    def step(m):
        return remote(halo_own.at[halo - 1 - m], halo_got.at[m], h_send.at[m], h_recv.at[m], (dp, t - 1 - m))

    ahead = [(t + 1 + m < n_tensor, (dp, t + 1 + m)) for m in range(halo)]
    back = [(t - 1 - m >= 0, (dp, t - 1 - m)) for m in range(halo)]
    tile = min(128, chunk)

    def rows_first():
        core_stage(n_tensor - 1)
        for j in range(halo):
            @pl.loop(0, chunk // tile)
            def _(i):
                here = pl.multiple_of(i * tile, tile)
                total = jnp.zeros((tile, d), f32)
                for p in range(n_tensor):
                    total = total + dot(grad_kv[p, pl.ds(j * chunk + here, tile)], qkv_all[p, :, lanes:], NT)
                halo_own[j, pl.ds(here, tile)] = total.astype(low)

        for m in range(halo):
            when(back[m][0], lambda: step(m).start())

        @pl.loop(0, chunk // tile)
        def _(i):
            here = pl.multiple_of(i * tile, tile)
            total = jnp.zeros((tile, d), f32)
            for p in range(n_tensor):
                total = total + dot(grad_kv[p, pl.ds(behind + here, tile)], qkv_all[p, :, lanes:], NT)
                total = total + dot(grad_q[p, pl.ds(here, tile)], qkv_all[p, :, :lanes], NT)
            first[pl.ds(here, tile)] = total

    def rows_last():
        for m in range(halo):
            @pl.when(ahead[m][0])
            def _():
                step(m).wait_recv()
                add_rows(first, [first, halo_got.at[m]])

            when(back[m][0], lambda: step(m).wait_send())

        @pl.loop(0, n_tensor)
        def _(p):
            x_stage(p)
            pair_settle(p)

    return work, ahead + back, rows_first, rows_last


norm_eps = 1e-05


def normalized(values):
    offset = values - jnp.mean(values, axis=-1, keepdims=True)
    rate = lax.rsqrt(jnp.mean(offset * offset, axis=-1, keepdims=True) + norm_eps)
    return offset * rate, rate


def norm_input_term(xhat, rate, gain, grad):
    e = grad * gain
    return rate * (e - jnp.mean(e, axis=-1, keepdims=True) - xhat * jnp.mean(e * xhat, axis=-1, keepdims=True))


def gelu_and_slope(u):
    c, a = 0.7978845608028654, 0.044715
    th = jnp.tanh(c * (u + a * u * u * u))
    slope = 0.5 * (1.0 + th) + 0.5 * u * (1.0 - th * th) * (c * (1.0 + 3.0 * a * u * u))
    return 0.5 * u * (1.0 + th), slope


far_off = 1e33
longest = 512


def rows_sum(v):
    return jnp.sum(v, axis=0)


def per_device(
    tokens, segment_ids, first_gain, first_shift, qkv_weight, qv_bias, out_weight, out_bias, second_gain, second_shift,
    up_weight, up_bias, down_weight, down_bias, cotangent,
):
    low, f32 = jnp.bfloat16, jnp.float32
    nt = lax.axis_size("tensor")
    lines, wide = grid_of(nt)
    t = lax.axis_index("tensor")
    z, y = t // wide, t % wide
    length, d = tokens.shape
    chunk = length // nt
    halo = -(-(longest - 1) // chunk)
    behind = halo * chunk
    span = behind + chunk
    heads_here, width = qkv_weight.shape[1], qkv_weight.shape[2] // 3
    lanes = heads_here * width
    hidden_here = up_weight.shape[1]

    qkv_own = qkv_weight.reshape(d, heads_here, 3, width).transpose(0, 2, 1, 3).reshape(d, 3 * lanes)
    bias_own = jnp.pad(qv_bias.reshape(heads_here, 2, width).transpose(1, 0, 2).reshape(2, lanes), ((0, 0), (0, 128 - lanes)))
    small = jnp.concatenate([bias_own.reshape(256), up_bias])
    small = jnp.pad(small, (0, 64 * 128 - small.shape[0])).reshape(64, 128)

    padded = jnp.concatenate([jnp.zeros((behind, d), low), tokens])
    near = lax.dynamic_slice_in_dim(padded, t * chunk, span, 0)
    seg_row = jnp.concatenate([jnp.full((behind,), -1, jnp.int32), segment_ids[0]])
    seg_near = lax.dynamic_slice_in_dim(seg_row, t * chunk, span, 0)
    seg_mine = seg_near[behind:]
    distance = (behind + jnp.arange(chunk)[:, None]) - jnp.arange(span)[None, :]
    allowed = (seg_mine[:, None] == seg_near[None, :]) & (distance >= 0)
    dist = jnp.where(allowed, distance.astype(f32), far_off)
    total_heads = heads_here * nt
    slopes = jnp.exp2(-8.0 * (jnp.arange(total_heads, dtype=jnp.int32) + 1).astype(f32) / total_heads)

    gain1, shift1 = first_gain.astype(f32), first_shift.astype(f32)
    gain2, shift2 = second_gain.astype(f32), second_shift.astype(f32)
    rows = jnp.stack([gain1, shift1, gain2, shift2, out_bias.astype(f32)] + [shift1] * 3)
    (qkv_all, out_all, small_all, up_all, down_all, query, keys, values, context, middle, second_pair, normed_t) = front(
        nt, [qkv_own, out_weight, small], [up_weight, down_weight], slopes, dist, near, rows
    )
    small_all = small_all.reshape(nt, 64 * 128).astype(f32)
    up_bias_all = lax.dynamic_index_in_dim(
        small_all[:, 256 : 256 + hidden_here].reshape(lines, wide, hidden_here), y, 1, keepdims=False
    )
    xhat1, rate1 = normalized(near[behind:].astype(f32))
    xhat2, rate2 = normalized(middle)
    second_pair = second_pair.reshape(wide * chunk, d)

    cot_pair = lax.dynamic_slice_in_dim(cotangent, z * (wide * chunk), wide * chunk, 0)
    sum_up, sum_down, grad_up_bias, grad_second, output_mine = mlp(
        nt, second_pair, cot_pair, up_all, down_all, jnp.broadcast_to(up_bias_all[:, None], (lines, 8, hidden_here)),
        middle + down_bias.astype(f32),
    )
    grad_up_bias = grad_up_bias[:, 0]
    cot_mine = lax.dynamic_slice_in_dim(cotangent, t * chunk, chunk, 0).astype(f32)
    grad_middle = cot_mine + norm_input_term(xhat2, rate2, gain2, grad_second)
    pull = [
        slopes, dist.T, query, keys, values, grad_middle.astype(low), context, out_all, qkv_all, normed_t,
    ]
    g_up, g_down, output_all, sum_qkv, sum_out, grad_first, q_sum, v_sum = finish(
        nt, [], [sum_up, sum_down], output_mine, None, 1, "finish_mlp", pull
    )
    grad_tokens = (grad_middle + norm_input_term(xhat1, rate1, gain1, grad_first)).astype(low)

    up_slots = jnp.where(jnp.arange(wide)[None, :, None] == y, grad_up_bias[:, None, :], 0.0)
    vectors = jnp.concatenate(
        [
            rows_sum(grad_first * xhat1), rows_sum(grad_first), rows_sum(grad_middle),
            rows_sum(grad_second * xhat2), rows_sum(grad_second), rows_sum(cot_mine),
            q_sum[:, 0].reshape(-1), v_sum[:, 0].reshape(-1), up_slots.reshape(-1),
        ]
    )
    g_qkv, g_out, grad_tokens_all, vectors = finish(
        nt, [sum_qkv, sum_out], [], grad_tokens, vectors.reshape(-1, 128), 5, "finish_attn"
    )
    vectors = vectors.reshape(-1)
    g_first_gain, g_first_shift, g_out_bias, g_second_gain, g_second_shift, g_down_bias = (
        vectors[i * d : (i + 1) * d] for i in range(6)
    )
    rest = vectors[6 * d :]
    g_q = lax.dynamic_index_in_dim(rest[:d].reshape(nt, heads_here, width), t, 0, keepdims=False)
    g_v = lax.dynamic_index_in_dim(rest[d : 2 * d].reshape(nt, heads_here, width), t, 0, keepdims=False)
    g_up_bias = lax.dynamic_index_in_dim(rest[2 * d :].reshape(nt, hidden_here), t, 0, keepdims=False)
    g_qkv = g_qkv.reshape(d, 3, heads_here, width).transpose(0, 2, 1, 3).reshape(d, heads_here, 3 * width)
    return (
        output_all.reshape(length, d), grad_tokens_all.reshape(length, d), g_first_gain, g_first_shift, g_qkv,
        jnp.concatenate([g_q, g_v], axis=1), g_out, g_out_bias, g_second_gain, g_second_shift,
        g_up, g_up_bias, g_down, g_down_bias,
    )


def solution(mesh):
    rows, cols, both = P("dp", None), P(None, "tensor"), P("tensor", None)
    return jax.shard_map(
        per_device,
        mesh=mesh,
        in_specs=(
            rows, rows, P(), P(), P(None, "tensor", None), both, both, P(), P(), P(), cols, P("tensor"), both, P(), rows,
        ),
        out_specs=(
            rows, rows, P(), P(), P(None, "tensor", None), both, both, P(), P(), P(), cols, P("tensor"), both, P(),
        ),
        check_vma=False,
    )
```

```python
import functools
import math

import jax
import jax.numpy as jnp
from jax import lax
from jax.experimental import pallas as pl
from jax.experimental.pallas import tpu as pltpu
from jax.sharding import PartitionSpec as P

MESH = pl.DeviceIdType.MESH
ANY = pl.BlockSpec(memory_space=pl.ANY)
VM = pl.BlockSpec(memory_space=pltpu.VMEM)


def grid_of(n_tensor):
    lines = min(4, n_tensor)
    return lines, n_tensor // lines


def where_am_i(n_tensor):
    lines, wide = grid_of(n_tensor)
    dp, t = lax.axis_index("dp"), lax.axis_index("tensor")
    return dp, t, t // wide, t % wide


def remote(src, dst, send, recv, peer):
    return pltpu.make_async_remote_copy(
        src_ref=src, dst_ref=dst, send_sem=send, recv_sem=recv, device_id=peer, device_id_type=MESH
    )


def as_row(vector):
    return vector[...].astype(jnp.float32).reshape(1, vector.shape[0])


def when(condition, body):
    pl.when(condition)(body)


def greet(peers):
    barrier = pltpu.get_barrier_semaphore()
    for ok, peer in peers:
        @pl.when(ok)
        def _():
            pl.semaphore_signal(barrier, inc=1, device_id=peer, device_id_type=MESH)
    pl.semaphore_wait(barrier, sum(jnp.int32(ok) for ok, peer in peers))


def neighbours(n_tensor, use_y=True, use_x=True, use_core=True):
    lines, wide = grid_of(n_tensor)
    dp, t, z, y = where_am_i(n_tensor)
    out = [(z > 0, (dp, t - wide)), (z < lines - 1, (dp, t + wide))]
    if use_y:
        out += [(y > 0, (dp, t - 1)), (y < wide - 1, (dp, t + 1))]
    if use_x:
        out.append((dp >= 0, (dp ^ 2, t)))
    if use_core:
        out.append((dp >= 0, (dp ^ 1, t)))
    return out


def front_kernel(n_tensor, heads, n_attn, n_mlp, *refs):
    lines, wide = grid_of(n_tensor)
    dp, t, z, y = where_am_i(n_tensor)
    n = n_attn + n_mlp
    refs = list(refs)

    def take(count):
        got, refs[:] = refs[:count], refs[count:]
        return got

    own, inputs = take(n), take(front_inputs)
    full, outputs = take(n), take(front_outputs)
    z_send, z_recv, y_send, y_recv, x_send, x_recv, c_send, c_recv, l_sem = take(9)
    before, work, after, share, share_end = front_program(n_tensor, heads, inputs, full[:n_attn], outputs, refs)
    quad = dp % 4

    items, group_of = [], ([], [])
    for a in range(n):
        size = own[a].shape[0]
        split = a < n_attn and size % 128 == 0
        for item in [(a, 0, size // 8, True), (a, size // 2, size // 4, False)] if split else [(a, 0, size // 4, True)]:
            group_of[a >= n_attn].append(len(items))
            items.append(item)

    def slot(i, zz, yy):
        return zz * wide + yy if items[i][0] < n_attn else zz

    def piece(ref, i, q):
        a, first, size, by_x = items[i]
        return ref.at[pl.ds(pl.multiple_of(first + (q if by_x else q % 2) * size, size), size)]

    def block(i, zz, yy, q):
        return piece(full[items[i][0]].at[slot(i, zz, yy)], i, q)

    peers = neighbours(n_tensor)
    if wide > 2:
        peers += [(yy != y, (dp, z * wide + yy)) for yy in range(wide)]
    greet(peers)
    local = [pltpu.make_async_copy(own[a], full[a].at[z * wide + y if a < n_attn else z], l_sem.at[a]) for a in range(n)]
    for c in local:
        c.start()
    up, down = (dp, t + wide), (dp, t - wide)
    z_has = ((z < lines - 1), (z > 0))
    y_has = ((y < wide - 1), (y > 0))

    def z_copy(a, zz, side, mine=False):
        src = piece(own[items[a][0]], a, quad) if mine else block(a, zz, y, quad)
        return remote(src, block(a, zz, y, quad), z_send.at[side, a, zz], z_recv.at[side, a, zz], (up, down)[side])

    def y_copy(a, zz, yy, side, mine=False):
        src = piece(own[items[a][0]], a, quad) if mine else block(a, zz, yy, quad)
        peer = ((dp, t + 1), (dp, t - 1))[side]
        return remote(src, block(a, zz, yy, quad), y_send.at[side, a, zz, yy], y_recv.at[side, a, zz, yy], peer)

    def x_copy(a, zz, yy, q):
        return remote(block(a, zz, yy, q), block(a, zz, yy, q), x_send.at[a, zz, yy], x_recv.at[a, zz, yy], (dp ^ 2, t))

    def c_copy(a, zz, yy, q, hop):
        return remote(
            block(a, zz, yy, q), block(a, zz, yy, q), c_send.at[hop, a, zz, yy], c_recv.at[hop, a, zz, yy], (dp ^ 1, t)
        )

    def spread(a, zz, yy):
        if items[a][3]:
            x_copy(a, zz, yy, quad).start()
        c_copy(a, zz, yy, quad, 0).start()

    def arrays(group):
        return group_of[group]

    def y_start(zz, yy, side, mine=False):
        @pl.when(y_has[side])
        def _():
            for a in arrays(0):
                y_copy(a, zz, yy, side, mine).start()

    def z_begin(group):
        for side in range(2):
            @pl.when(z_has[side])
            def _():
                for a in arrays(group):
                    z_copy(a, z, side, True).start()

    def z_step(group, k):
        for side in range(2):
            zz = z - k if side == 0 else z + k

            @pl.when((zz >= 0) if side == 0 else (zz < lines))
            def _():
                for a in arrays(group):
                    z_copy(a, zz, side).wait_recv()

                @pl.when(z_has[side])
                def _():
                    for a in arrays(group):
                        z_copy(a, zz, side).start()

                if group == 0:
                    for s in range(2):
                        y_start(zz, y, s)
                for a in arrays(group):
                    spread(a, zz, y)

    def others(group, zs, body):
        for zz in zs:
            for yy in range(wide) if group == 0 else [y]:
                @pl.when((zz != z) | (yy != y))
                def _():
                    body(zz, yy)

    def pass_on(group, zs):
        def body(zz, yy):
            for a in arrays(group):
                if items[a][3]:
                    x_copy(a, zz, yy, quad ^ 2).wait_recv()
                    c_copy(a, zz, yy, quad ^ 2, 1).start()

        others(group, zs, body)

    def arrived(group):
        def body(zz, yy):
            for a in arrays(group):
                for hop in range(1 + items[a][3]):
                    c_copy(a, zz, yy, quad ^ (1 + 2 * hop), hop).wait_recv()

        others(group, range(lines), body)

    def settle(group):
        def body(zz, yy):
            for a in arrays(group):
                for hop in range(1 + items[a][3]):
                    c_copy(a, zz, yy, quad ^ (2 * hop), hop).wait_send()
                if items[a][3]:
                    x_copy(a, zz, yy, quad).wait_send()

        others(group, range(lines), body)
        for side in range(2):
            for k in range(lines):
                zz = z - k if side == 0 else z + k

                @pl.when(z_has[side] & (zz >= 0) & (zz < lines))
                def _():
                    for a in arrays(group):
                        z_copy(a, zz, side).wait_send()

    z_begin(0)
    for side in range(2):
        y_start(z, y, side, True)
    before()
    for k in range(1, lines):
        z_step(0, k)
    z_begin(1)
    for m in range(1, wide):
        for side in range(2):
            yy = y - m if side == 0 else y + m

            @pl.when((yy >= 0) if side == 0 else (yy < wide))
            def _():
                for zz in range(lines):
                    for a in arrays(0):
                        y_copy(a, zz, yy, side).wait_recv()
                    if m < wide - 1:
                        y_start(zz, yy, side)
                    for a in arrays(0):
                        spread(a, zz, yy)
    z_step(1, 1)
    for zz in range(lines):
        pass_on(0, [zz])
        if zz == lines // 2:
            z_step(1, 2)
    arrived(0)
    for c in local:
        c.wait()
    @pl.loop(0, n_tensor)
    def _(p):
        work(p)
        for k in range(3, lines):
            when(p == k - 2, functools.partial(z_step, 1, k))

    after()
    share()
    for zz in range(lines):
        pass_on(1, [zz])
    share_end()
    arrived(1)
    settle(0)
    settle(1)
    for side in range(2):
        @pl.when(y_has[side])
        def _():
            for zz in range(lines):
                for m in range(wide):
                    yy = y - m if side == 0 else y + m

                    @pl.when((yy >= 0) if side == 0 else (yy < wide))
                    def _():
                        for a in arrays(0):
                            y_copy(a, zz, yy, side).wait_send()


def front(n_tensor, attn, mlp, slopes, segments, tokens, rows):
    lines, wide = grid_of(n_tensor)
    n = len(attn) + len(mlp)
    arrays = list(attn) + list(mlp)
    d = tokens.shape[1]
    chunk, span = tokens.shape[0] // n_tensor, segments.shape[1]
    lanes = attn[0].shape[1] // 3
    shape, low, f32 = jax.ShapeDtypeStruct, jnp.bfloat16, jnp.float32
    outs = [shape(((n_tensor if i < len(attn) else lines),) + a.shape, a.dtype) for i, a in enumerate(arrays)]
    outs += [
        shape((n_tensor, chunk, lanes), low), shape((n_tensor, span, lanes), low), shape((n_tensor, span, lanes), low),
        shape((n_tensor, chunk, lanes), low), shape((chunk, d), f32), shape((wide, chunk, d), low), shape((d, span), low),
    ]
    dma = pltpu.SemaphoreType.DMA
    return pl.pallas_call(
        functools.partial(front_kernel, n_tensor, slopes.shape[0] // n_tensor, len(attn), len(mlp)),
        out_shape=outs,
        in_specs=[VM] * n + [pl.BlockSpec(memory_space=pltpu.SMEM), VM, ANY] + [VM] * len(rows),
        out_specs=[VM] * len(attn) + [ANY] * len(mlp) + [VM] * front_outputs,
        scratch_shapes=[dma((2, 2 * n, lines))] * 2
        + [dma((2, 2 * n, lines, wide))] * 2
        + [dma((2 * n, lines, wide))] * 2
        + [dma((2, 2 * n, lines, wide))] * 2
        + [dma((n,))]
        + [pltpu.VMEM((chunk, span), f32)] + [pltpu.VMEM((span, d), low)] * 2 + [dma((span // chunk,)), dma((wide,)), dma((wide,))],
        compiler_params=pltpu.CompilerParams(collective_id=0, has_side_effects=True, vmem_limit_bytes=60 * 2**20),
        name="front",
    )(*arrays, slopes, segments, tokens, *rows)


def add_rows(dst, terms):
    rows = dst.shape[0]
    step = 32 if rows % 32 == 0 else rows

    @pl.loop(0, rows // step)
    def _(i):
        part = pl.ds(pl.multiple_of(i * step, step), step)
        total = terms[0][part].astype(jnp.float32)
        for term in terms[1:]:
            total = total + term[part].astype(jnp.float32)
        dst[part] = total.astype(dst.dtype)


def pair_sums(n_tensor, terms, sums, from_c, to_x, from_x, c_send, c_recv, x_send, x_recv):
    dp, t, z, y = where_am_i(n_tensor)
    quad = dp % 4
    side_x, core = quad // 2, quad % 2
    arrays = range(len(terms))

    def quarter(a, s, q):
        rows = terms[a].shape[1] // 4
        return terms[a].at[s, pl.ds(pl.multiple_of(q * rows, rows), rows)]

    def c_copy(a, s, h):
        return remote(
            quarter(a, s, h * 2 + 1 - core), from_c[a].at[s, h], c_send.at[a, s, h], c_recv.at[a, s, h], (dp ^ 1, t)
        )

    def x_copy(a, s):
        return remote(to_x[a].at[s], from_x[a].at[s], x_send.at[a, s], x_recv.at[a, s], (dp ^ 2, t))

    def start(s):
        for a in arrays:
            for h in range(2):
                c_copy(a, s, h).start()

    def core_stage(s):
        for a in arrays:
            for h in range(2):
                c_copy(a, s, h).wait_recv()
            add_rows(to_x[a].at[s], [quarter(a, s, (1 - side_x) * 2 + core), from_c[a].at[s, 1 - side_x]])
            x_copy(a, s).start()
            add_rows(sums[a].at[s], [quarter(a, s, quad), from_c[a].at[s, side_x]])

    def x_stage(s):
        for a in arrays:
            x_copy(a, s).wait_recv()
            add_rows(sums[a].at[s], [sums[a].at[s], from_x[a].at[s]])

    def settle(s):
        for a in arrays:
            for h in range(2):
                c_copy(a, s, h).wait_send()
            x_copy(a, s).wait_send()

    return start, core_stage, x_stage, settle


def pair_scratch(shapes, slots):
    low, dma = jnp.bfloat16, pltpu.SemaphoreType.DMA
    n = len(shapes)
    quarters = [(r // 4, c) for r, c in shapes]
    return (
        [pltpu.VMEM((slots, 2) + q, low) for q in quarters]
        + [pltpu.VMEM((slots,) + q, low) for q in quarters] * 2
        + [dma((n, slots, 2))] * 2 + [dma((n, slots))] * 2
    )


def doubling_peers(n_tensor):
    dp, t, z, y = where_am_i(n_tensor)
    bits = lambda size: [1 << i for i in range((size - 1).bit_length())]
    return [(dp ^ b, t) for b in bits(lax.axis_size("dp"))] + [(dp, t ^ b) for b in bits(n_tensor)]


def doubling_program(n_tensor, own, out, total, got, send, recv):
    peers = doubling_peers(n_tensor)

    def step(i):
        return remote(total.at[i], got.at[i], send.at[i], recv.at[i], peers[i])

    def begin():
        total[0] = own[...]
        step(0).start()

    def advance(i):
        step(i).wait_recv()
        if i + 1 < len(peers):
            total[i + 1] = total[i] + got[i]
            step(i + 1).start()
        else:
            out[...] = total[i] + got[i]

    def settle():
        for i in range(len(peers)):
            step(i).wait_send()

    return [begin] + [functools.partial(advance, i) for i in range(len(peers))] + [settle]


def finish_kernel(n_tensor, n_attn, n_mlp, with_vectors, pull, *refs):
    lines, wide = grid_of(n_tensor)
    dp, t, z, y = where_am_i(n_tensor)
    n = n_attn + n_mlp
    refs = list(refs)

    def take(count):
        got, refs[:] = refs[:count], refs[count:]
        return got

    terms, rows_own = take(n), take(1)
    vec_own = take(1)[0] if with_vectors else None
    pull_in = take(pull_inputs) if pull else []
    final, rows_full = take(n), take(1)
    vec_out = take(1)[0] if with_vectors else None
    pull_out = take(pull_outputs) if pull else []
    acc, from_y, from_z, whole = (take(n) for i in range(4))
    y_send, y_recv, z_send, z_recv, q_send, q_recv = take(6)
    rows_steps = rows_program(n_tensor, rows_own, rows_full, *take(5))
    vec_steps = doubling_program(n_tensor, vec_own, vec_out, *take(4)) if with_vectors else []
    if pull:
        pull_prepare, work, pull_peers, pull_first, pull_last = pull_program(n_tensor, pull, pull_in, pull_out, refs)
    quad = dp % 4
    core_peer, x_peer = (dp ^ 1, t), (dp ^ 2, t)
    lines_order = [i // 2 if i % 2 else lines - 1 - i // 2 for i in range(lines)]
    attn, mlp, order = list(range(n_attn)), list(range(n_attn, n)), list(range(n))

    def index(a, zz, yy):
        return zz * wide + yy if a < n_attn else zz

    def quarter(ref, q):
        rows = ref.shape[0] // 4
        return ref.at[pl.ds(pl.multiple_of(q * rows, rows), rows)]

    def y_copy(a, zz, yy, side):
        peer = ((dp, t + 1), (dp, t - 1))[side]
        lane = zz * wide + yy
        return remote(acc[a].at[lane], from_y[a].at[side, lane], y_send.at[side, a, lane], y_recv.at[side, a, lane], peer)

    def z_copy(a, zz, side):
        peer = ((dp, t + wide), (dp, t - wide))[side]
        return remote(
            acc[a].at[index(a, zz, y)], from_z[a].at[side, zz], z_send.at[side, a, zz], z_recv.at[side, a, zz], peer
        )

    def y_begin(zz):
        for m in range(wide):
            yy = (y + 1 + m) % wide
            for a in attn:
                lane = zz * wide + yy
                add_rows(acc[a].at[lane], [terms[a].at[lane]])
                when((y == 0) & (yy > y), lambda: y_copy(a, zz, yy, 0).start())
                when((y == wide - 1) & (yy < y), lambda: y_copy(a, zz, yy, 1).start())

    def y_stage(zz):
        for a in attn:
            for k in range(wide):
                for side, yy in ((0, wide - 1 - k), (1, k)):
                    @pl.when(((yy >= y) & (y > 0)) if side == 0 else ((yy <= y) & (y < wide - 1)))
                    def _():
                        lane = zz * wide + yy
                        y_copy(a, zz, yy, side).wait_recv()
                        add_rows(acc[a].at[lane], [acc[a].at[lane], from_y[a].at[side, lane]])
                        when(yy != y, lambda: y_copy(a, zz, yy, side).start())

    def z_round(r, chosen):
        for side in range(2):
            zz = lines - 1 - r + z if side == 0 else z - (lines - 1 - r)

            @pl.when((zz < lines) & (zz >= 0))
            def _():
                @pl.when((z > 0) if side == 0 else (z < lines - 1))
                def _():
                    for a in chosen:
                        s = index(a, zz, y)
                        z_copy(a, zz, side).wait_recv()
                        add_rows(acc[a].at[s], [acc[a].at[s], from_z[a].at[side, zz]])

                if r < lines - 1:
                    for a in chosen:
                        z_copy(a, zz, side).start()

    def q_copy(a, q, hop, peer):
        return remote(quarter(whole[a], q), quarter(whole[a], q), q_send.at[hop, a], q_recv.at[hop, a], peer)

    def home(a):
        add_rows(quarter(whole[a], quad), [acc[a].at[index(a, z, y)]])
        q_copy(a, quad, 0, x_peer).start()
        q_copy(a, quad, 1, core_peer).start()

    def widen(a, q):
        add_rows(quarter(final[a], q), [quarter(whole[a], q)])

    def aside():
        if len(rows_steps) > 1:
            rows_steps.pop(0)()
        if len(vec_steps) > 1:
            vec_steps.pop(0)()

    def late(r):
        aside()
        if r == 1:
            z_round(1, mlp)
            z_round(0, attn)
        else:
            z_round(r, mlp)
            z_round(r - 1, attn)

    peers = neighbours(n_tensor)
    if pull:
        peers += pull_peers
    if with_vectors:
        peers += [(dp >= 0, peer) for peer in doubling_peers(n_tensor)]
    greet(peers)
    for zz in lines_order:
        y_begin(zz)
        for a in order[n_attn:]:
            add_rows(acc[a].at[zz], [terms[a].at[zz]])
    z_round(0, mlp)
    rows_steps.pop(0)()
    if with_vectors:
        vec_steps.pop(0)()
    if attn:
        for zz in lines_order:
            y_stage(zz)
            if with_vectors:
                vec_steps.pop(0)()
    steps = [functools.partial(late, r) for r in range(1, lines)]
    if pull:
        pull_prepare()

        @pl.loop(0, n_tensor)
        def _(p):
            work(p)
            for k in (n_tensor // 2, n_tensor - 1):
                when(p == k, steps.pop(0))

        pull_first()
    for step in steps:
        step()
    for a in mlp:
        home(a)
    z_round(lines - 1, attn)
    for a in attn:
        home(a)
    aside()
    for a in mlp + attn:
        widen(a, quad)
        q_copy(a, quad ^ 2, 0, x_peer).wait_recv()
        q_copy(a, quad ^ 2, 2, core_peer).start()
        widen(a, quad ^ 2)
    if pull:
        pull_last()
    while rows_steps:
        rows_steps.pop(0)()
    while vec_steps:
        vec_steps.pop(0)()
    for a in order:
        q_copy(a, quad ^ 1, 1, core_peer).wait_recv()
        widen(a, quad ^ 1)
        q_copy(a, quad ^ 3, 2, core_peer).wait_recv()
        widen(a, quad ^ 3)
        q_copy(a, quad, 0, x_peer).wait_send()
        q_copy(a, quad, 1, core_peer).wait_send()
        q_copy(a, quad ^ 2, 2, core_peer).wait_send()
        if a < n_attn:
            for zz in range(lines):
                for yy in range(wide):
                    when(yy > y, lambda: y_copy(a, zz, yy, 0).wait_send())
                    when(yy < y, lambda: y_copy(a, zz, yy, 1).wait_send())
        for zz in range(lines):
            when(zz > z, lambda: z_copy(a, zz, 0).wait_send())
            when(zz < z, lambda: z_copy(a, zz, 1).wait_send())


def finish(n_tensor, attn, mlp, rows, vectors, cid, name, pull=None):
    lines, wide = grid_of(n_tensor)
    arrays = list(attn) + list(mlp)
    n = len(arrays)
    vm, dma = pltpu.VMEM, pltpu.SemaphoreType.DMA
    low, f32 = jnp.bfloat16, jnp.float32
    quarters = [a.shape[1:] for a in arrays]
    each = lambda lead: [vm(lead(a, i) + q, low) for i, (a, q) in enumerate(zip(arrays, quarters))]
    steps = (lax.axis_size("dp") - 1).bit_length() + (n_tensor - 1).bit_length()
    scratch = (
        each(lambda a, i: (a.shape[0],))
        + each(lambda a, i: (2, n_tensor) if i < len(attn) else (1, 1))
        + each(lambda a, i: (2, lines))
        + [vm((4 * q[0], q[1]), low) for q in quarters]
    )
    sems = (
        [dma((2, max(1, len(attn)), n_tensor))] * 2 + [dma((2, n, lines))] * 2 + [dma((3, n))] * 2
        + [dma((2, 1, lines))] * 2 + [dma((2, 1, lines, wide))] * 2 + [dma((1,))]
    )
    inputs, in_specs = arrays + [rows], [VM] * n + [VM]
    out_shape = [jax.ShapeDtypeStruct((4 * q[0], q[1]), f32) for q in quarters]
    out_shape.append(jax.ShapeDtypeStruct((n_tensor,) + rows.shape, low))
    out_specs = [VM] * n + [ANY]
    if vectors is not None:
        inputs, in_specs = inputs + [vectors], in_specs + [VM]
        out_shape.append(jax.ShapeDtypeStruct(vectors.shape, vectors.dtype))
        out_specs.append(VM)
        sems += [vm((steps,) + vectors.shape, jnp.float32)] * 2 + [dma((steps,))] * 2
    heads = 0
    if pull is not None:
        heads = pull[0].shape[0] // n_tensor
        inputs, in_specs = inputs + list(pull), in_specs + [pl.BlockSpec(memory_space=pltpu.SMEM)] + [VM] * (pull_inputs - 3) + [ANY, VM]
        shapes, more = pull_shapes(n_tensor, pull)
        out_shape += shapes
        out_specs += [VM] * pull_outputs
        sems += more
    out = pl.pallas_call(
        functools.partial(
            finish_kernel, n_tensor, len(attn), len(mlp), vectors is not None, heads
        ),
        out_shape=out_shape,
        in_specs=in_specs,
        out_specs=out_specs,
        scratch_shapes=scratch + sems,
        compiler_params=pltpu.CompilerParams(collective_id=cid, has_side_effects=True, vmem_limit_bytes=63 * 2**20),
        name=name,
    )(*inputs)
    sums = out[:n]
    if lax.axis_size("dp") > 4:
        sums = [lax.psum(s, "dp") * 0.25 for s in sums]
    return list(sums) + list(out[n:])


def mlp_kernel(n_tensor, *refs):
    lines, wide = grid_of(n_tensor)
    dp, t, z, y = where_am_i(n_tensor)
    second, cot_all, up, down, bias, middle, gain2, down_bias = refs[:8]
    sum_up, sum_down, up_sum, grad_middle, grad_low, output, columns = refs[8:15]
    terms_up, terms_down = refs[15:17]
    pair, (feed, grad, second_t, share_own, share_got, grad_second, cot) = refs[17:27], refs[27:34]
    s_send, s_recv, l_sem = refs[34:]
    sums, terms = (sum_up, sum_down), (terms_up, terms_down)
    pair_start, core_stage, x_stage, pair_settle = pair_sums(
        n_tensor, terms, sums, pair[0:2], pair[2:4], pair[4:6], *pair[6:]
    )
    low, f32 = jnp.bfloat16, jnp.float32
    chunk = output.shape[0]
    tile = min(128, chunk)

    def share(kind, yy, slot):
        return remote(
            share_own.at[kind, yy], share_got.at[kind, slot], s_send.at[kind, yy], s_recv.at[kind, slot],
            (dp, z * wide + yy),
        )

    peers = [(dp >= 0, (dp ^ 1, t)), (dp >= 0, (dp ^ 2, t))]
    peers += [(yy != y, (dp, z * wide + yy)) for yy in range(wide)]
    count = second.shape[0]
    load = pltpu.make_async_copy(cot_all.at[pl.ds(pl.multiple_of(z * count, count), count)], cot, l_sem)
    load.start()
    greet(peers)
    feed[...] = jnp.zeros(feed.shape, f32)
    grad[...] = jnp.zeros(grad.shape, f32)

    @pl.loop(0, second.shape[0] // tile)
    def _(i):
        here = pl.ds(pl.multiple_of(i * tile, tile), tile)
        second_t[:, here] = second[here].T

    load.wait()

    @pl.loop(0, lines)
    def _(s):
        upper = dot(second[...], up[s], NN) + bias[s, 0:1]
        hidden, slope = gelu_and_slope(upper)
        hidden = hidden.astype(low)
        grad_upper = (dot(cot[...], down[s], NT) * slope).astype(low)
        up_sum[s] = jnp.broadcast_to(jnp.sum(grad_upper.astype(f32), axis=0, keepdims=True), up_sum.shape[1:])
        terms_down[s] = dot(hidden, cot[...], TN).astype(low)
        terms_up[s] = dot(second_t[...], grad_upper, NN).astype(low)
        pair_start(s)
        feed[...] += dot(hidden, down[s], NN)
        grad[...] += dot(grad_upper, up[s], NT)
        when(s >= 1, lambda: core_stage(jnp.maximum(s - 1, 0)))

    for kind, whole in ((0, grad), (1, feed)):
        for yy in range(wide):
            @pl.when(yy != y)
            def _():
                add_rows(share_own.at[kind, yy], [whole.at[pl.ds(yy * chunk, chunk)]])
                share(kind, yy, y).start()
    core_stage(lines - 1)

    def collect(kind, whole, out, more):
        share_got[kind, y] = jnp.zeros((chunk, second.shape[1]), low)
        for yy in range(wide):
            when(yy != y, lambda: share(kind, yy, yy).wait_recv())
        mine = whole.at[pl.ds(pl.multiple_of(y * chunk, chunk), chunk)]
        add_rows(out, [mine] + [share_got.at[kind, yy] for yy in range(wide)] + more)

    for s in range(lines // 2):
        x_stage(s)
    collect(0, grad, grad_second, [])
    columns[...] = jnp.zeros(columns.shape, f32)

    @pl.loop(0, chunk // tile)
    def _(i):
        here = pl.ds(pl.multiple_of(i * tile, tile), tile)
        mine = cot[pl.ds(pl.multiple_of(y * chunk + i * tile, tile), tile)].astype(f32)
        xhat, rate = normalized(middle[here])
        got = grad_second[here]
        total = mine + norm_input_term(xhat, rate, as_row(gain2), got)
        grad_middle[here] = total
        grad_low[here] = total.astype(low)
        for j, term in enumerate((got * xhat, got, total, mine)):
            columns[j : j + 1] += jnp.sum(term, axis=0, keepdims=True)
        feed[pl.ds(pl.multiple_of(y * chunk + i * tile, tile), tile)] += middle[here] + as_row(down_bias)

    for s in range(lines // 2, lines - 1):
        x_stage(s)
    collect(1, feed, output, [])
    x_stage(lines - 1)
    for yy in range(wide):
        for kind in range(2):
            when(yy != y, lambda: share(kind, yy, y).wait_send())
    for s in range(lines):
        pair_settle(s)


def mlp(n_tensor, second, cot, up, down, bias, middle, gain2, down_bias):
    lines, wide = grid_of(n_tensor)
    shape, vm, dma = jax.ShapeDtypeStruct, pltpu.VMEM, pltpu.SemaphoreType.DMA
    low, f32 = jnp.bfloat16, jnp.float32
    d, hidden = up.shape[1:]
    chunk = middle.shape[0]
    quarters = [(d // 4, hidden), (hidden // 4, d)]
    return pl.pallas_call(
        functools.partial(mlp_kernel, n_tensor),
        out_shape=[shape((lines,) + q, low) for q in quarters]
        + [shape((lines, 8, hidden), f32), shape((chunk, d), f32), shape((chunk, d), low), shape((chunk, d), low), shape((8, d), f32)],
        in_specs=[VM, ANY] + [VM] * 6,
        out_specs=[VM] * 7,
        scratch_shapes=[vm(up.shape, low), vm(down.shape, low)] + pair_scratch([up.shape[1:], down.shape[1:]], lines)
        + [vm(second.shape, f32)] * 2 + [vm((d, second.shape[0]), low)] + [vm((2, wide, chunk, d), low)] * 2
        + [vm((chunk, d), f32), vm(second.shape, low)] + [dma((2, wide))] * 2 + [dma],
        compiler_params=pltpu.CompilerParams(collective_id=3, has_side_effects=True, vmem_limit_bytes=60 * 2**20),
        name="mlp",
    )(second, cot, up, down, bias, middle, gain2, down_bias)


def rows_program(n_tensor, own, full, z_send, z_recv, y_send, y_recv, l_sem):
    lines, wide = grid_of(n_tensor)
    dp, t, z, y = where_am_i(n_tensor)
    n = len(own)

    def z_copy(a, zz, side, mine=False):
        dst = full[a].at[zz * wide + y]
        peer = ((dp, t + wide), (dp, t - wide))[side]
        return remote(own[a] if mine else dst, dst, z_send.at[side, a, zz], z_recv.at[side, a, zz], peer)

    def y_copy(a, zz, yy, side, mine=False):
        dst = full[a].at[zz * wide + yy]
        peer = ((dp, t + 1), (dp, t - 1))[side]
        return remote(own[a] if mine else dst, dst, y_send.at[side, a, zz, yy], y_recv.at[side, a, zz, yy], peer)

    z_has = ((z < lines - 1), (z > 0))
    y_has = ((y < wide - 1), (y > 0))
    local = [pltpu.make_async_copy(own[a], full[a].at[t], l_sem.at[a]) for a in range(n)]

    def begin():
        for side in range(2):
            for a in range(n):
                when(z_has[side], lambda: z_copy(a, z, side, True).start())
                when(y_has[side], lambda: y_copy(a, z, y, side, True).start())
        for c in local:
            c.start()

    def along_z(k):
        for side in range(2):
            zz = z - k if side == 0 else z + k

            @pl.when((zz >= 0) & (zz < lines))
            def _():
                for a in range(n):
                    z_copy(a, zz, side).wait_recv()
                    when(z_has[side], lambda: z_copy(a, zz, side).start())
                    for s in range(2):
                        when(y_has[s], lambda: y_copy(a, zz, y, s).start())

    def along_y(m):
        for side in range(2):
            yy = y - m if side == 0 else y + m

            @pl.when((yy >= 0) & (yy < wide))
            def _():
                for zz in range(lines):
                    for a in range(n):
                        y_copy(a, zz, yy, side).wait_recv()
                        if m < wide - 1:
                            when(y_has[side], lambda: y_copy(a, zz, yy, side).start())

    def settle():
        for side in range(2):
            for k in range(lines):
                zz = z - k if side == 0 else z + k

                @pl.when(z_has[side] & (zz >= 0) & (zz < lines))
                def _():
                    for a in range(n):
                        z_copy(a, zz, side).wait_send()
            for m in range(wide):
                yy = y - m if side == 0 else y + m

                @pl.when(y_has[side] & (yy >= 0) & (yy < wide))
                def _():
                    for zz in range(lines):
                        for a in range(n):
                            y_copy(a, zz, yy, side).wait_send()
        for c in local:
            c.wait()

    return (
        [begin]
        + [functools.partial(along_z, k) for k in range(1, lines)]
        + [functools.partial(along_y, m) for m in range(1, wide)]
        + [settle]
    )


def dot(a, b, contract, **kwargs):
    return lax.dot_general(a, b, (contract, ((), ())), preferred_element_type=jnp.float32, **kwargs)


NN, NT, TN = ((1,), (0,)), ((1,), (1,)), ((0,), (0,))


def head_of_lane(shape, heads):
    return lax.broadcasted_iota(jnp.int32, shape, 1) // (shape[1] // heads)


def attend(heads, slope_of, dist, query, keys, values):
    scale = 1.0 / math.sqrt(query.shape[1] // heads)
    head = head_of_lane(query.shape, heads)
    out = jnp.zeros(query.shape, jnp.float32)
    for h in range(heads):
        masked = jnp.where(head == h, query * jnp.bfloat16(scale), jnp.bfloat16(0))
        scores = dot(masked, keys, NT) - slope_of(h) * dist[...]
        peak = jnp.max(scores, axis=1, keepdims=True)
        expo = jnp.exp(scores - peak)
        total = jnp.sum(expo, axis=1, keepdims=True)
        part = dot(expo.astype(jnp.bfloat16), values, NN) / total
        out = jnp.where(head == h, part, out)
    return out.astype(jnp.bfloat16)


front_inputs, front_outputs = 8, 7


def column_of(row):
    return jnp.broadcast_to(row.astype(jnp.float32), (128, row.shape[1])).T[:, 0:1].astype(jnp.int32)


def masked_distance(left, top, left_start, top_start):
    shape = (left.shape[0], top.shape[1])
    down = left_start + lax.broadcasted_iota(jnp.int32, shape, 0)
    across = top_start + lax.broadcasted_iota(jnp.int32, shape, 1)
    far = down - across if left_start else across - down
    return jnp.where((left == top) & (far >= 0), far.astype(jnp.float32), far_off)


def front_program(n_tensor, heads, ins, weights, outs, scratch):
    lines, wide = grid_of(n_tensor)
    dp, t, z, y = where_am_i(n_tensor)
    slopes, segments, tokens, *rows = ins
    qkv_all, out_all, small_all = weights
    q, k, v, context, middle, second, normed_t = outs
    dist, near, normed, l_sem, s_send, s_recv = scratch
    chunk, lanes = q.shape[1:]
    span, d = near.shape
    behind = span - chunk
    low, f32 = jnp.bfloat16, jnp.float32
    tile = min(128, chunk)

    def row(i):
        return as_row(rows[i])

    def before():
        loads = [
            pltpu.make_async_copy(
                tokens.at[pl.ds(pl.multiple_of(jnp.maximum(t - behind // chunk + j, 0) * chunk, chunk), chunk)],
                near.at[pl.ds(j * chunk, chunk)], l_sem.at[j],
            )
            for j in range(span // chunk)
        ]
        for load in loads:
            load.start()
        own = column_of(segments[0:1, behind:])
        dist[...] = masked_distance(own, segments[0:1, :], behind, 0)
        for load in loads:
            load.wait()

        @pl.loop(0, span // tile)
        def _(i):
            here = pl.ds(pl.multiple_of(i * tile, tile), tile)
            xhat, rate = normalized(near[here].astype(f32))
            value = (xhat * row(0) + row(1)).astype(low)
            normed[here] = value
            normed_t[:, here] = value.T

    def work(p):
        bias = small_all[p, 0:16, :].astype(f32)
        query = (dot(normed[behind:], qkv_all[p, :, :lanes], NN) + bias[0:1, :lanes]).astype(low)
        both = dot(normed[...], qkv_all[p, :, lanes:], NN)
        keys = both[:, :lanes].astype(low)
        values = (both[:, lanes:] + bias[1:2, :lanes]).astype(low)
        q[p], k[p], v[p] = query, keys, values
        context[p] = attend(heads, lambda h: slopes[p * heads + h], dist, query, keys, values)

    def after():
        @pl.loop(0, chunk // tile)
        def _(i):
            start = pl.multiple_of(i * tile, tile)
            here = pl.ds(start, tile)
            total = near[pl.ds(behind + start, tile)].astype(f32) + row(4)
            for p in range(n_tensor):
                total = total + dot(context[p, here], out_all[p], NN)
            middle[here] = total
            xhat, rate = normalized(total)
            second[y, here] = (xhat * row(2) + row(3)).astype(low)

    def step(yy, slot):
        return remote(second.at[slot], second.at[slot], s_send.at[yy], s_recv.at[slot], (dp, z * wide + yy))

    def share():
        for yy in range(wide):
            when(yy != y, lambda: step(yy, y).start())

    def share_end():
        for yy in range(wide):
            @pl.when(yy != y)
            def _():
                step(yy, yy).wait_recv()
                step(yy, y).wait_send()

    return before, work, after, share, share_end


def pull_scores(heads, slope_of, dist, query, keys, values, grad):
    lanes = query.shape[1]
    scale = 1.0 / math.sqrt(lanes // heads)
    head = head_of_lane(query.shape, heads)
    head_rows = lax.broadcasted_iota(jnp.int32, (lanes, query.shape[0]), 0) // (lanes // heads)
    low = jnp.bfloat16
    grad_q = jnp.zeros((lanes, query.shape[0]), jnp.float32)
    grad_k = jnp.zeros(keys.shape, jnp.float32)
    grad_v = jnp.zeros(keys.shape, jnp.float32)
    for h in range(heads):
        masked = jnp.where(head == h, query * low(scale), low(0))
        masked_grad = jnp.where(head == h, grad, low(0))
        scores = dot(keys, masked, NT) - slope_of(h) * dist[...]
        peak = jnp.max(scores, axis=0, keepdims=True)
        expo = jnp.exp(scores - peak)
        probs = expo * (1.0 / jnp.sum(expo, axis=0, keepdims=True))
        grad_probs = dot(values, masked_grad, NT)
        inner = jnp.sum(probs * grad_probs, axis=0, keepdims=True)
        grad_scores = (probs * (grad_probs - inner)).astype(low)
        grad_v = grad_v + dot(probs.astype(low), masked_grad, NN)
        grad_k = grad_k + dot(grad_scores, masked, NN)
        grad_q = jnp.where(head_rows == h, dot(keys, grad_scores, TN), grad_q)
    return (jnp.transpose(grad_q) * scale).astype(low), grad_k.astype(low), grad_v.astype(low)


pull_inputs, pull_outputs = 13, 6


def pull_shapes(n_tensor, pull):
    slopes, segments, q, k, v, grad, context, out_all, qkv_all, normed_t, grad_middle, tokens, gain1 = pull
    span, chunk, lanes, d = k.shape[1], q.shape[1], q.shape[2], normed_t.shape[0]
    halo = (span - chunk) // chunk
    low, f32 = jnp.bfloat16, jnp.float32
    shape = jax.ShapeDtypeStruct
    vm, dma = pltpu.VMEM, pltpu.SemaphoreType.DMA
    outs = [
        shape((n_tensor, d // 4, 3 * lanes), low), shape((n_tensor, lanes // 4, d), low), shape((chunk, d), low), shape((8, d), f32),
        shape((n_tensor, 8, lanes), f32), shape((n_tensor, 8, lanes), f32),
    ]
    scratch = [vm(qkv_all.shape, low), vm(out_all.shape, low)]
    scratch += pair_scratch([qkv_all.shape[1:], out_all.shape[1:]], n_tensor) + [
        vm(q.shape, low), vm((n_tensor, span, 2 * lanes), low), vm((halo, chunk, d), low), vm((halo, chunk, d), low),
        dma((halo,)), dma((halo,)), vm((chunk, d), f32), vm((chunk, d), low), dma, vm((span, chunk), f32),
    ]
    return outs, scratch


def pull_program(n_tensor, heads, ins, outs, scratch):
    dp, t, z, y = where_am_i(n_tensor)
    slopes, segments, q, k, v, grad, context, out_all, qkv_all, normed_t, grad_middle, tokens, gain1 = ins
    sum_qkv, sum_out, grad_tokens, columns, q_sum, v_sum = outs
    (grad_qkv, grad_out), pair = scratch[:2], scratch[2:12]
    grad_q, grad_kv, halo_own, halo_got, h_send, h_recv, first, mine, l_sem, dist = scratch[12:]
    pair_start, core_stage, x_stage, pair_settle = pair_sums(
        n_tensor, (grad_qkv, grad_out), (sum_qkv, sum_out), pair[0:2], pair[2:4], pair[4:6], *pair[6:]
    )
    halo, chunk, d = halo_own.shape
    span, lanes = k.shape[1], q.shape[2]
    behind = span - chunk
    low, f32 = jnp.bfloat16, jnp.float32

    def prepare():
        dist[...] = masked_distance(column_of(segments[0:1, :]), segments[0:1, behind:], 0, behind)

    def work(p):
        grad_context = dot(grad[...], out_all[p], NT).astype(low)
        grad_out[p] = dot(context[p], grad[...], TN).astype(low)
        gq, gk, gv = pull_scores(heads, lambda h: slopes[p * heads + h], dist, q[p], k[p], v[p], grad_context)
        grad_q[p] = gq
        grad_kv[p, :, :lanes] = gk
        grad_kv[p, :, lanes:] = gv
        q_sum[p] = jnp.broadcast_to(jnp.sum(gq.astype(f32), axis=0, keepdims=True), (8, lanes))
        v_sum[p] = jnp.broadcast_to(jnp.sum(gv.astype(f32), axis=0, keepdims=True), (8, lanes))
        grad_qkv[p, :, :lanes] = dot(normed_t[:, behind:], gq, NN).astype(low)
        grad_qkv[p, :, lanes:] = dot(normed_t[...], grad_kv[p], NN).astype(low)
        pair_start(p)
        when(p >= 1, lambda: core_stage(jnp.maximum(p - 1, 0)))

    def step(m):
        return remote(halo_own.at[halo - 1 - m], halo_got.at[m], h_send.at[m], h_recv.at[m], (dp, t - 1 - m))

    ahead = [(t + 1 + m < n_tensor, (dp, t + 1 + m)) for m in range(halo)]
    back = [(t - 1 - m >= 0, (dp, t - 1 - m)) for m in range(halo)]
    tile = min(128, chunk)

    load = pltpu.make_async_copy(tokens.at[pl.ds(pl.multiple_of(t * chunk, chunk), chunk)], mine, l_sem)

    def rows_first():
        load.start()
        core_stage(n_tensor - 1)
        for j in range(halo):
            @pl.loop(0, chunk // tile)
            def _(i):
                here = pl.multiple_of(i * tile, tile)
                total = jnp.zeros((tile, d), f32)
                for p in range(n_tensor):
                    total = total + dot(grad_kv[p, pl.ds(j * chunk + here, tile)], qkv_all[p, :, lanes:], NT)
                halo_own[j, pl.ds(here, tile)] = total.astype(low)

        for m in range(halo):
            when(back[m][0], lambda: step(m).start())

        @pl.loop(0, chunk // tile)
        def _(i):
            here = pl.multiple_of(i * tile, tile)
            total = jnp.zeros((tile, d), f32)
            for p in range(n_tensor):
                total = total + dot(grad_kv[p, pl.ds(behind + here, tile)], qkv_all[p, :, lanes:], NT)
                total = total + dot(grad_q[p, pl.ds(here, tile)], qkv_all[p, :, :lanes], NT)
            first[pl.ds(here, tile)] = total

    def rows_last():
        for m in range(halo):
            @pl.when(ahead[m][0])
            def _():
                step(m).wait_recv()
                add_rows(first, [first, halo_got.at[m]])

            when(back[m][0], lambda: step(m).wait_send())

        load.wait()
        columns[...] = jnp.zeros(columns.shape, f32)

        @pl.loop(0, chunk // tile)
        def _(i):
            here = pl.ds(pl.multiple_of(i * tile, tile), tile)
            xhat, rate = normalized(mine[here].astype(f32))
            got = first[here]
            grad_tokens[here] = (grad_middle[here] + norm_input_term(xhat, rate, as_row(gain1), got)).astype(low)
            for j, term in enumerate((got * xhat, got)):
                columns[j : j + 1] += jnp.sum(term, axis=0, keepdims=True)

        @pl.loop(0, n_tensor)
        def _(p):
            x_stage(p)
            pair_settle(p)

    return prepare, work, ahead + back, rows_first, rows_last


norm_eps = 1e-05


def normalized(values):
    offset = values - jnp.mean(values, axis=-1, keepdims=True)
    rate = lax.rsqrt(jnp.mean(offset * offset, axis=-1, keepdims=True) + norm_eps)
    return offset * rate, rate


def norm_input_term(xhat, rate, gain, grad):
    e = grad * gain
    return rate * (e - jnp.mean(e, axis=-1, keepdims=True) - xhat * jnp.mean(e * xhat, axis=-1, keepdims=True))


def gelu_and_slope(u):
    c, a = 0.7978845608028654, 0.044715
    th = jnp.tanh(c * (u + a * u * u * u))
    slope = 0.5 * (1.0 + th) + 0.5 * u * (1.0 - th * th) * (c * (1.0 + 3.0 * a * u * u))
    return 0.5 * u * (1.0 + th), slope


far_off = 1e33
longest = 512


def per_device(
    tokens, segment_ids, first_gain, first_shift, qkv_weight, qv_bias, out_weight, out_bias, second_gain, second_shift,
    up_weight, up_bias, down_weight, down_bias, cotangent,
):
    low, f32 = jnp.bfloat16, jnp.float32
    nt = lax.axis_size("tensor")
    lines, wide = grid_of(nt)
    t = lax.axis_index("tensor")
    z, y = t // wide, t % wide
    length, d = tokens.shape
    chunk = length // nt
    halo = -(-(longest - 1) // chunk)
    behind = halo * chunk
    span = behind + chunk
    heads_here, width = qkv_weight.shape[1], qkv_weight.shape[2] // 3
    lanes = heads_here * width
    hidden_here = up_weight.shape[1]

    qkv_own = qkv_weight.reshape(d, heads_here, 3, width).transpose(0, 2, 1, 3).reshape(d, 3 * lanes)
    bias_own = jnp.pad(qv_bias.reshape(heads_here, 2, width).transpose(1, 0, 2).reshape(2, lanes), ((0, 0), (0, 128 - lanes)))
    small = jnp.concatenate([bias_own.reshape(256), up_bias])
    small = jnp.pad(small, (0, 64 * 128 - small.shape[0])).reshape(64, 128)

    seg_row = jnp.concatenate([jnp.full((behind,), -1, jnp.int32), segment_ids[0]])
    seg_near = lax.dynamic_slice_in_dim(seg_row, t * chunk, span, 0)
    segments = jnp.broadcast_to(seg_near[None], (8, span))
    total_heads = heads_here * nt
    slopes = jnp.exp2(-8.0 * (jnp.arange(total_heads, dtype=jnp.int32) + 1).astype(f32) / total_heads)

    (qkv_all, out_all, small_all, up_all, down_all, query, keys, values, context, middle, second_pair, normed_t) = front(
        nt, [qkv_own, out_weight, small], [up_weight, down_weight], slopes, segments, tokens,
        [first_gain, first_shift, second_gain, second_shift, out_bias],
    )
    small_all = small_all.reshape(nt, 64 * 128).astype(f32)
    up_bias_all = lax.dynamic_index_in_dim(
        small_all[:, 256 : 256 + hidden_here].reshape(lines, wide, hidden_here), y, 1, keepdims=False
    )
    second_pair = second_pair.reshape(wide * chunk, d)

    sum_up, sum_down, grad_up_bias, grad_middle, grad_middle_low, output_mine, columns2 = mlp(
        nt, second_pair, cotangent, up_all, down_all, jnp.broadcast_to(up_bias_all[:, None], (lines, 8, hidden_here)),
        middle, second_gain, down_bias,
    )
    grad_up_bias = grad_up_bias[:, 0]
    pull = [
        slopes, segments, query, keys, values, grad_middle_low, context, out_all, qkv_all, normed_t, grad_middle, tokens,
        first_gain,
    ]
    g_down, output_all, sum_qkv, sum_out, grad_tokens, columns1, q_sum, v_sum = finish(
        nt, [], [sum_down], output_mine, None, 1, "finish_mlp", pull
    )
    up_slots = jnp.where(jnp.arange(wide)[None, :, None] == y, grad_up_bias[:, None, :], 0.0)
    vectors = jnp.concatenate(
        [
            columns1[0], columns1[1], columns2[2], columns2[0], columns2[1], columns2[3],
            q_sum[:, 0].reshape(-1), v_sum[:, 0].reshape(-1), up_slots.reshape(-1),
        ]
    )
    g_qkv, g_out, g_up, grad_tokens_all, vectors = finish(
        nt, [sum_qkv, sum_out], [sum_up], grad_tokens, vectors.reshape(-1, 128), 5, "finish_attn"
    )
    vectors = vectors.reshape(-1)
    g_first_gain, g_first_shift, g_out_bias, g_second_gain, g_second_shift, g_down_bias = (
        vectors[i * d : (i + 1) * d] for i in range(6)
    )
    rest = vectors[6 * d :]
    g_q = lax.dynamic_index_in_dim(rest[:d].reshape(nt, heads_here, width), t, 0, keepdims=False)
    g_v = lax.dynamic_index_in_dim(rest[d : 2 * d].reshape(nt, heads_here, width), t, 0, keepdims=False)
    g_up_bias = lax.dynamic_index_in_dim(rest[2 * d :].reshape(nt, hidden_here), t, 0, keepdims=False)
    g_qkv = g_qkv.reshape(d, 3, heads_here, width).transpose(0, 2, 1, 3).reshape(d, heads_here, 3 * width)
    return (
        output_all.reshape(length, d), grad_tokens_all.reshape(length, d), g_first_gain, g_first_shift, g_qkv,
        jnp.concatenate([g_q, g_v], axis=1), g_out, g_out_bias, g_second_gain, g_second_shift,
        g_up, g_up_bias, g_down, g_down_bias,
    )


def solution(mesh):
    rows, cols, both = P("dp", None), P(None, "tensor"), P("tensor", None)
    return jax.shard_map(
        per_device,
        mesh=mesh,
        in_specs=(
            rows, rows, P(), P(), P(None, "tensor", None), both, both, P(), P(), P(), cols, P("tensor"), both, P(), rows,
        ),
        out_specs=(
            rows, rows, P(), P(), P(None, "tensor", None), both, both, P(), P(), P(), cols, P("tensor"), both, P(),
        ),
        check_vma=False,
    )
```

```python
import functools
import math

import jax
import jax.numpy as jnp
from jax import lax
from jax.experimental import pallas as pl
from jax.experimental.pallas import tpu as pltpu
from jax.sharding import PartitionSpec as P

MESH = pl.DeviceIdType.MESH
ANY = pl.BlockSpec(memory_space=pl.ANY)
VM = pl.BlockSpec(memory_space=pltpu.VMEM)


def grid_of(n_tensor):
    lines = min(4, n_tensor)
    return lines, n_tensor // lines


def where_am_i(n_tensor):
    lines, wide = grid_of(n_tensor)
    dp, t = lax.axis_index("dp"), lax.axis_index("tensor")
    return dp, t, t // wide, t % wide


def remote(src, dst, send, recv, peer):
    return pltpu.make_async_remote_copy(
        src_ref=src, dst_ref=dst, send_sem=send, recv_sem=recv, device_id=peer, device_id_type=MESH
    )


def as_row(vector):
    return vector[...].astype(jnp.float32).reshape(1, vector.shape[0])


def when(condition, body):
    pl.when(condition)(body)


def greet(peers):
    barrier = pltpu.get_barrier_semaphore()
    for ok, peer in peers:
        @pl.when(ok)
        def _():
            pl.semaphore_signal(barrier, inc=1, device_id=peer, device_id_type=MESH)
    pl.semaphore_wait(barrier, sum(jnp.int32(ok) for ok, peer in peers))


def neighbours(n_tensor, use_y=True, use_x=True, use_core=True):
    lines, wide = grid_of(n_tensor)
    dp, t, z, y = where_am_i(n_tensor)
    out = [(z > 0, (dp, t - wide)), (z < lines - 1, (dp, t + wide))]
    if use_y:
        out += [(y > 0, (dp, t - 1)), (y < wide - 1, (dp, t + 1))]
    if use_x:
        out.append((dp >= 0, (dp ^ 2, t)))
    if use_core:
        out.append((dp >= 0, (dp ^ 1, t)))
    return out


def front_kernel(n_tensor, heads, n_attn, n_mlp, *refs):
    lines, wide = grid_of(n_tensor)
    dp, t, z, y = where_am_i(n_tensor)
    n = n_attn + n_mlp
    refs = list(refs)

    def take(count):
        got, refs[:] = refs[:count], refs[count:]
        return got

    own, inputs = take(n), take(front_inputs)
    full, outputs = take(n), take(front_outputs)
    z_send, z_recv, y_send, y_recv, x_send, x_recv, c_send, c_recv, l_sem = take(9)
    before, work, after, share, share_end = front_program(n_tensor, heads, inputs, full[:n_attn], outputs, refs)
    quad = dp % 4

    items, group_of = [], ([], [])
    for a in range(n):
        size = own[a].shape[0]
        split = a < n_attn and size % 128 == 0
        for item in [(a, 0, size // 8, True), (a, size // 2, size // 4, False)] if split else [(a, 0, size // 4, True)]:
            group_of[a >= n_attn].append(len(items))
            items.append(item)

    def slot(i, zz, yy):
        return zz * wide + yy if items[i][0] < n_attn else zz

    def piece(ref, i, q):
        a, first, size, by_x = items[i]
        return ref.at[pl.ds(pl.multiple_of(first + (q if by_x else q % 2) * size, size), size)]

    def block(i, zz, yy, q):
        return piece(full[items[i][0]].at[slot(i, zz, yy)], i, q)

    peers = neighbours(n_tensor)
    if wide > 2:
        peers += [(yy != y, (dp, z * wide + yy)) for yy in range(wide)]
    greet(peers)
    local = [pltpu.make_async_copy(own[a], full[a].at[z * wide + y if a < n_attn else z], l_sem.at[a]) for a in range(n)]
    for c in local:
        c.start()
    up, down = (dp, t + wide), (dp, t - wide)
    z_has = ((z < lines - 1), (z > 0))
    y_has = ((y < wide - 1), (y > 0))

    def z_copy(a, zz, side, mine=False):
        src = piece(own[items[a][0]], a, quad) if mine else block(a, zz, y, quad)
        return remote(src, block(a, zz, y, quad), z_send.at[side, a, zz], z_recv.at[side, a, zz], (up, down)[side])

    def y_copy(a, zz, yy, side, mine=False):
        src = piece(own[items[a][0]], a, quad) if mine else block(a, zz, yy, quad)
        peer = ((dp, t + 1), (dp, t - 1))[side]
        return remote(src, block(a, zz, yy, quad), y_send.at[side, a, zz, yy], y_recv.at[side, a, zz, yy], peer)

    def x_copy(a, zz, yy, q):
        return remote(block(a, zz, yy, q), block(a, zz, yy, q), x_send.at[a, zz, yy], x_recv.at[a, zz, yy], (dp ^ 2, t))

    def c_copy(a, zz, yy, q, hop):
        return remote(
            block(a, zz, yy, q), block(a, zz, yy, q), c_send.at[hop, a, zz, yy], c_recv.at[hop, a, zz, yy], (dp ^ 1, t)
        )

    def spread(a, zz, yy):
        if items[a][3]:
            x_copy(a, zz, yy, quad).start()
        c_copy(a, zz, yy, quad, 0).start()

    def arrays(group):
        return group_of[group]

    def y_start(zz, yy, side, mine=False):
        @pl.when(y_has[side])
        def _():
            for a in arrays(0):
                y_copy(a, zz, yy, side, mine).start()

    def z_begin(group):
        for side in range(2):
            @pl.when(z_has[side])
            def _():
                for a in arrays(group):
                    z_copy(a, z, side, True).start()

    def z_step(group, k):
        for side in range(2):
            zz = z - k if side == 0 else z + k

            @pl.when((zz >= 0) if side == 0 else (zz < lines))
            def _():
                for a in arrays(group):
                    z_copy(a, zz, side).wait_recv()

                @pl.when(z_has[side])
                def _():
                    for a in arrays(group):
                        z_copy(a, zz, side).start()

                if group == 0:
                    for s in range(2):
                        y_start(zz, y, s)
                for a in arrays(group):
                    spread(a, zz, y)

    def others(group, zs, body):
        for zz in zs:
            for yy in range(wide) if group == 0 else [y]:
                @pl.when((zz != z) | (yy != y))
                def _():
                    body(zz, yy)

    def pass_on(group, zs):
        def body(zz, yy):
            for a in arrays(group):
                if items[a][3]:
                    x_copy(a, zz, yy, quad ^ 2).wait_recv()
                    c_copy(a, zz, yy, quad ^ 2, 1).start()

        others(group, zs, body)

    def arrived(group):
        def body(zz, yy):
            for a in arrays(group):
                for hop in range(1 + items[a][3]):
                    c_copy(a, zz, yy, quad ^ (1 + 2 * hop), hop).wait_recv()

        others(group, range(lines), body)

    def settle(group):
        def body(zz, yy):
            for a in arrays(group):
                for hop in range(1 + items[a][3]):
                    c_copy(a, zz, yy, quad ^ (2 * hop), hop).wait_send()
                if items[a][3]:
                    x_copy(a, zz, yy, quad).wait_send()

        others(group, range(lines), body)
        for side in range(2):
            for k in range(lines):
                zz = z - k if side == 0 else z + k

                @pl.when(z_has[side] & (zz >= 0) & (zz < lines))
                def _():
                    for a in arrays(group):
                        z_copy(a, zz, side).wait_send()

    z_begin(0)
    for side in range(2):
        y_start(z, y, side, True)
    before()
    for k in range(1, lines):
        z_step(0, k)
    z_begin(1)
    for m in range(1, wide):
        for side in range(2):
            yy = y - m if side == 0 else y + m

            @pl.when((yy >= 0) if side == 0 else (yy < wide))
            def _():
                for zz in range(lines):
                    for a in arrays(0):
                        y_copy(a, zz, yy, side).wait_recv()
                    if m < wide - 1:
                        y_start(zz, yy, side)
                    for a in arrays(0):
                        spread(a, zz, yy)
    z_step(1, 1)
    for zz in range(lines):
        pass_on(0, [zz])
        if zz == lines // 2:
            z_step(1, 2)
    arrived(0)
    for c in local:
        c.wait()
    @pl.loop(0, n_tensor)
    def _(p):
        work(p)
        for k in range(3, lines):
            when(p == k - 2, functools.partial(z_step, 1, k))

    after()
    share()
    for zz in range(lines):
        pass_on(1, [zz])
    share_end()
    arrived(1)
    settle(0)
    settle(1)
    for side in range(2):
        @pl.when(y_has[side])
        def _():
            for zz in range(lines):
                for m in range(wide):
                    yy = y - m if side == 0 else y + m

                    @pl.when((yy >= 0) if side == 0 else (yy < wide))
                    def _():
                        for a in arrays(0):
                            y_copy(a, zz, yy, side).wait_send()


def front(n_tensor, attn, mlp, slopes, segments, tokens, rows):
    lines, wide = grid_of(n_tensor)
    n = len(attn) + len(mlp)
    arrays = list(attn) + list(mlp)
    d = tokens.shape[1]
    chunk, span = tokens.shape[0] // n_tensor, segments.shape[1]
    lanes = attn[0].shape[1] // 3
    shape, low, f32 = jax.ShapeDtypeStruct, jnp.bfloat16, jnp.float32
    outs = [shape(((n_tensor if i < len(attn) else lines),) + a.shape, a.dtype) for i, a in enumerate(arrays)]
    outs += [
        shape((n_tensor, chunk, lanes), low), shape((n_tensor, span, lanes), low), shape((n_tensor, span, lanes), low),
        shape((n_tensor, chunk, lanes), low), shape((chunk, d), f32), shape((wide, chunk, d), low), shape((d, span), low),
    ]
    dma = pltpu.SemaphoreType.DMA
    return pl.pallas_call(
        functools.partial(front_kernel, n_tensor, slopes.shape[0] // n_tensor, len(attn), len(mlp)),
        out_shape=outs,
        in_specs=[VM] * n + [pl.BlockSpec(memory_space=pltpu.SMEM), VM, ANY] + [VM] * len(rows),
        out_specs=[VM] * len(attn) + [ANY] * len(mlp) + [VM] * front_outputs,
        scratch_shapes=[dma((2, 2 * n, lines))] * 2
        + [dma((2, 2 * n, lines, wide))] * 2
        + [dma((2 * n, lines, wide))] * 2
        + [dma((2, 2 * n, lines, wide))] * 2
        + [dma((n,))]
        + [pltpu.VMEM((chunk, span), f32)] + [pltpu.VMEM((span, d), low)] * 2 + [dma((span // chunk,)), dma((wide,)), dma((wide,))],
        compiler_params=pltpu.CompilerParams(collective_id=0, has_side_effects=True, vmem_limit_bytes=60 * 2**20),
        name="front",
    )(*arrays, slopes, segments, tokens, *rows)


def add_rows(dst, terms):
    rows = dst.shape[0]
    step = 32 if rows % 32 == 0 else rows

    @pl.loop(0, rows // step)
    def _(i):
        part = pl.ds(pl.multiple_of(i * step, step), step)
        total = terms[0][part].astype(jnp.float32)
        for term in terms[1:]:
            total = total + term[part].astype(jnp.float32)
        dst[part] = total.astype(dst.dtype)


def pair_sums(n_tensor, terms, sums, from_c, to_x, from_x, c_send, c_recv, x_send, x_recv, held=()):
    dp, t, z, y = where_am_i(n_tensor)
    quad = dp % 4
    side_x, core = quad // 2, quad % 2
    arrays = range(len(terms))

    def quarter(a, s, q):
        rows = terms[a].shape[1] // 4
        return terms[a].at[s, pl.ds(pl.multiple_of(q * rows, rows), rows)]

    def c_copy(a, s, h):
        return remote(
            quarter(a, s, h * 2 + 1 - core), from_c[a].at[s, h], c_send.at[a, s, h], c_recv.at[a, s, h], (dp ^ 1, t)
        )

    def x_copy(a, s):
        return remote(to_x[a].at[s], from_x[a].at[s], x_send.at[a, s], x_recv.at[a, s], (dp ^ 2, t))

    def start(s):
        for a in arrays:
            for h in range(2):
                c_copy(a, s, h).start()

    def core_stage(s):
        for a in arrays:
            for h in range(2):
                c_copy(a, s, h).wait_recv()
            add_rows(to_x[a].at[s], [quarter(a, s, (1 - side_x) * 2 + core), from_c[a].at[s, 1 - side_x]])
            if a not in held:
                x_copy(a, s).start()
            add_rows(sums[a].at[s], [quarter(a, s, quad), from_c[a].at[s, side_x]])

    def x_stage(s):
        for a in [a for a in arrays if a not in held]:
            x_copy(a, s).wait_recv()
            add_rows(sums[a].at[s], [sums[a].at[s], from_x[a].at[s]])

    def settle(s):
        for a in arrays:
            for h in range(2):
                c_copy(a, s, h).wait_send()
            if a not in held:
                x_copy(a, s).wait_send()

    return start, core_stage, x_stage, settle


def pair_scratch(shapes, slots):
    low, dma = jnp.bfloat16, pltpu.SemaphoreType.DMA
    n = len(shapes)
    quarters = [(r // 4, c) for r, c in shapes]
    return (
        [pltpu.VMEM((slots, 2) + q, low) for q in quarters]
        + [pltpu.VMEM((slots,) + q, low) for q in quarters] * 2
        + [dma((n, slots, 2))] * 2 + [dma((n, slots))] * 2
    )


def doubling_peers(n_tensor):
    dp, t, z, y = where_am_i(n_tensor)
    bits = lambda size: [1 << i for i in range((size - 1).bit_length())]
    return [(dp ^ b, t) for b in bits(lax.axis_size("dp"))] + [(dp, t ^ b) for b in bits(n_tensor)]


def doubling_program(n_tensor, own, out, total, got, send, recv):
    peers = doubling_peers(n_tensor)

    def step(i):
        return remote(total.at[i], got.at[i], send.at[i], recv.at[i], peers[i])

    def begin():
        total[0] = own[...]
        step(0).start()

    def advance(i):
        step(i).wait_recv()
        if i + 1 < len(peers):
            total[i + 1] = total[i] + got[i]
            step(i + 1).start()
        else:
            out[...] = total[i] + got[i]

    def settle():
        for i in range(len(peers)):
            step(i).wait_send()

    return [begin] + [functools.partial(advance, i) for i in range(len(peers))] + [settle]


def finish_kernel(n_tensor, n_attn, n_mlp, with_vectors, pull, *refs):
    lines, wide = grid_of(n_tensor)
    dp, t, z, y = where_am_i(n_tensor)
    n = n_attn + n_mlp
    refs = list(refs)

    def take(count):
        got, refs[:] = refs[:count], refs[count:]
        return got

    terms, rows_own = take(n), take(1)
    vec_own = take(1)[0] if with_vectors else None
    pull_in = take(pull_inputs) if pull else []
    final, rows_full = take(n), take(1)
    vec_out = take(1)[0] if with_vectors else None
    pull_out = take(pull_outputs) if pull else []
    acc, from_y, from_z, whole = (take(n) for i in range(4))
    y_send, y_recv, z_send, z_recv, q_send, q_recv = take(6)
    rows_steps = rows_program(n_tensor, rows_own, rows_full, *take(5))
    vec_steps = doubling_program(n_tensor, vec_own, vec_out, *take(4)) if with_vectors else []
    if pull:
        pull_prepare, work, pull_peers, pull_first, pull_last = pull_program(n_tensor, pull, pull_in, pull_out, refs)
    quad = dp % 4
    core_peer, x_peer = (dp ^ 1, t), (dp ^ 2, t)
    lines_order = [i // 2 if i % 2 else lines - 1 - i // 2 for i in range(lines)]
    attn, mlp, order = list(range(n_attn)), list(range(n_attn, n)), list(range(n))

    def index(a, zz, yy):
        return zz * wide + yy if a < n_attn else zz

    def quarter(ref, q):
        rows = ref.shape[0] // 4
        return ref.at[pl.ds(pl.multiple_of(q * rows, rows), rows)]

    def y_copy(a, zz, yy, side):
        peer = ((dp, t + 1), (dp, t - 1))[side]
        lane = zz * wide + yy
        return remote(acc[a].at[lane], from_y[a].at[side, lane], y_send.at[side, a, lane], y_recv.at[side, a, lane], peer)

    def z_copy(a, zz, side):
        peer = ((dp, t + wide), (dp, t - wide))[side]
        return remote(
            acc[a].at[index(a, zz, y)], from_z[a].at[side, zz], z_send.at[side, a, zz], z_recv.at[side, a, zz], peer
        )

    def y_begin(zz):
        for m in range(wide):
            yy = (y + 1 + m) % wide
            for a in attn:
                lane = zz * wide + yy
                add_rows(acc[a].at[lane], [terms[a].at[lane]])
                when((y == 0) & (yy > y), lambda: y_copy(a, zz, yy, 0).start())
                when((y == wide - 1) & (yy < y), lambda: y_copy(a, zz, yy, 1).start())

    def y_stage(zz):
        for a in attn:
            for k in range(wide):
                for side, yy in ((0, wide - 1 - k), (1, k)):
                    @pl.when(((yy >= y) & (y > 0)) if side == 0 else ((yy <= y) & (y < wide - 1)))
                    def _():
                        lane = zz * wide + yy
                        y_copy(a, zz, yy, side).wait_recv()
                        add_rows(acc[a].at[lane], [acc[a].at[lane], from_y[a].at[side, lane]])
                        when(yy != y, lambda: y_copy(a, zz, yy, side).start())

    def z_round(r, chosen):
        for side in range(2):
            zz = lines - 1 - r + z if side == 0 else z - (lines - 1 - r)

            @pl.when((zz < lines) & (zz >= 0))
            def _():
                @pl.when((z > 0) if side == 0 else (z < lines - 1))
                def _():
                    for a in chosen:
                        s = index(a, zz, y)
                        z_copy(a, zz, side).wait_recv()
                        add_rows(acc[a].at[s], [acc[a].at[s], from_z[a].at[side, zz]])

                if r < lines - 1:
                    for a in chosen:
                        z_copy(a, zz, side).start()

    def q_copy(a, q, hop, peer):
        return remote(quarter(whole[a], q), quarter(whole[a], q), q_send.at[hop, a], q_recv.at[hop, a], peer)

    def home(a):
        add_rows(quarter(whole[a], quad), [acc[a].at[index(a, z, y)]])
        q_copy(a, quad, 0, x_peer).start()
        q_copy(a, quad, 1, core_peer).start()

    def widen(a, q):
        add_rows(quarter(final[a], q), [quarter(whole[a], q)])

    def aside():
        if len(rows_steps) > 1:
            rows_steps.pop(0)()
        if len(vec_steps) > 1:
            vec_steps.pop(0)()

    def late(r):
        aside()
        if r == 1:
            z_round(1, mlp)
            z_round(0, attn)
        else:
            z_round(r, mlp)
            z_round(r - 1, attn)

    peers = neighbours(n_tensor)
    if pull:
        peers += pull_peers
    if with_vectors:
        peers += [(dp >= 0, peer) for peer in doubling_peers(n_tensor)]
    greet(peers)
    for zz in lines_order:
        y_begin(zz)
        for a in order[n_attn:]:
            add_rows(acc[a].at[zz], [terms[a].at[zz]])
    z_round(0, mlp)
    rows_steps.pop(0)()
    if with_vectors:
        vec_steps.pop(0)()
    if attn:
        for zz in lines_order:
            y_stage(zz)
            if with_vectors:
                vec_steps.pop(0)()
    steps = [functools.partial(late, r) for r in range(1, lines)]
    if pull:
        pull_prepare()

        @pl.loop(0, n_tensor)
        def _(p):
            work(p)
            for k in (n_tensor // 2, n_tensor - 1):
                when(p == k, steps.pop(0))

        pull_first()
    for step in steps:
        step()
    for a in mlp:
        home(a)
    z_round(lines - 1, attn)
    for a in attn:
        home(a)
    aside()
    for a in mlp + attn:
        widen(a, quad)
        q_copy(a, quad ^ 2, 0, x_peer).wait_recv()
        q_copy(a, quad ^ 2, 2, core_peer).start()
        widen(a, quad ^ 2)
    if pull:
        pull_last()
    while rows_steps:
        rows_steps.pop(0)()
    while vec_steps:
        vec_steps.pop(0)()
    for a in order:
        q_copy(a, quad ^ 1, 1, core_peer).wait_recv()
        widen(a, quad ^ 1)
        q_copy(a, quad ^ 3, 2, core_peer).wait_recv()
        widen(a, quad ^ 3)
        q_copy(a, quad, 0, x_peer).wait_send()
        q_copy(a, quad, 1, core_peer).wait_send()
        q_copy(a, quad ^ 2, 2, core_peer).wait_send()
        if a < n_attn:
            for zz in range(lines):
                for yy in range(wide):
                    when(yy > y, lambda: y_copy(a, zz, yy, 0).wait_send())
                    when(yy < y, lambda: y_copy(a, zz, yy, 1).wait_send())
        for zz in range(lines):
            when(zz > z, lambda: z_copy(a, zz, 0).wait_send())
            when(zz < z, lambda: z_copy(a, zz, 1).wait_send())


def finish(n_tensor, attn, mlp, rows, vectors, cid, name, pull=None):
    lines, wide = grid_of(n_tensor)
    arrays = list(attn) + list(mlp)
    n = len(arrays)
    vm, dma = pltpu.VMEM, pltpu.SemaphoreType.DMA
    low, f32 = jnp.bfloat16, jnp.float32
    quarters = [a.shape[1:] for a in arrays]
    each = lambda lead: [vm(lead(a, i) + q, low) for i, (a, q) in enumerate(zip(arrays, quarters))]
    steps = (lax.axis_size("dp") - 1).bit_length() + (n_tensor - 1).bit_length()
    scratch = (
        each(lambda a, i: (a.shape[0],))
        + each(lambda a, i: (2, n_tensor) if i < len(attn) else (1, 1))
        + each(lambda a, i: (2, lines))
        + [vm((4 * q[0], q[1]), low) for q in quarters]
    )
    sems = (
        [dma((2, max(1, len(attn)), n_tensor))] * 2 + [dma((2, n, lines))] * 2 + [dma((3, n))] * 2
        + [dma((2, 1, lines))] * 2 + [dma((2, 1, lines, wide))] * 2 + [dma((1,))]
    )
    inputs, in_specs = arrays + [rows], [VM] * n + [VM]
    out_shape = [jax.ShapeDtypeStruct((4 * q[0], q[1]), f32) for q in quarters]
    out_shape.append(jax.ShapeDtypeStruct((n_tensor,) + rows.shape, low))
    out_specs = [VM] * n + [ANY]
    if vectors is not None:
        inputs, in_specs = inputs + [vectors], in_specs + [VM]
        out_shape.append(jax.ShapeDtypeStruct(vectors.shape, vectors.dtype))
        out_specs.append(VM)
        sems += [vm((steps,) + vectors.shape, jnp.float32)] * 2 + [dma((steps,))] * 2
    heads = 0
    if pull is not None:
        heads = pull[0].shape[0] // n_tensor
        inputs, in_specs = inputs + list(pull), in_specs + [pl.BlockSpec(memory_space=pltpu.SMEM)] + [VM] * (pull_inputs - 3) + [ANY, VM]
        shapes, more = pull_shapes(n_tensor, pull)
        out_shape += shapes
        out_specs += [VM] * pull_outputs
        sems += more
    out = pl.pallas_call(
        functools.partial(
            finish_kernel, n_tensor, len(attn), len(mlp), vectors is not None, heads
        ),
        out_shape=out_shape,
        in_specs=in_specs,
        out_specs=out_specs,
        scratch_shapes=scratch + sems,
        compiler_params=pltpu.CompilerParams(collective_id=cid, has_side_effects=True, vmem_limit_bytes=63 * 2**20),
        name=name,
    )(*inputs)
    sums = out[:n]
    if lax.axis_size("dp") > 4:
        sums = [lax.psum(s, "dp") * 0.25 for s in sums]
    return list(sums) + list(out[n:])


def mlp_kernel(n_tensor, *refs):
    lines, wide = grid_of(n_tensor)
    dp, t, z, y = where_am_i(n_tensor)
    second, cot_all, up, down, bias, middle, gain2, down_bias = refs[:8]
    sum_up, sum_down, up_sum, grad_middle, grad_low, output, columns, give_up = refs[8:16]
    terms_up, terms_down = refs[16:18]
    pair, (feed, grad, second_t, share_own, share_got, grad_second, cot) = refs[18:28], refs[28:35]
    s_send, s_recv, l_sem = refs[35:]
    sums, terms = (sum_up, sum_down), (terms_up, terms_down)
    pair_start, core_stage, x_stage, pair_settle = pair_sums(
        n_tensor, terms, sums, pair[0:2], (give_up, pair[3]), pair[4:6], *pair[6:], held=(0,)
    )
    low, f32 = jnp.bfloat16, jnp.float32
    chunk = output.shape[0]
    tile = min(128, chunk)

    def share(kind, yy, slot):
        return remote(
            share_own.at[kind, yy], share_got.at[kind, slot], s_send.at[kind, yy], s_recv.at[kind, slot],
            (dp, z * wide + yy),
        )

    peers = [(dp >= 0, (dp ^ 1, t)), (dp >= 0, (dp ^ 2, t))]
    peers += [(yy != y, (dp, z * wide + yy)) for yy in range(wide)]
    count = second.shape[0]
    load = pltpu.make_async_copy(cot_all.at[pl.ds(pl.multiple_of(z * count, count), count)], cot, l_sem)
    load.start()
    greet(peers)
    feed[...] = jnp.zeros(feed.shape, f32)
    grad[...] = jnp.zeros(grad.shape, f32)

    @pl.loop(0, second.shape[0] // tile)
    def _(i):
        here = pl.ds(pl.multiple_of(i * tile, tile), tile)
        second_t[:, here] = second[here].T

    load.wait()

    @pl.loop(0, lines)
    def _(s):
        upper = dot(second[...], up[s], NN) + bias[s, 0:1]
        hidden, slope = gelu_and_slope(upper)
        hidden = hidden.astype(low)
        grad_upper = (dot(cot[...], down[s], NT) * slope).astype(low)
        up_sum[s] = jnp.broadcast_to(jnp.sum(grad_upper.astype(f32), axis=0, keepdims=True), up_sum.shape[1:])
        terms_down[s] = dot(hidden, cot[...], TN).astype(low)
        terms_up[s] = dot(second_t[...], grad_upper, NN).astype(low)
        pair_start(s)
        feed[...] += dot(hidden, down[s], NN)
        grad[...] += dot(grad_upper, up[s], NT)
        when(s >= 1, lambda: core_stage(jnp.maximum(s - 1, 0)))

    for kind, whole in ((0, grad), (1, feed)):
        for yy in range(wide):
            @pl.when(yy != y)
            def _():
                add_rows(share_own.at[kind, yy], [whole.at[pl.ds(yy * chunk, chunk)]])
                share(kind, yy, y).start()
    core_stage(lines - 1)

    def collect(kind, whole, out, more):
        share_got[kind, y] = jnp.zeros((chunk, second.shape[1]), low)
        for yy in range(wide):
            when(yy != y, lambda: share(kind, yy, yy).wait_recv())
        mine = whole.at[pl.ds(pl.multiple_of(y * chunk, chunk), chunk)]
        add_rows(out, [mine] + [share_got.at[kind, yy] for yy in range(wide)] + more)

    for s in range(lines // 2):
        x_stage(s)
    collect(0, grad, grad_second, [])
    columns[...] = jnp.zeros(columns.shape, f32)

    @pl.loop(0, chunk // tile)
    def _(i):
        here = pl.ds(pl.multiple_of(i * tile, tile), tile)
        mine = cot[pl.ds(pl.multiple_of(y * chunk + i * tile, tile), tile)].astype(f32)
        xhat, rate = normalized(middle[here])
        got = grad_second[here]
        total = mine + norm_input_term(xhat, rate, as_row(gain2), got)
        grad_middle[here] = total
        grad_low[here] = total.astype(low)
        for j, term in enumerate((got * xhat, got, total, mine)):
            columns[j : j + 1] += jnp.sum(term, axis=0, keepdims=True)
        feed[pl.ds(pl.multiple_of(y * chunk + i * tile, tile), tile)] += middle[here] + as_row(down_bias)

    for s in range(lines // 2, lines - 1):
        x_stage(s)
    collect(1, feed, output, [])
    x_stage(lines - 1)
    for yy in range(wide):
        for kind in range(2):
            when(yy != y, lambda: share(kind, yy, y).wait_send())
    for s in range(lines):
        pair_settle(s)


def mlp(n_tensor, second, cot, up, down, bias, middle, gain2, down_bias):
    lines, wide = grid_of(n_tensor)
    shape, vm, dma = jax.ShapeDtypeStruct, pltpu.VMEM, pltpu.SemaphoreType.DMA
    low, f32 = jnp.bfloat16, jnp.float32
    d, hidden = up.shape[1:]
    chunk = middle.shape[0]
    quarters = [(d // 4, hidden), (hidden // 4, d)]
    return pl.pallas_call(
        functools.partial(mlp_kernel, n_tensor),
        out_shape=[shape((lines,) + q, low) for q in quarters]
        + [shape((lines, 8, hidden), f32), shape((chunk, d), f32), shape((chunk, d), low), shape((chunk, d), low), shape((8, d), f32),
           shape((lines,) + quarters[0], low)],
        in_specs=[VM, ANY] + [VM] * 6,
        out_specs=[VM] * 8,
        scratch_shapes=[vm(up.shape, low), vm(down.shape, low)] + pair_scratch([up.shape[1:], down.shape[1:]], lines)
        + [vm(second.shape, f32)] * 2 + [vm((d, second.shape[0]), low)] + [vm((2, wide, chunk, d), low)] * 2
        + [vm((chunk, d), f32), vm(second.shape, low)] + [dma((2, wide))] * 2 + [dma],
        compiler_params=pltpu.CompilerParams(collective_id=3, has_side_effects=True, vmem_limit_bytes=60 * 2**20),
        name="mlp",
    )(second, cot, up, down, bias, middle, gain2, down_bias)


def rows_program(n_tensor, own, full, z_send, z_recv, y_send, y_recv, l_sem):
    lines, wide = grid_of(n_tensor)
    dp, t, z, y = where_am_i(n_tensor)
    n = len(own)

    def z_copy(a, zz, side, mine=False):
        dst = full[a].at[zz * wide + y]
        peer = ((dp, t + wide), (dp, t - wide))[side]
        return remote(own[a] if mine else dst, dst, z_send.at[side, a, zz], z_recv.at[side, a, zz], peer)

    def y_copy(a, zz, yy, side, mine=False):
        dst = full[a].at[zz * wide + yy]
        peer = ((dp, t + 1), (dp, t - 1))[side]
        return remote(own[a] if mine else dst, dst, y_send.at[side, a, zz, yy], y_recv.at[side, a, zz, yy], peer)

    z_has = ((z < lines - 1), (z > 0))
    y_has = ((y < wide - 1), (y > 0))
    local = [pltpu.make_async_copy(own[a], full[a].at[t], l_sem.at[a]) for a in range(n)]

    def begin():
        for side in range(2):
            for a in range(n):
                when(z_has[side], lambda: z_copy(a, z, side, True).start())
                when(y_has[side], lambda: y_copy(a, z, y, side, True).start())
        for c in local:
            c.start()

    def along_z(k):
        for side in range(2):
            zz = z - k if side == 0 else z + k

            @pl.when((zz >= 0) & (zz < lines))
            def _():
                for a in range(n):
                    z_copy(a, zz, side).wait_recv()
                    when(z_has[side], lambda: z_copy(a, zz, side).start())
                    for s in range(2):
                        when(y_has[s], lambda: y_copy(a, zz, y, s).start())

    def along_y(m):
        for side in range(2):
            yy = y - m if side == 0 else y + m

            @pl.when((yy >= 0) & (yy < wide))
            def _():
                for zz in range(lines):
                    for a in range(n):
                        y_copy(a, zz, yy, side).wait_recv()
                        if m < wide - 1:
                            when(y_has[side], lambda: y_copy(a, zz, yy, side).start())

    def settle():
        for side in range(2):
            for k in range(lines):
                zz = z - k if side == 0 else z + k

                @pl.when(z_has[side] & (zz >= 0) & (zz < lines))
                def _():
                    for a in range(n):
                        z_copy(a, zz, side).wait_send()
            for m in range(wide):
                yy = y - m if side == 0 else y + m

                @pl.when(y_has[side] & (yy >= 0) & (yy < wide))
                def _():
                    for zz in range(lines):
                        for a in range(n):
                            y_copy(a, zz, yy, side).wait_send()
        for c in local:
            c.wait()

    return (
        [begin]
        + [functools.partial(along_z, k) for k in range(1, lines)]
        + [functools.partial(along_y, m) for m in range(1, wide)]
        + [settle]
    )


def dot(a, b, contract, **kwargs):
    return lax.dot_general(a, b, (contract, ((), ())), preferred_element_type=jnp.float32, **kwargs)


NN, NT, TN = ((1,), (0,)), ((1,), (1,)), ((0,), (0,))


def head_of_lane(shape, heads):
    return lax.broadcasted_iota(jnp.int32, shape, 1) // (shape[1] // heads)


def attend(heads, slope_of, dist, query, keys, values):
    scale = 1.0 / math.sqrt(query.shape[1] // heads)
    head = head_of_lane(query.shape, heads)
    out = jnp.zeros(query.shape, jnp.float32)
    for h in range(heads):
        masked = jnp.where(head == h, query * jnp.bfloat16(scale), jnp.bfloat16(0))
        scores = dot(masked, keys, NT) - slope_of(h) * dist[...]
        peak = jnp.max(scores, axis=1, keepdims=True)
        expo = jnp.exp(scores - peak)
        total = jnp.sum(expo, axis=1, keepdims=True)
        part = dot(expo.astype(jnp.bfloat16), values, NN) / total
        out = jnp.where(head == h, part, out)
    return out.astype(jnp.bfloat16)


front_inputs, front_outputs = 8, 7


def column_of(row):
    return jnp.broadcast_to(row.astype(jnp.float32), (128, row.shape[1])).T[:, 0:1].astype(jnp.int32)


def masked_distance(left, top, left_start, top_start):
    shape = (left.shape[0], top.shape[1])
    down = left_start + lax.broadcasted_iota(jnp.int32, shape, 0)
    across = top_start + lax.broadcasted_iota(jnp.int32, shape, 1)
    far = down - across if left_start else across - down
    return jnp.where((left == top) & (far >= 0), far.astype(jnp.float32), far_off)


def front_program(n_tensor, heads, ins, weights, outs, scratch):
    lines, wide = grid_of(n_tensor)
    dp, t, z, y = where_am_i(n_tensor)
    slopes, segments, tokens, *rows = ins
    qkv_all, out_all, small_all = weights
    q, k, v, context, middle, second, normed_t = outs
    dist, near, normed, l_sem, s_send, s_recv = scratch
    chunk, lanes = q.shape[1:]
    span, d = near.shape
    behind = span - chunk
    low, f32 = jnp.bfloat16, jnp.float32
    tile = min(128, chunk)

    def row(i):
        return as_row(rows[i])

    def before():
        loads = [
            pltpu.make_async_copy(
                tokens.at[pl.ds(pl.multiple_of(jnp.maximum(t - behind // chunk + j, 0) * chunk, chunk), chunk)],
                near.at[pl.ds(j * chunk, chunk)], l_sem.at[j],
            )
            for j in range(span // chunk)
        ]
        for load in loads:
            load.start()
        own = column_of(segments[0:1, behind:])
        dist[...] = masked_distance(own, segments[0:1, :], behind, 0)
        for load in loads:
            load.wait()

        @pl.loop(0, span // tile)
        def _(i):
            here = pl.ds(pl.multiple_of(i * tile, tile), tile)
            xhat, rate = normalized(near[here].astype(f32))
            value = (xhat * row(0) + row(1)).astype(low)
            normed[here] = value
            normed_t[:, here] = value.T

    def work(p):
        bias = small_all[p, 0:16, :].astype(f32)
        query = (dot(normed[behind:], qkv_all[p, :, :lanes], NN) + bias[0:1, :lanes]).astype(low)
        both = dot(normed[...], qkv_all[p, :, lanes:], NN)
        keys = both[:, :lanes].astype(low)
        values = (both[:, lanes:] + bias[1:2, :lanes]).astype(low)
        q[p], k[p], v[p] = query, keys, values
        context[p] = attend(heads, lambda h: slopes[p * heads + h], dist, query, keys, values)

    def after():
        @pl.loop(0, chunk // tile)
        def _(i):
            start = pl.multiple_of(i * tile, tile)
            here = pl.ds(start, tile)
            total = near[pl.ds(behind + start, tile)].astype(f32) + row(4)
            for p in range(n_tensor):
                total = total + dot(context[p, here], out_all[p], NN)
            middle[here] = total
            xhat, rate = normalized(total)
            second[y, here] = (xhat * row(2) + row(3)).astype(low)

    def step(yy, slot):
        return remote(second.at[slot], second.at[slot], s_send.at[yy], s_recv.at[slot], (dp, z * wide + yy))

    def share():
        for yy in range(wide):
            when(yy != y, lambda: step(yy, y).start())

    def share_end():
        for yy in range(wide):
            @pl.when(yy != y)
            def _():
                step(yy, yy).wait_recv()
                step(yy, y).wait_send()

    return before, work, after, share, share_end


def pull_scores(heads, slope_of, dist, query, keys, values, grad):
    lanes = query.shape[1]
    scale = 1.0 / math.sqrt(lanes // heads)
    head = head_of_lane(query.shape, heads)
    head_rows = lax.broadcasted_iota(jnp.int32, (lanes, query.shape[0]), 0) // (lanes // heads)
    low = jnp.bfloat16
    grad_q = jnp.zeros((lanes, query.shape[0]), jnp.float32)
    grad_k = jnp.zeros(keys.shape, jnp.float32)
    grad_v = jnp.zeros(keys.shape, jnp.float32)
    for h in range(heads):
        masked = jnp.where(head == h, query * low(scale), low(0))
        masked_grad = jnp.where(head == h, grad, low(0))
        scores = dot(keys, masked, NT) - slope_of(h) * dist[...]
        peak = jnp.max(scores, axis=0, keepdims=True)
        expo = jnp.exp(scores - peak)
        probs = expo * (1.0 / jnp.sum(expo, axis=0, keepdims=True))
        grad_probs = dot(values, masked_grad, NT)
        inner = jnp.sum(probs * grad_probs, axis=0, keepdims=True)
        grad_scores = (probs * (grad_probs - inner)).astype(low)
        grad_v = grad_v + dot(probs.astype(low), masked_grad, NN)
        grad_k = grad_k + dot(grad_scores, masked, NN)
        grad_q = jnp.where(head_rows == h, dot(keys, grad_scores, TN), grad_q)
    return (jnp.transpose(grad_q) * scale).astype(low), grad_k.astype(low), grad_v.astype(low)


pull_inputs, pull_outputs = 15, 7


def pull_shapes(n_tensor, pull):
    slopes, segments, q, k, v, grad, context, out_all, qkv_all, normed_t, grad_middle, keep_up, give_up, tokens, gain1 = pull
    span, chunk, lanes, d = k.shape[1], q.shape[1], q.shape[2], normed_t.shape[0]
    halo = (span - chunk) // chunk
    low, f32 = jnp.bfloat16, jnp.float32
    shape = jax.ShapeDtypeStruct
    vm, dma = pltpu.VMEM, pltpu.SemaphoreType.DMA
    outs = [
        shape((n_tensor, d // 4, 3 * lanes), low), shape((n_tensor, lanes // 4, d), low), shape((chunk, d), low), shape((8, d), f32),
        shape((n_tensor, 8, lanes), f32), shape((n_tensor, 8, lanes), f32), shape(keep_up.shape, low),
    ]
    scratch = [vm(qkv_all.shape, low), vm(out_all.shape, low)]
    scratch += pair_scratch([qkv_all.shape[1:], out_all.shape[1:]], n_tensor) + [
        vm(q.shape, low), vm((n_tensor, span, 2 * lanes), low), vm((halo, chunk, d), low), vm((halo, chunk, d), low),
        dma((halo,)), dma((halo,)), vm((chunk, d), f32), vm((chunk, d), low), dma, vm((span, chunk), f32),
        vm(keep_up.shape, low), dma((keep_up.shape[0],)), dma((keep_up.shape[0],)),
    ]
    return outs, scratch


def pull_program(n_tensor, heads, ins, outs, scratch):
    dp, t, z, y = where_am_i(n_tensor)
    slopes, segments, q, k, v, grad, context, out_all, qkv_all, normed_t, grad_middle, keep_up, give_up, tokens, gain1 = ins
    sum_qkv, sum_out, grad_tokens, columns, q_sum, v_sum, sum_up = outs
    (grad_qkv, grad_out), pair = scratch[:2], scratch[2:12]
    grad_q, grad_kv, halo_own, halo_got, h_send, h_recv, first, mine, l_sem, dist, got_up, u_send, u_recv = scratch[12:]
    pair_start, core_stage, x_stage, pair_settle = pair_sums(
        n_tensor, (grad_qkv, grad_out), (sum_qkv, sum_out), pair[0:2], pair[2:4], pair[4:6], *pair[6:]
    )
    halo, chunk, d = halo_own.shape
    span, lanes = k.shape[1], q.shape[2]
    behind = span - chunk
    low, f32 = jnp.bfloat16, jnp.float32

    def up_copy(s):
        return remote(give_up.at[s], got_up.at[s], u_send.at[s], u_recv.at[s], (dp ^ 2, t))

    def prepare():
        for s in range(give_up.shape[0]):
            up_copy(s).start()
        dist[...] = masked_distance(column_of(segments[0:1, :]), segments[0:1, behind:], 0, behind)

    def work(p):
        grad_context = dot(grad[...], out_all[p], NT).astype(low)
        grad_out[p] = dot(context[p], grad[...], TN).astype(low)
        gq, gk, gv = pull_scores(heads, lambda h: slopes[p * heads + h], dist, q[p], k[p], v[p], grad_context)
        grad_q[p] = gq
        grad_kv[p, :, :lanes] = gk
        grad_kv[p, :, lanes:] = gv
        q_sum[p] = jnp.broadcast_to(jnp.sum(gq.astype(f32), axis=0, keepdims=True), (8, lanes))
        v_sum[p] = jnp.broadcast_to(jnp.sum(gv.astype(f32), axis=0, keepdims=True), (8, lanes))
        grad_qkv[p, :, :lanes] = dot(normed_t[:, behind:], gq, NN).astype(low)
        grad_qkv[p, :, lanes:] = dot(normed_t[...], grad_kv[p], NN).astype(low)
        pair_start(p)
        when(p >= 1, lambda: core_stage(jnp.maximum(p - 1, 0)))

    def step(m):
        return remote(halo_own.at[halo - 1 - m], halo_got.at[m], h_send.at[m], h_recv.at[m], (dp, t - 1 - m))

    ahead = [(t + 1 + m < n_tensor, (dp, t + 1 + m)) for m in range(halo)]
    back = [(t - 1 - m >= 0, (dp, t - 1 - m)) for m in range(halo)]
    tile = min(128, chunk)

    load = pltpu.make_async_copy(tokens.at[pl.ds(pl.multiple_of(t * chunk, chunk), chunk)], mine, l_sem)

    def rows_first():
        load.start()
        core_stage(n_tensor - 1)
        for j in range(halo):
            @pl.loop(0, chunk // tile)
            def _(i):
                here = pl.multiple_of(i * tile, tile)
                total = jnp.zeros((tile, d), f32)
                for p in range(n_tensor):
                    total = total + dot(grad_kv[p, pl.ds(j * chunk + here, tile)], qkv_all[p, :, lanes:], NT)
                halo_own[j, pl.ds(here, tile)] = total.astype(low)

        for m in range(halo):
            when(back[m][0], lambda: step(m).start())

        @pl.loop(0, chunk // tile)
        def _(i):
            here = pl.multiple_of(i * tile, tile)
            total = jnp.zeros((tile, d), f32)
            for p in range(n_tensor):
                total = total + dot(grad_kv[p, pl.ds(behind + here, tile)], qkv_all[p, :, lanes:], NT)
                total = total + dot(grad_q[p, pl.ds(here, tile)], qkv_all[p, :, :lanes], NT)
            first[pl.ds(here, tile)] = total

    def rows_last():
        for m in range(halo):
            @pl.when(ahead[m][0])
            def _():
                step(m).wait_recv()
                add_rows(first, [first, halo_got.at[m]])

            when(back[m][0], lambda: step(m).wait_send())

        load.wait()
        columns[...] = jnp.zeros(columns.shape, f32)

        @pl.loop(0, chunk // tile)
        def _(i):
            here = pl.ds(pl.multiple_of(i * tile, tile), tile)
            xhat, rate = normalized(mine[here].astype(f32))
            got = first[here]
            grad_tokens[here] = (grad_middle[here] + norm_input_term(xhat, rate, as_row(gain1), got)).astype(low)
            for j, term in enumerate((got * xhat, got)):
                columns[j : j + 1] += jnp.sum(term, axis=0, keepdims=True)

        for s in range(give_up.shape[0]):
            up_copy(s).wait_recv()
            add_rows(sum_up.at[s], [keep_up.at[s], got_up.at[s]])
            up_copy(s).wait_send()

        @pl.loop(0, n_tensor)
        def _(p):
            x_stage(p)
            pair_settle(p)

    return prepare, work, ahead + back, rows_first, rows_last


norm_eps = 1e-05


def normalized(values):
    offset = values - jnp.mean(values, axis=-1, keepdims=True)
    rate = lax.rsqrt(jnp.mean(offset * offset, axis=-1, keepdims=True) + norm_eps)
    return offset * rate, rate


def norm_input_term(xhat, rate, gain, grad):
    e = grad * gain
    return rate * (e - jnp.mean(e, axis=-1, keepdims=True) - xhat * jnp.mean(e * xhat, axis=-1, keepdims=True))


def gelu_and_slope(u):
    c, a = 0.7978845608028654, 0.044715
    th = jnp.tanh(c * (u + a * u * u * u))
    slope = 0.5 * (1.0 + th) + 0.5 * u * (1.0 - th * th) * (c * (1.0 + 3.0 * a * u * u))
    return 0.5 * u * (1.0 + th), slope


far_off = 1e33
longest = 512


def per_device(
    tokens, segment_ids, first_gain, first_shift, qkv_weight, qv_bias, out_weight, out_bias, second_gain, second_shift,
    up_weight, up_bias, down_weight, down_bias, cotangent,
):
    low, f32 = jnp.bfloat16, jnp.float32
    nt = lax.axis_size("tensor")
    lines, wide = grid_of(nt)
    t = lax.axis_index("tensor")
    z, y = t // wide, t % wide
    length, d = tokens.shape
    chunk = length // nt
    halo = -(-(longest - 1) // chunk)
    behind = halo * chunk
    span = behind + chunk
    heads_here, width = qkv_weight.shape[1], qkv_weight.shape[2] // 3
    lanes = heads_here * width
    hidden_here = up_weight.shape[1]

    qkv_own = qkv_weight.reshape(d, heads_here, 3, width).transpose(0, 2, 1, 3).reshape(d, 3 * lanes)
    bias_own = jnp.pad(qv_bias.reshape(heads_here, 2, width).transpose(1, 0, 2).reshape(2, lanes), ((0, 0), (0, 128 - lanes)))
    small = jnp.concatenate([bias_own.reshape(256), up_bias])
    small = jnp.pad(small, (0, 64 * 128 - small.shape[0])).reshape(64, 128)

    seg_row = jnp.concatenate([jnp.full((behind,), -1, jnp.int32), segment_ids[0]])
    seg_near = lax.dynamic_slice_in_dim(seg_row, t * chunk, span, 0)
    segments = jnp.broadcast_to(seg_near[None], (8, span))
    total_heads = heads_here * nt
    slopes = jnp.exp2(-8.0 * (jnp.arange(total_heads, dtype=jnp.int32) + 1).astype(f32) / total_heads)

    (qkv_all, out_all, small_all, up_all, down_all, query, keys, values, context, middle, second_pair, normed_t) = front(
        nt, [qkv_own, out_weight, small], [up_weight, down_weight], slopes, segments, tokens,
        [first_gain, first_shift, second_gain, second_shift, out_bias],
    )
    small_all = small_all.reshape(nt, 64 * 128).astype(f32)
    up_bias_all = lax.dynamic_index_in_dim(
        small_all[:, 256 : 256 + hidden_here].reshape(lines, wide, hidden_here), y, 1, keepdims=False
    )
    second_pair = second_pair.reshape(wide * chunk, d)

    keep_up, sum_down, grad_up_bias, grad_middle, grad_middle_low, output_mine, columns2, give_up = mlp(
        nt, second_pair, cotangent, up_all, down_all, jnp.broadcast_to(up_bias_all[:, None], (lines, 8, hidden_here)),
        middle, second_gain, down_bias,
    )
    grad_up_bias = grad_up_bias[:, 0]
    pull = [
        slopes, segments, query, keys, values, grad_middle_low, context, out_all, qkv_all, normed_t, grad_middle, keep_up,
        give_up, tokens, first_gain,
    ]
    g_down, output_all, sum_qkv, sum_out, grad_tokens, columns1, q_sum, v_sum, sum_up = finish(
        nt, [], [sum_down], output_mine, None, 1, "finish_mlp", pull
    )
    up_slots = jnp.where(jnp.arange(wide)[None, :, None] == y, grad_up_bias[:, None, :], 0.0)
    vectors = jnp.concatenate(
        [
            columns1[0], columns1[1], columns2[2], columns2[0], columns2[1], columns2[3],
            q_sum[:, 0].reshape(-1), v_sum[:, 0].reshape(-1), up_slots.reshape(-1),
        ]
    )
    g_qkv, g_out, g_up, grad_tokens_all, vectors = finish(
        nt, [sum_qkv, sum_out], [sum_up], grad_tokens, vectors.reshape(-1, 128), 5, "finish_attn"
    )
    vectors = vectors.reshape(-1)
    g_first_gain, g_first_shift, g_out_bias, g_second_gain, g_second_shift, g_down_bias = (
        vectors[i * d : (i + 1) * d] for i in range(6)
    )
    rest = vectors[6 * d :]
    g_q = lax.dynamic_index_in_dim(rest[:d].reshape(nt, heads_here, width), t, 0, keepdims=False)
    g_v = lax.dynamic_index_in_dim(rest[d : 2 * d].reshape(nt, heads_here, width), t, 0, keepdims=False)
    g_up_bias = lax.dynamic_index_in_dim(rest[2 * d :].reshape(nt, hidden_here), t, 0, keepdims=False)
    g_qkv = g_qkv.reshape(d, 3, heads_here, width).transpose(0, 2, 1, 3).reshape(d, heads_here, 3 * width)
    return (
        output_all.reshape(length, d), grad_tokens_all.reshape(length, d), g_first_gain, g_first_shift, g_qkv,
        jnp.concatenate([g_q, g_v], axis=1), g_out, g_out_bias, g_second_gain, g_second_shift,
        g_up, g_up_bias, g_down, g_down_bias,
    )


def solution(mesh):
    rows, cols, both = P("dp", None), P(None, "tensor"), P("tensor", None)
    return jax.shard_map(
        per_device,
        mesh=mesh,
        in_specs=(
            rows, rows, P(), P(), P(None, "tensor", None), both, both, P(), P(), P(), cols, P("tensor"), both, P(), rows,
        ),
        out_specs=(
            rows, rows, P(), P(), P(None, "tensor", None), both, both, P(), P(), P(), cols, P("tensor"), both, P(),
        ),
        check_vma=False,
    )
```
